256 devices in a mesh: tm: 64 (over x, z, core), col: 4 (over y).
Axes of the slice: x: 4, y: 4, z: 8, core: 2. Of those that a mesh axis runs over, the one named last changes fastest.
Arguments:
- observations: float32 [1024, 64, 256], P('tm', 'col'), may hold values from -6 to 6
- band_index: int32 [1024], P('tm'), may hold values from 0 to 3
- obs_mask: int32 [1024], P('tm'), may hold values 0 or 1
- diffusivity: float32 [4, 256], replicated, may hold values from 0.005 to 0.05
- mode_correction_factors: float32 [4, 256, 256], replicated, may hold values from -0.01 to 0.06
- mode_backward_factors: float32 [4, 256, 256], replicated, may hold values from -0.01 to 1.01
- initial_mean: float32 [256], replicated, may hold values from -6 to 6
Outputs:
- filtered: float32 [1024, 64, 256], P('tm', 'col')
- smoothed: float32 [1024, 64, 256], P('tm', 'col')
The draws below stay inside these ranges and needn't reach their ends.
All inputs are finite; a program needn't handle non-finite values. No bound on the sum of `obs_mask` on one device may be relied on, other than what follows from the above.
Results may differ from the reference program's by a relative error of at most 0.0003.
Values sent between devices are 32-bit elements; how exact they have to be, the bound alone decides.
A program may use at most 64 MiB of HBM per device.

```python
import math
import jax
import jax.numpy as jnp
from jax import lax

GRID = 16
STATE = 256
BANDS = 4
RECORDS = 64
STEPS = 1024


def draw_mode_correction_factors(key, part):
    diag_key, off_key = jax.random.split(jax.random.fold_in(key, 11))
    diagonal = jnp.exp(jax.random.uniform(diag_key, (BANDS, STATE), jnp.float32, math.log(0.002), math.log(0.05)))
    noise = jnp.clip(jax.random.normal(off_key, (BANDS, STATE, STATE), jnp.float32), -3.0, 3.0)
    offdiag = 0.02 / math.sqrt(STATE) * noise
    return offdiag + diagonal[:, :, None] * jnp.eye(STATE, dtype=jnp.float32)


def draw_mode_backward_factors(key, part):
    pick_key, slow_key, fast_key, off_key = jax.random.split(jax.random.fold_in(key, 23), 4)
    slow_share = 0.5
    slow_cells = (jax.random.uniform(pick_key, (1, STATE), jnp.float32) < slow_share).astype(jnp.float32)
    slow_rate = jnp.exp(jax.random.uniform(slow_key, (BANDS, STATE), jnp.float32, math.log(0.1), math.log(2.0))) / STEPS
    fast_rate = 1.0 / jax.random.uniform(fast_key, (BANDS, STATE), jnp.float32, 30.0, 50.0)
    diagonal = jnp.exp(-(slow_cells * slow_rate + (1.0 - slow_cells) * fast_rate))
    noise = jnp.clip(jax.random.normal(off_key, (BANDS, STATE, STATE), jnp.float32), -3.0, 3.0)
    offdiag = 0.5 / (math.sqrt(STATE) * STEPS) * noise
    return offdiag + diagonal[:, :, None] * jnp.eye(STATE, dtype=jnp.float32)


def touch_ends(result, rng, least, top_value):
    extent = result.shape
    index_at = [jax.random.randint(jax.random.fold_in(rng, axis), (), 0, extent[axis]) for axis in range(len(extent))]
    result = result.at[tuple(index_at)].set(least)
    longest = extent.index(max(extent))
    index_at[longest] = (index_at[longest] + 1) % extent[longest]
    return result.at[tuple(index_at)].set(top_value)


def shard_levels(own_key, extent, cuts, least, high):
    loudness, own = 1.0, jax.random.fold_in(own_key, 6)
    for dim, parts in cuts:
        draws = jnp.exp(jax.random.uniform(jax.random.fold_in(own, dim), (parts,), jnp.float32, least / len(cuts), high / len(cuts)))
        loudness = loudness * jnp.repeat(draws, extent[dim] // parts).reshape([-1 if axis == dim else 1 for axis in range(len(extent))])
    return loudness


def bell_draw(key, shape, spread, reach, cuts=(), held_as=jnp.bfloat16):
    level = shard_levels(key, shape, cuts, -0.22, 0.18) if cuts else 1.0
    drawn = jax.random.normal(key, shape, jnp.float32) * spread * level
    return jnp.minimum(jnp.maximum(drawn, -reach), reach).astype(held_as)


def setup_inputs(seed: int = 0) -> dict:
    key_of = jax.random.split(jax.random.key(seed), 8)
    return {
        "observations": bell_draw(key_of[0], (STEPS, RECORDS, STATE), 1.0, 6.0, ((0, 64), (1, 4)), jnp.float32),
        "band_index": touch_ends(jax.random.randint(key_of[1], (STEPS,), 0, BANDS), jax.random.fold_in(key_of[1], 1), 0, BANDS - 1).astype(jnp.int32),
        "obs_mask": touch_ends((jax.random.randint(key_of[2], (STEPS,), 0, 32) < 1).astype(jnp.int32), jax.random.fold_in(key_of[2], 1), 0, 1),
        "diffusivity": jnp.clip(jnp.exp(jax.random.uniform(key_of[3], (BANDS, STATE), jnp.float32, math.log(0.005), math.log(0.05))), 0.005, 0.05),
        "mode_correction_factors": draw_mode_correction_factors(jax.random.fold_in(key_of[7], 71), 0),
        "mode_backward_factors": draw_mode_backward_factors(jax.random.fold_in(key_of[7], 71), 0),
        "initial_mean": bell_draw(key_of[6], (STATE,), 1.0, 6.0, (), jnp.float32),
    }


def accurate_matmul_result(first_factor, second_factor):
    return jnp.dot(first_factor, second_factor, precision=lax.Precision.HIGHEST)


def diffusion_matrices(diffusivity, side_cells):
    cell_count = side_cells * side_cells
    cell_ids = jnp.arange(cell_count)
    cell_row = cell_ids // side_cells
    cell_col = cell_ids % side_cells
    adjacent = (jnp.abs(cell_row[:, None] - cell_row[None, :]) + jnp.abs(cell_col[:, None] - cell_col[None, :])) == 1
    coupling = 0.5 * (diffusivity[:, :, None] + diffusivity[:, None, :]) * adjacent.astype(diffusivity.dtype)
    keeping = 1.0 - jnp.sum(coupling, axis=2)
    return coupling + keeping[:, :, None] * jnp.eye(cell_count, dtype=diffusivity.dtype)


def reference(observations, band_index, obs_mask, diffusivity, mode_correction_factors, mode_backward_factors, initial_mean):
    dynamics_operator_matrix = diffusion_matrices(diffusivity, GRID)
    start_rows = jnp.zeros((RECORDS, STATE), jnp.float32) + initial_mean[None, :]

    def filter_step(current_hidden_vector, argument_entries):
        entry_measurement, current_strip, current_measured_flag = argument_entries
        projected_field_vector = accurate_matmul_result(current_hidden_vector, dynamics_operator_matrix[current_strip])
        corrected_hidden_vector = projected_field_vector + current_measured_flag.astype(jnp.float32) * accurate_matmul_result(entry_measurement - projected_field_vector, mode_correction_factors[current_strip].T)
        return corrected_hidden_vector, (corrected_hidden_vector, projected_field_vector)

    _, (filtered, predicted) = lax.scan(filter_step, start_rows, (observations, band_index, obs_mask))
    next_predicted = jnp.concatenate([predicted[1:], jnp.zeros_like(predicted[:1])], axis=0)
    final_flag = (jnp.arange(STEPS) == STEPS - 1).astype(jnp.float32)

    def smooth_step(following_lines, argument_entries):
        current_average, projected_field_vector, current_strip, current_closing_flag = argument_entries
        current_refined_estimate = current_average + (1.0 - current_closing_flag) * accurate_matmul_result(following_lines - projected_field_vector, mode_backward_factors[current_strip].T)
        return current_refined_estimate, current_refined_estimate

    _, smoothed = lax.scan(smooth_step, jnp.zeros_like(start_rows), (filtered, next_predicted, band_index, final_flag), reverse=True)
    return filtered, smoothed
```

```python
import jax
import jax.numpy as jnp
from jax import lax
from jax.sharding import PartitionSpec as P

GRID = 16


def passed_along(block, axis, distance):
    devices = range(lax.axis_size(axis))
    route = [(i - distance, i) for i in devices if i - distance in devices]
    return lax.ppermute(block, axis, route)


def doubling_scan(matrix, records, axis, reverse):
    peers, index = (lax.axis_size(axis), lax.axis_index(axis))
    distance = 1
    while distance < peers:
        step = -distance if reverse else distance
        reached = index + distance < peers if reverse else index >= distance
        got_records = passed_along(records, axis, step)
        new_records = accurate_matmul_result(got_records, matrix) + records
        if 2 * distance < peers:
            got_matrix = passed_along(matrix, axis, step)
            matrix = jnp.where(reached, accurate_matmul_result(got_matrix, matrix), matrix)
        records = jnp.where(reached, new_records, records)
        distance *= 2
    return records


def accurate_matmul_result(first_factor, second_factor):
    return jnp.dot(first_factor, second_factor, precision=lax.Precision.HIGHEST)


def apply_flipped_matrix(first_factor, second_factor):
    return lax.dot_general(
        first_factor, second_factor, (((1,), (1,)), ((), ())), precision=lax.Precision.HIGHEST
    )


def diffusion_matrices(diffusivity, side_cells):
    cell_count = side_cells * side_cells
    cell_ids = jnp.arange(cell_count)
    cell_row = cell_ids // side_cells
    cell_col = cell_ids % side_cells
    adjacent = (
        jnp.abs(cell_row[:, None] - cell_row[None, :])
        + jnp.abs(cell_col[:, None] - cell_col[None, :])
        == 1
    )
    coupling = (
        0.5 * (diffusivity[:, :, None] + diffusivity[:, None, :]) * adjacent.astype(jnp.float32)
    )
    keeping = 1.0 - jnp.sum(coupling, axis=2)
    return coupling + keeping[:, :, None] * jnp.eye(cell_count, dtype=jnp.float32)


def compose_pair(earlier, later):
    return (
        accurate_matmul_result(earlier[0], later[0]),
        accurate_matmul_result(earlier[1], later[0]) + later[1],
    )


def shards(
    observations,
    band_index,
    obs_mask,
    diffusivity,
    mode_correction_factors,
    mode_backward_factors,
    initial_mean,
):
    steps_dev = observations.shape[0]
    record_rows = observations.shape[1]
    states = initial_mean.shape[0]
    column_share = states // lax.axis_size("col")
    column_index = lax.axis_index("col")
    time_devices = lax.axis_size("tm")
    time_index = lax.axis_index("tm")
    dynamics_operator_matrix = diffusion_matrices(diffusivity, GRID)
    corrected = dynamics_operator_matrix - jax.vmap(apply_flipped_matrix)(
        dynamics_operator_matrix, mode_correction_factors
    )
    tables = jnp.stack([dynamics_operator_matrix, corrected], axis=1)
    identity = jnp.eye(states, dtype=jnp.float32)
    own_identity = lax.dynamic_slice_in_dim(identity, column_index * column_share, column_share, 0)
    blank_records = jnp.zeros((record_rows, states), jnp.float32)
    blank_columns = jnp.zeros((column_share, states), jnp.float32)
    initial_rows = jnp.concatenate([own_identity, blank_records], axis=0)
    final_here = (time_index == time_devices - 1) & (jnp.arange(steps_dev) == steps_dev - 1)
    live_flags = 1.0 - final_here.astype(jnp.float32)

    def compose_filter(element_rows, argument_entries):
        entry_measurement, current_strip, current_measured_flag = argument_entries
        source = current_measured_flag.astype(jnp.float32) * apply_flipped_matrix(
            entry_measurement, mode_correction_factors[current_strip]
        )
        element_rows = accurate_matmul_result(
            element_rows, tables[current_strip, current_measured_flag]
        ) + jnp.concatenate([blank_columns, source], axis=0)
        return (element_rows, None)

    forward_rows, _ = lax.scan(compose_filter, initial_rows, (observations, band_index, obs_mask))
    whole_matrix = lax.all_gather(forward_rows[:column_share], "col", axis=0, tiled=True)
    first_block = time_index == 0
    block_records = forward_rows[column_share:]
    folded_records = jnp.where(
        first_block, accurate_matmul_result(initial_mean[None, :], whole_matrix) + block_records, block_records
    )
    folded_matrix = jnp.where(first_block, jnp.zeros_like(whole_matrix), whole_matrix)
    ending_records = doubling_scan(folded_matrix, folded_records, "tm", False)
    start_rows = jnp.where(
        first_block,
        jnp.broadcast_to(initial_mean[None, :], blank_records.shape),
        passed_along(ending_records, "tm", 1),
    )

    def filter_step(current_hidden_vector, argument_entries):
        entry_measurement, current_strip, current_measured_flag = argument_entries
        projected_field_vector = accurate_matmul_result(
            current_hidden_vector, dynamics_operator_matrix[current_strip]
        )
        corrected_hidden_vector = projected_field_vector + current_measured_flag.astype(
            jnp.float32
        ) * apply_flipped_matrix(
            entry_measurement - projected_field_vector, mode_correction_factors[current_strip]
        )
        return (corrected_hidden_vector, (corrected_hidden_vector, projected_field_vector))

    _, (filtered, predicted) = lax.scan(
        filter_step, start_rows, (observations, band_index, obs_mask)
    )
    following = passed_along(predicted[0], "tm", -1)
    next_predicted = jnp.concatenate([predicted[1:], following[None]], axis=0)

    def compose_smoother(element_rows, argument_entries):
        current_average, projected_field_vector, current_strip, current_active_flag = (
            argument_entries
        )
        current_correction_factor = mode_backward_factors[current_strip] * current_active_flag
        beginning_shift_amount = current_average - apply_flipped_matrix(
            projected_field_vector, current_correction_factor
        )
        element_rows = apply_flipped_matrix(
            element_rows, current_correction_factor
        ) + jnp.concatenate([blank_columns, beginning_shift_amount], axis=0)
        return (element_rows, beginning_shift_amount)

    backward_rows, offsets = lax.scan(
        compose_smoother,
        initial_rows,
        (filtered, next_predicted, band_index, live_flags),
        reverse=True,
    )
    whole_back = lax.all_gather(backward_rows[:column_share], "col", axis=0, tiled=True)
    opening_records = doubling_scan(whole_back, backward_rows[column_share:], "tm", True)
    after_records = passed_along(opening_records, "tm", -1)

    def smooth_step(following_lines, argument_entries):
        current_strip, current_active_flag, beginning_shift_amount = argument_entries
        current_refined_estimate = (
            apply_flipped_matrix(
                following_lines, mode_backward_factors[current_strip] * current_active_flag
            )
            + beginning_shift_amount
        )
        return (current_refined_estimate, current_refined_estimate)

    _, smoothed = lax.scan(
        smooth_step, after_records, (band_index, live_flags, offsets), reverse=True
    )
    return (filtered, smoothed)


def solution(mesh):
    return jax.shard_map(
        shards,
        mesh=mesh,
        in_specs=(P("tm", "col", None), P("tm"), P("tm"), P(), P(), P(), P()),
        out_specs=(P("tm", "col", None), P("tm", "col", None)),
        check_vma=False,
    )
```

```python
import functools

import jax
import jax.numpy as jnp
from jax import lax
from jax.experimental import pallas as pl
from jax.experimental.pallas import tpu as pltpu
from jax.sharding import PartitionSpec as P

GRID = 16


def passed_along(block, axis, distance):
    devices = range(lax.axis_size(axis))
    route = [(i - distance, i) for i in devices if i - distance in devices]
    return lax.ppermute(block, axis, route)


def accurate_matmul_result(first_factor, second_factor):
    return jnp.dot(first_factor, second_factor, precision=lax.Precision.HIGHEST)


def doubling_scan(matrix, records, axis, reverse):
    peers, index = (lax.axis_size(axis), lax.axis_index(axis))
    distance = 1
    while distance < peers:
        step = -distance if reverse else distance
        reached = index + distance < peers if reverse else index >= distance
        got_records = passed_along(records, axis, step)
        new_records = accurate_matmul_result(got_records, matrix) + records
        if 2 * distance < peers:
            got_matrix = passed_along(matrix, axis, step)
            matrix = jnp.where(reached, accurate_matmul_result(got_matrix, matrix), matrix)
        records = jnp.where(reached, new_records, records)
        distance *= 2
    return records


def diffusion_matrices(diffusivity, side_cells):
    cell_count = side_cells * side_cells
    cell_ids = jnp.arange(cell_count)
    cell_row = cell_ids // side_cells
    cell_col = cell_ids % side_cells
    adjacent = (
        jnp.abs(cell_row[:, None] - cell_row[None, :])
        + jnp.abs(cell_col[:, None] - cell_col[None, :])
        == 1
    )
    coupling = (
        0.5 * (diffusivity[:, :, None] + diffusivity[:, None, :]) * adjacent.astype(jnp.float32)
    )
    keeping = 1.0 - jnp.sum(coupling, axis=2)
    return coupling + keeping[:, :, None] * jnp.eye(cell_count, dtype=jnp.float32)


def recurrence_kernel(*refs, steps, reverse, store_all, side):
    if side:
        pick_ref, side_pick_ref, start_ref, table_ref, side_ref, source_ref, out_ref, side_out_ref = refs
    else:
        pick_ref, start_ref, table_ref, source_ref, out_ref = refs
    rows = start_ref[...]
    order = range(steps - 1, -1, -1) if reverse else range(steps)
    for t in order:
        if side:
            side_out_ref[t] = jnp.dot(
                rows,
                side_ref[side_pick_ref[t]],
                precision=lax.Precision.HIGHEST,
                preferred_element_type=jnp.float32,
            )
        rows = (
            jnp.dot(
                rows,
                table_ref[pick_ref[t]],
                precision=lax.Precision.HIGHEST,
                preferred_element_type=jnp.float32,
            )
            + source_ref[t]
        )
        if store_all:
            out_ref[t] = rows
    if not store_all:
        out_ref[...] = rows


def recurrence(pick, start, table, source, reverse, store_all, side=None):
    steps = source.shape[0]
    smem = pl.BlockSpec(memory_space=pltpu.SMEM)
    vmem = pl.BlockSpec(memory_space=pltpu.VMEM)
    out_shape = jax.ShapeDtypeStruct(source.shape if store_all else start.shape, jnp.float32)
    if side is None:
        operands = (pick, start, table, source)
        in_specs = [smem, vmem, vmem, vmem]
        out_specs = vmem
    else:
        side_pick, side_table = side
        operands = (pick, side_pick, start, table, side_table, source)
        in_specs = [smem, smem, vmem, vmem, vmem, vmem]
        out_shape = (out_shape, jax.ShapeDtypeStruct(source.shape, jnp.float32))
        out_specs = (vmem, vmem)
    return pl.pallas_call(
        functools.partial(
            recurrence_kernel,
            steps=steps,
            reverse=reverse,
            store_all=store_all,
            side=side is not None,
        ),
        out_shape=out_shape,
        in_specs=in_specs,
        out_specs=out_specs,
    )(*operands)


def per_band_products(lines, factors, weights):
    steps, rows, states = lines.shape
    bands = factors.shape[0]
    every = accurate_matmul_result(
        lines.reshape(steps * rows, states),
        jnp.transpose(factors, (1, 0, 2)).reshape(states, bands * states),
    ).reshape(steps, rows, bands, states)
    return jnp.sum(every * weights[:, None, :, None], axis=2)


def shards(
    observations,
    band_index,
    obs_mask,
    diffusivity,
    mode_correction_factors,
    mode_backward_factors,
    initial_mean,
):
    steps_dev = observations.shape[0]
    record_rows = observations.shape[1]
    states = initial_mean.shape[0]
    bands = diffusivity.shape[0]
    column_share = states // lax.axis_size("col")
    column_index = lax.axis_index("col")
    time_devices = lax.axis_size("tm")
    time_index = lax.axis_index("tm")
    dynamics = diffusion_matrices(diffusivity, GRID)
    gain = jnp.transpose(mode_correction_factors, (0, 2, 1))
    corrected = dynamics - jnp.einsum(
        "bij,bjk->bik", dynamics, gain, precision=lax.Precision.HIGHEST
    )
    forward_table = jnp.stack([dynamics, corrected], axis=1).reshape(2 * bands, states, states)
    forward_pick = 2 * band_index + obs_mask
    identity = jnp.eye(states, dtype=jnp.float32)
    own_identity = lax.dynamic_slice_in_dim(identity, column_index * column_share, column_share, 0)
    blank_columns = jnp.zeros((steps_dev, column_share, states), jnp.float32)
    initial_rows = jnp.concatenate(
        [own_identity, jnp.zeros((record_rows, states), jnp.float32)], axis=0
    )
    band_weights = (band_index[:, None] == jnp.arange(bands)[None, :]).astype(jnp.float32)
    observed_weights = band_weights * obs_mask.astype(jnp.float32)[:, None]
    measured = per_band_products(observations, gain, observed_weights)

    forward_rows = recurrence(
        forward_pick,
        initial_rows,
        forward_table,
        jnp.concatenate([blank_columns, measured], axis=1),
        False,
        False,
    )
    whole_matrix = lax.all_gather(forward_rows[:column_share], "col", axis=0, tiled=True)
    first_block = time_index == 0
    block_records = forward_rows[column_share:]
    folded_records = jnp.where(
        first_block,
        accurate_matmul_result(initial_mean[None, :], whole_matrix) + block_records,
        block_records,
    )
    folded_matrix = jnp.where(first_block, jnp.zeros_like(whole_matrix), whole_matrix)
    ending_records = doubling_scan(folded_matrix, folded_records, "tm", False)
    start_rows = jnp.where(
        first_block,
        jnp.broadcast_to(initial_mean[None, :], (record_rows, states)),
        passed_along(ending_records, "tm", 1),
    )

    filtered, predicted = recurrence(
        forward_pick,
        start_rows,
        forward_table,
        measured,
        False,
        True,
        side=(band_index, dynamics),
    )
    following = passed_along(predicted[0], "tm", -1)
    next_predicted = jnp.concatenate([predicted[1:], following[None]], axis=0)

    final_here = (time_index == time_devices - 1) & (jnp.arange(steps_dev) == steps_dev - 1)
    backward = jnp.transpose(mode_backward_factors, (0, 2, 1))
    backward_table = jnp.concatenate([backward, jnp.zeros_like(backward[:1])], axis=0)
    backward_pick = jnp.where(final_here, bands, band_index)
    live_weights = band_weights * (1.0 - final_here.astype(jnp.float32))[:, None]
    shift = filtered - per_band_products(next_predicted, backward, live_weights)

    backward_rows = recurrence(
        backward_pick,
        initial_rows,
        backward_table,
        jnp.concatenate([blank_columns, shift], axis=1),
        True,
        False,
    )
    whole_back = lax.all_gather(backward_rows[:column_share], "col", axis=0, tiled=True)
    opening_records = doubling_scan(whole_back, backward_rows[column_share:], "tm", True)
    after_records = passed_along(opening_records, "tm", -1)

    smoothed = recurrence(backward_pick, after_records, backward_table, shift, True, True)
    return (filtered, smoothed)


def solution(mesh):
    return jax.shard_map(
        shards,
        mesh=mesh,
        in_specs=(P("tm", "col", None), P("tm"), P("tm"), P(), P(), P(), P()),
        out_specs=(P("tm", "col", None), P("tm", "col", None)),
        check_vma=False,
    )
```

```python
import functools

import jax
import jax.numpy as jnp
from jax import lax
from jax.experimental import pallas as pl
from jax.experimental.pallas import tpu as pltpu
from jax.sharding import PartitionSpec as P

GRID = 16


def passed_along(block, axis, distance):
    devices = range(lax.axis_size(axis))
    route = [(i - distance, i) for i in devices if i - distance in devices]
    return lax.ppermute(block, axis, route)


def accurate_matmul_result(first_factor, second_factor):
    return jnp.dot(first_factor, second_factor, precision=lax.Precision.HIGHEST)


def doubling_maps(matrix, axis, reverse):
    peers, index = (lax.axis_size(axis), lax.axis_index(axis))
    maps = [matrix]
    distance = 1
    while 2 * distance < peers:
        step = -distance if reverse else distance
        reached = index + distance < peers if reverse else index >= distance
        got_matrix = passed_along(matrix, axis, step)
        matrix = jnp.where(reached, accurate_matmul_result(got_matrix, matrix), matrix)
        maps.append(matrix)
        distance *= 2
    return maps


def doubling_records(maps, records, axis, reverse):
    peers, index = (lax.axis_size(axis), lax.axis_index(axis))
    distance = 1
    for matrix in maps:
        step = -distance if reverse else distance
        reached = index + distance < peers if reverse else index >= distance
        got_records = passed_along(records, axis, step)
        records = jnp.where(
            reached, accurate_matmul_result(got_records, matrix) + records, records
        )
        distance *= 2
    return records


def diffusion_matrices(diffusivity, side_cells):
    cell_count = side_cells * side_cells
    cell_ids = jnp.arange(cell_count)
    cell_row = cell_ids // side_cells
    cell_col = cell_ids % side_cells
    adjacent = (
        jnp.abs(cell_row[:, None] - cell_row[None, :])
        + jnp.abs(cell_col[:, None] - cell_col[None, :])
        == 1
    )
    coupling = (
        0.5 * (diffusivity[:, :, None] + diffusivity[:, None, :]) * adjacent.astype(jnp.float32)
    )
    keeping = 1.0 - jnp.sum(coupling, axis=2)
    return coupling + keeping[:, :, None] * jnp.eye(cell_count, dtype=jnp.float32)


def recurrence_kernel(*refs, steps, reverse, store_all, side):
    if side:
        pick_ref, side_pick_ref, start_ref, table_ref, side_ref, source_ref, out_ref, side_out_ref = refs
    else:
        pick_ref, start_ref, table_ref, source_ref, out_ref = refs
    rows = start_ref[...]
    order = range(steps - 1, -1, -1) if reverse else range(steps)
    for t in order:
        if side:
            side_out_ref[t] = jnp.dot(
                rows,
                side_ref[side_pick_ref[t]],
                precision=lax.Precision.HIGHEST,
                preferred_element_type=jnp.float32,
            )
        rows = (
            jnp.dot(
                rows,
                table_ref[pick_ref[t]],
                precision=lax.Precision.HIGHEST,
                preferred_element_type=jnp.float32,
            )
            + source_ref[t]
        )
        if store_all:
            out_ref[t] = rows
    if not store_all:
        out_ref[...] = rows


def recurrence(pick, start, table, source, reverse, store_all, side=None):
    steps = source.shape[0]
    smem = pl.BlockSpec(memory_space=pltpu.SMEM)
    vmem = pl.BlockSpec(memory_space=pltpu.VMEM)
    out_shape = jax.ShapeDtypeStruct(source.shape if store_all else start.shape, jnp.float32)
    if side is None:
        operands = (pick, start, table, source)
        in_specs = [smem, vmem, vmem, vmem]
        out_specs = vmem
    else:
        side_pick, side_table = side
        operands = (pick, side_pick, start, table, side_table, source)
        in_specs = [smem, smem, vmem, vmem, vmem, vmem]
        out_shape = (out_shape, jax.ShapeDtypeStruct(source.shape, jnp.float32))
        out_specs = (vmem, vmem)
    return pl.pallas_call(
        functools.partial(
            recurrence_kernel,
            steps=steps,
            reverse=reverse,
            store_all=store_all,
            side=side is not None,
        ),
        out_shape=out_shape,
        in_specs=in_specs,
        out_specs=out_specs,
    )(*operands)


def per_band_products(lines, factors, weights):
    steps, rows, states = lines.shape
    bands = factors.shape[0]
    every = accurate_matmul_result(
        lines.reshape(steps * rows, states),
        jnp.transpose(factors, (1, 0, 2)).reshape(states, bands * states),
    ).reshape(steps, rows, bands, states)
    return jnp.sum(every * weights[:, None, :, None], axis=2)


def shards(
    observations,
    band_index,
    obs_mask,
    diffusivity,
    mode_correction_factors,
    mode_backward_factors,
    initial_mean,
):
    steps_dev = observations.shape[0]
    record_rows = observations.shape[1]
    states = initial_mean.shape[0]
    bands = diffusivity.shape[0]
    column_share = states // lax.axis_size("col")
    column_index = lax.axis_index("col")
    time_devices = lax.axis_size("tm")
    time_index = lax.axis_index("tm")
    dynamics = diffusion_matrices(diffusivity, GRID)
    gain = jnp.transpose(mode_correction_factors, (0, 2, 1))
    corrected = dynamics - jnp.einsum(
        "bij,bjk->bik", dynamics, gain, precision=lax.Precision.HIGHEST
    )
    forward_table = jnp.stack([dynamics, corrected], axis=1).reshape(2 * bands, states, states)
    forward_pick = 2 * band_index + obs_mask
    identity = jnp.eye(states, dtype=jnp.float32)
    own_identity = lax.dynamic_slice_in_dim(identity, column_index * column_share, column_share, 0)
    blank_columns = jnp.zeros((steps_dev, column_share, states), jnp.float32)
    band_weights = (band_index[:, None] == jnp.arange(bands)[None, :]).astype(jnp.float32)
    observed_weights = band_weights * obs_mask.astype(jnp.float32)[:, None]
    measured = per_band_products(observations, gain, observed_weights)

    blank_records = jnp.zeros((record_rows, states), jnp.float32)
    forward_rows = recurrence(
        forward_pick, own_identity, forward_table, blank_columns, False, False
    )
    whole_matrix = lax.all_gather(forward_rows, "col", axis=0, tiled=True)
    first_block = time_index == 0
    forward_maps = doubling_maps(
        jnp.where(first_block, jnp.zeros_like(whole_matrix), whole_matrix), "tm", False
    )

    final_here = (time_index == time_devices - 1) & (jnp.arange(steps_dev) == steps_dev - 1)
    backward = jnp.transpose(mode_backward_factors, (0, 2, 1))
    backward_table = jnp.concatenate([backward, jnp.zeros_like(backward[:1])], axis=0)
    backward_pick = jnp.where(final_here, bands, band_index)
    backward_rows = recurrence(
        backward_pick, own_identity, backward_table, blank_columns, True, False
    )
    whole_back = lax.all_gather(backward_rows, "col", axis=0, tiled=True)
    backward_maps = doubling_maps(whole_back, "tm", True)

    block_records = recurrence(
        forward_pick, blank_records, forward_table, measured, False, False
    )
    folded_records = jnp.where(
        first_block,
        accurate_matmul_result(initial_mean[None, :], whole_matrix) + block_records,
        block_records,
    )
    ending_records = doubling_records(forward_maps, folded_records, "tm", False)
    start_rows = jnp.where(
        first_block,
        jnp.broadcast_to(initial_mean[None, :], (record_rows, states)),
        passed_along(ending_records, "tm", 1),
    )

    filtered, predicted = recurrence(
        forward_pick,
        start_rows,
        forward_table,
        measured,
        False,
        True,
        side=(band_index, dynamics),
    )
    following = passed_along(predicted[0], "tm", -1)
    next_predicted = jnp.concatenate([predicted[1:], following[None]], axis=0)

    live_weights = band_weights * (1.0 - final_here.astype(jnp.float32))[:, None]
    shift = filtered - per_band_products(next_predicted, backward, live_weights)

    back_records = recurrence(backward_pick, blank_records, backward_table, shift, True, False)
    opening_records = doubling_records(backward_maps, back_records, "tm", True)
    after_records = passed_along(opening_records, "tm", -1)

    smoothed = recurrence(backward_pick, after_records, backward_table, shift, True, True)
    return (filtered, smoothed)


def solution(mesh):
    return jax.shard_map(
        shards,
        mesh=mesh,
        in_specs=(P("tm", "col", None), P("tm"), P("tm"), P(), P(), P(), P()),
        out_specs=(P("tm", "col", None), P("tm", "col", None)),
        check_vma=False,
    )
```

```python
import functools

import jax
import jax.numpy as jnp
from jax import lax
from jax.experimental import pallas as pl
from jax.experimental.pallas import tpu as pltpu
from jax.sharding import PartitionSpec as P

GRID = 16
UNROLL = 4


def passed_along(block, axis, distance):
    devices = range(lax.axis_size(axis))
    route = [(i - distance, i) for i in devices if i - distance in devices]
    return lax.ppermute(block, axis, route)


def gathered_rows(part, axis):
    peers, index = (lax.axis_size(axis), lax.axis_index(axis))
    rows = part.shape[0]
    whole = jnp.zeros((peers * rows,) + part.shape[1:], part.dtype)
    for shift in range(peers):
        if shift == 0:
            got = part
        else:
            got = lax.ppermute(part, axis, [(i, (i + shift) % peers) for i in range(peers)])
        owner = lax.rem(index - shift + peers, peers)
        whole = lax.dynamic_update_slice_in_dim(whole, got, owner * rows, 0)
    return whole


def accurate_matmul_result(first_factor, second_factor):
    return jnp.dot(first_factor, second_factor, precision=lax.Precision.HIGHEST)


def doubling_maps(matrix, axis, reverse):
    peers, index = (lax.axis_size(axis), lax.axis_index(axis))
    maps = [matrix]
    distance = 1
    while 2 * distance < peers:
        step = -distance if reverse else distance
        reached = index + distance < peers if reverse else index >= distance
        got_matrix = passed_along(matrix, axis, step)
        matrix = jnp.where(reached, accurate_matmul_result(got_matrix, matrix), matrix)
        maps.append(matrix)
        distance *= 2
    return maps


def doubling_records(maps, records, axis, reverse):
    peers, index = (lax.axis_size(axis), lax.axis_index(axis))
    distance = 1
    for matrix in maps:
        step = -distance if reverse else distance
        reached = index + distance < peers if reverse else index >= distance
        got_records = passed_along(records, axis, step)
        records = jnp.where(
            reached, accurate_matmul_result(got_records, matrix) + records, records
        )
        distance *= 2
    return records


def diffusion_matrices(diffusivity, side_cells):
    cell_count = side_cells * side_cells
    cell_ids = jnp.arange(cell_count)
    cell_row = cell_ids // side_cells
    cell_col = cell_ids % side_cells
    adjacent = (
        jnp.abs(cell_row[:, None] - cell_row[None, :])
        + jnp.abs(cell_col[:, None] - cell_col[None, :])
        == 1
    )
    coupling = (
        0.5 * (diffusivity[:, :, None] + diffusivity[:, None, :]) * adjacent.astype(jnp.float32)
    )
    keeping = 1.0 - jnp.sum(coupling, axis=2)
    return coupling + keeping[:, :, None] * jnp.eye(cell_count, dtype=jnp.float32)


def recurrence_kernel(*refs, steps, reverse, store_all, side):
    if side:
        pick_ref, side_pick_ref, start_ref, table_ref, side_ref, source_ref, out_ref, side_out_ref = refs
    else:
        pick_ref, start_ref, table_ref, source_ref, out_ref = refs
    def advance(i, rows):
        t = steps - 1 - i if reverse else i
        if side:
            side_out_ref[t] = jnp.dot(
                rows,
                side_ref[side_pick_ref[t]],
                precision=lax.Precision.HIGHEST,
                preferred_element_type=jnp.float32,
            )
        rows = (
            jnp.dot(
                rows,
                table_ref[pick_ref[t]],
                precision=lax.Precision.HIGHEST,
                preferred_element_type=jnp.float32,
            )
            + source_ref[t]
        )
        if store_all:
            out_ref[t] = rows
        return rows

    rows = lax.fori_loop(0, steps, advance, start_ref[...], unroll=UNROLL)
    if not store_all:
        out_ref[...] = rows


def recurrence(pick, start, table, source, reverse, store_all, side=None):
    steps = source.shape[0]
    smem = pl.BlockSpec(memory_space=pltpu.SMEM)
    vmem = pl.BlockSpec(memory_space=pltpu.VMEM)
    out_shape = jax.ShapeDtypeStruct(source.shape if store_all else start.shape, jnp.float32)
    if side is None:
        operands = (pick, start, table, source)
        in_specs = [smem, vmem, vmem, vmem]
        out_specs = vmem
    else:
        side_pick, side_table = side
        operands = (pick, side_pick, start, table, side_table, source)
        in_specs = [smem, smem, vmem, vmem, vmem, vmem]
        out_shape = (out_shape, jax.ShapeDtypeStruct(source.shape, jnp.float32))
        out_specs = (vmem, vmem)
    return pl.pallas_call(
        functools.partial(
            recurrence_kernel,
            steps=steps,
            reverse=reverse,
            store_all=store_all,
            side=side is not None,
        ),
        out_shape=out_shape,
        in_specs=in_specs,
        out_specs=out_specs,
    )(*operands)


def per_band_products(lines, factors, weights):
    steps, rows, states = lines.shape
    bands = factors.shape[0]
    every = accurate_matmul_result(
        lines.reshape(steps * rows, states),
        jnp.transpose(factors, (1, 0, 2)).reshape(states, bands * states),
    ).reshape(steps, rows, bands, states)
    return jnp.sum(every * weights[:, None, :, None], axis=2)


def shards(
    observations,
    band_index,
    obs_mask,
    diffusivity,
    mode_correction_factors,
    mode_backward_factors,
    initial_mean,
):
    steps_dev = observations.shape[0]
    record_rows = observations.shape[1]
    states = initial_mean.shape[0]
    bands = diffusivity.shape[0]
    column_share = states // lax.axis_size("col")
    column_index = lax.axis_index("col")
    time_devices = lax.axis_size("tm")
    time_index = lax.axis_index("tm")
    dynamics = diffusion_matrices(diffusivity, GRID)
    gain = jnp.transpose(mode_correction_factors, (0, 2, 1))
    corrected = dynamics - jnp.einsum(
        "bij,bjk->bik", dynamics, gain, precision=lax.Precision.HIGHEST
    )
    forward_table = jnp.stack([dynamics, corrected], axis=1).reshape(2 * bands, states, states)
    forward_pick = 2 * band_index + obs_mask
    identity = jnp.eye(states, dtype=jnp.float32)
    own_identity = lax.dynamic_slice_in_dim(identity, column_index * column_share, column_share, 0)
    blank_columns = jnp.zeros((steps_dev, column_share, states), jnp.float32)
    band_weights = (band_index[:, None] == jnp.arange(bands)[None, :]).astype(jnp.float32)
    observed_weights = band_weights * obs_mask.astype(jnp.float32)[:, None]
    measured = per_band_products(observations, gain, observed_weights)

    blank_records = jnp.zeros((record_rows, states), jnp.float32)
    forward_rows = recurrence(
        forward_pick, own_identity, forward_table, blank_columns, False, False
    )
    whole_matrix = gathered_rows(forward_rows, "col")
    first_block = time_index == 0
    forward_maps = doubling_maps(
        jnp.where(first_block, jnp.zeros_like(whole_matrix), whole_matrix), "tm", False
    )

    final_here = (time_index == time_devices - 1) & (jnp.arange(steps_dev) == steps_dev - 1)
    backward = jnp.transpose(mode_backward_factors, (0, 2, 1))
    backward_table = jnp.concatenate([backward, jnp.zeros_like(backward[:1])], axis=0)
    backward_pick = jnp.where(final_here, bands, band_index)
    backward_rows = recurrence(
        backward_pick, own_identity, backward_table, blank_columns, True, False
    )
    whole_back = gathered_rows(backward_rows, "col")
    backward_maps = doubling_maps(whole_back, "tm", True)

    block_records = recurrence(
        forward_pick, blank_records, forward_table, measured, False, False
    )
    folded_records = jnp.where(
        first_block,
        accurate_matmul_result(initial_mean[None, :], whole_matrix) + block_records,
        block_records,
    )
    ending_records = doubling_records(forward_maps, folded_records, "tm", False)
    start_rows = jnp.where(
        first_block,
        jnp.broadcast_to(initial_mean[None, :], (record_rows, states)),
        passed_along(ending_records, "tm", 1),
    )

    filtered, predicted = recurrence(
        forward_pick,
        start_rows,
        forward_table,
        measured,
        False,
        True,
        side=(band_index, dynamics),
    )
    following = passed_along(predicted[0], "tm", -1)
    next_predicted = jnp.concatenate([predicted[1:], following[None]], axis=0)

    live_weights = band_weights * (1.0 - final_here.astype(jnp.float32))[:, None]
    shift = filtered - per_band_products(next_predicted, backward, live_weights)

    back_records = recurrence(backward_pick, blank_records, backward_table, shift, True, False)
    opening_records = doubling_records(backward_maps, back_records, "tm", True)
    after_records = passed_along(opening_records, "tm", -1)

    smoothed = recurrence(backward_pick, after_records, backward_table, shift, True, True)
    return (filtered, smoothed)


def solution(mesh):
    return jax.shard_map(
        shards,
        mesh=mesh,
        in_specs=(P("tm", "col", None), P("tm"), P("tm"), P(), P(), P(), P()),
        out_specs=(P("tm", "col", None), P("tm", "col", None)),
        check_vma=False,
    )
```

```python
import functools

import jax
import jax.numpy as jnp
from jax import lax
from jax.experimental import pallas as pl
from jax.experimental.pallas import tpu as pltpu
from jax.sharding import PartitionSpec as P

GRID = 16
UNROLL = 4


def passed_along(block, axis, distance):
    devices = range(lax.axis_size(axis))
    route = [(i - distance, i) for i in devices if i - distance in devices]
    return lax.ppermute(block, axis, route)


def gathered_rows(part, axis):
    peers, index = (lax.axis_size(axis), lax.axis_index(axis))
    rows = part.shape[0]
    whole = jnp.zeros((peers * rows,) + part.shape[1:], part.dtype)
    for shift in range(peers):
        if shift == 0:
            got = part
        else:
            got = lax.ppermute(part, axis, [(i, (i + shift) % peers) for i in range(peers)])
        owner = lax.rem(index - shift + peers, peers)
        whole = lax.dynamic_update_slice_in_dim(whole, got, owner * rows, 0)
    return whole


def accurate_matmul_result(first_factor, second_factor):
    return jnp.dot(first_factor, second_factor, precision=lax.Precision.HIGHEST)


def doubling_kernel(matrix_ref, records_ref, out_ref, maps, sums, map_in, sum_in, map_sems, sum_sems,
                    *, axis, reverse):
    peers, index = (lax.axis_size(axis), lax.axis_index(axis))
    other = lax.axis_index("col")
    rounds = max(1, (peers - 1).bit_length())
    barrier = pltpu.get_barrier_semaphore()
    for r in range(rounds):
        distance = 1 << r
        for partner, exists in ((index + distance, index + distance < peers),
                                (index - distance, index - distance >= 0)):
            @pl.when(exists)
            def _():
                pl.semaphore_signal(barrier, inc=1, device_id=(partner, other),
                                    device_id_type=pl.DeviceIdType.MESH)
    partners = 0
    for r in range(rounds):
        distance = 1 << r
        partners = partners + jnp.where(index + distance < peers, 1, 0)
        partners = partners + jnp.where(index - distance >= 0, 1, 0)
    pl.semaphore_wait(barrier, partners)

    for r in range(rounds):
        distance = 1 << r
        if reverse:
            target, sends = index - distance, index - distance >= 0
            receives = index + distance < peers
        else:
            target, sends = index + distance, index + distance < peers
            receives = index - distance >= 0
        own_map = matrix_ref if r == 0 else maps.at[r]
        own_sum = records_ref if r == 0 else sums.at[r]
        sum_copy = pltpu.make_async_remote_copy(
            src_ref=own_sum, dst_ref=sum_in.at[r], send_sem=sum_sems.at[0, r],
            recv_sem=sum_sems.at[1, r], device_id=(target, other),
            device_id_type=pl.DeviceIdType.MESH)
        map_copy = None
        if r + 1 < rounds:
            map_copy = pltpu.make_async_remote_copy(
                src_ref=own_map, dst_ref=map_in.at[r], send_sem=map_sems.at[0, r],
                recv_sem=map_sems.at[1, r], device_id=(target, other),
                device_id_type=pl.DeviceIdType.MESH)

        @pl.when(sends)
        def _():
            sum_copy.start()
            if map_copy is not None:
                map_copy.start()

        @pl.when(receives)
        def _():
            sum_copy.wait_recv()
            sums[r + 1] = jnp.dot(sum_in[r], own_map[...], precision=lax.Precision.HIGHEST,
                                  preferred_element_type=jnp.float32) + own_sum[...]
            if map_copy is not None:
                map_copy.wait_recv()
                maps[r + 1] = jnp.dot(map_in[r], own_map[...], precision=lax.Precision.HIGHEST,
                                      preferred_element_type=jnp.float32)

        @pl.when(jnp.logical_not(receives))
        def _():
            sums[r + 1] = own_sum[...]
            if map_copy is not None:
                maps[r + 1] = own_map[...]

        @pl.when(sends)
        def _():
            sum_copy.wait_send()
            if map_copy is not None:
                map_copy.wait_send()

    out_ref[...] = sums[rounds]


def doubling_scan(matrix, records, axis, reverse, collective_id):
    peers = lax.axis_size(axis)
    rounds = max(1, (peers - 1).bit_length())
    states = matrix.shape[0]
    vmem = pl.BlockSpec(memory_space=pltpu.VMEM)
    return pl.pallas_call(
        functools.partial(doubling_kernel, axis=axis, reverse=reverse),
        out_shape=jax.ShapeDtypeStruct(records.shape, jnp.float32),
        in_specs=[vmem, vmem],
        out_specs=vmem,
        scratch_shapes=[
            pltpu.VMEM((rounds, states, states), jnp.float32),
            pltpu.VMEM((rounds + 1,) + records.shape, jnp.float32),
            pltpu.VMEM((max(1, rounds - 1), states, states), jnp.float32),
            pltpu.VMEM((rounds,) + records.shape, jnp.float32),
            pltpu.SemaphoreType.DMA((2, max(1, rounds - 1))),
            pltpu.SemaphoreType.DMA((2, rounds)),
        ],
        compiler_params=pltpu.CompilerParams(collective_id=collective_id, has_side_effects=True),
    )(matrix, records)


def diffusion_matrices(diffusivity, side_cells):
    cell_count = side_cells * side_cells
    cell_ids = jnp.arange(cell_count)
    cell_row = cell_ids // side_cells
    cell_col = cell_ids % side_cells
    adjacent = (
        jnp.abs(cell_row[:, None] - cell_row[None, :])
        + jnp.abs(cell_col[:, None] - cell_col[None, :])
        == 1
    )
    coupling = (
        0.5 * (diffusivity[:, :, None] + diffusivity[:, None, :]) * adjacent.astype(jnp.float32)
    )
    keeping = 1.0 - jnp.sum(coupling, axis=2)
    return coupling + keeping[:, :, None] * jnp.eye(cell_count, dtype=jnp.float32)


def recurrence_kernel(*refs, steps, reverse, store_all, side):
    if side:
        pick_ref, side_pick_ref, start_ref, table_ref, side_ref, source_ref, out_ref, side_out_ref = refs
    else:
        pick_ref, start_ref, table_ref, source_ref, out_ref = refs
    def advance(i, rows):
        t = steps - 1 - i if reverse else i
        if side:
            side_out_ref[t] = jnp.dot(
                rows,
                side_ref[side_pick_ref[t]],
                precision=lax.Precision.HIGHEST,
                preferred_element_type=jnp.float32,
            )
        rows = (
            jnp.dot(
                rows,
                table_ref[pick_ref[t]],
                precision=lax.Precision.HIGHEST,
                preferred_element_type=jnp.float32,
            )
            + source_ref[t]
        )
        if store_all:
            out_ref[t] = rows
        return rows

    rows = lax.fori_loop(0, steps, advance, start_ref[...], unroll=UNROLL)
    if not store_all:
        out_ref[...] = rows


def recurrence(pick, start, table, source, reverse, store_all, side=None):
    steps = source.shape[0]
    smem = pl.BlockSpec(memory_space=pltpu.SMEM)
    vmem = pl.BlockSpec(memory_space=pltpu.VMEM)
    out_shape = jax.ShapeDtypeStruct(source.shape if store_all else start.shape, jnp.float32)
    if side is None:
        operands = (pick, start, table, source)
        in_specs = [smem, vmem, vmem, vmem]
        out_specs = vmem
    else:
        side_pick, side_table = side
        operands = (pick, side_pick, start, table, side_table, source)
        in_specs = [smem, smem, vmem, vmem, vmem, vmem]
        out_shape = (out_shape, jax.ShapeDtypeStruct(source.shape, jnp.float32))
        out_specs = (vmem, vmem)
    return pl.pallas_call(
        functools.partial(
            recurrence_kernel,
            steps=steps,
            reverse=reverse,
            store_all=store_all,
            side=side is not None,
        ),
        out_shape=out_shape,
        in_specs=in_specs,
        out_specs=out_specs,
    )(*operands)


def per_band_products(lines, factors, weights):
    steps, rows, states = lines.shape
    bands = factors.shape[0]
    every = accurate_matmul_result(
        lines.reshape(steps * rows, states),
        jnp.transpose(factors, (1, 0, 2)).reshape(states, bands * states),
    ).reshape(steps, rows, bands, states)
    return jnp.sum(every * weights[:, None, :, None], axis=2)


def shards(
    observations,
    band_index,
    obs_mask,
    diffusivity,
    mode_correction_factors,
    mode_backward_factors,
    initial_mean,
):
    steps_dev = observations.shape[0]
    record_rows = observations.shape[1]
    states = initial_mean.shape[0]
    bands = diffusivity.shape[0]
    column_share = states // lax.axis_size("col")
    column_index = lax.axis_index("col")
    time_devices = lax.axis_size("tm")
    time_index = lax.axis_index("tm")
    dynamics = diffusion_matrices(diffusivity, GRID)
    gain = jnp.transpose(mode_correction_factors, (0, 2, 1))
    corrected = dynamics - jnp.einsum(
        "bij,bjk->bik", dynamics, gain, precision=lax.Precision.HIGHEST
    )
    forward_table = jnp.stack([dynamics, corrected], axis=1).reshape(2 * bands, states, states)
    forward_pick = 2 * band_index + obs_mask
    identity = jnp.eye(states, dtype=jnp.float32)
    own_identity = lax.dynamic_slice_in_dim(identity, column_index * column_share, column_share, 0)
    blank_columns = jnp.zeros((steps_dev, column_share, states), jnp.float32)
    band_weights = (band_index[:, None] == jnp.arange(bands)[None, :]).astype(jnp.float32)
    observed_weights = band_weights * obs_mask.astype(jnp.float32)[:, None]
    measured = per_band_products(observations, gain, observed_weights)

    blank_records = jnp.zeros((record_rows, states), jnp.float32)
    forward_rows = recurrence(
        forward_pick, own_identity, forward_table, blank_columns, False, False
    )
    whole_matrix = gathered_rows(forward_rows, "col")
    first_block = time_index == 0

    final_here = (time_index == time_devices - 1) & (jnp.arange(steps_dev) == steps_dev - 1)
    backward = jnp.transpose(mode_backward_factors, (0, 2, 1))
    backward_table = jnp.concatenate([backward, jnp.zeros_like(backward[:1])], axis=0)
    backward_pick = jnp.where(final_here, bands, band_index)
    backward_rows = recurrence(
        backward_pick, own_identity, backward_table, blank_columns, True, False
    )
    whole_back = gathered_rows(backward_rows, "col")

    block_records = recurrence(
        forward_pick, blank_records, forward_table, measured, False, False
    )
    folded_records = jnp.where(
        first_block,
        accurate_matmul_result(initial_mean[None, :], whole_matrix) + block_records,
        block_records,
    )
    folded_matrix = jnp.where(first_block, jnp.zeros_like(whole_matrix), whole_matrix)
    ending_records = doubling_scan(folded_matrix, folded_records, "tm", False, 0)
    start_rows = jnp.where(
        first_block,
        jnp.broadcast_to(initial_mean[None, :], (record_rows, states)),
        passed_along(ending_records, "tm", 1),
    )

    filtered, predicted = recurrence(
        forward_pick,
        start_rows,
        forward_table,
        measured,
        False,
        True,
        side=(band_index, dynamics),
    )
    following = passed_along(predicted[0], "tm", -1)
    next_predicted = jnp.concatenate([predicted[1:], following[None]], axis=0)

    live_weights = band_weights * (1.0 - final_here.astype(jnp.float32))[:, None]
    shift = filtered - per_band_products(next_predicted, backward, live_weights)

    back_records = recurrence(backward_pick, blank_records, backward_table, shift, True, False)
    opening_records = doubling_scan(whole_back, back_records, "tm", True, 1)
    after_records = passed_along(opening_records, "tm", -1)

    smoothed = recurrence(backward_pick, after_records, backward_table, shift, True, True)
    return (filtered, smoothed)


def solution(mesh):
    return jax.shard_map(
        shards,
        mesh=mesh,
        in_specs=(P("tm", "col", None), P("tm"), P("tm"), P(), P(), P(), P()),
        out_specs=(P("tm", "col", None), P("tm", "col", None)),
        check_vma=False,
    )
```

```python
import functools

import jax
import jax.numpy as jnp
from jax import lax
from jax.experimental import pallas as pl
from jax.experimental.pallas import tpu as pltpu
from jax.sharding import PartitionSpec as P

GRID = 16
UNROLL = 4


def passed_along(block, axis, distance):
    devices = range(lax.axis_size(axis))
    route = [(i - distance, i) for i in devices if i - distance in devices]
    return lax.ppermute(block, axis, route)


def gathered_rows(part, axis):
    peers, index = (lax.axis_size(axis), lax.axis_index(axis))
    rows = part.shape[0]
    whole = jnp.zeros((peers * rows,) + part.shape[1:], part.dtype)
    for shift in range(peers):
        if shift == 0:
            got = part
        else:
            got = lax.ppermute(part, axis, [(i, (i + shift) % peers) for i in range(peers)])
        owner = lax.rem(index - shift + peers, peers)
        whole = lax.dynamic_update_slice_in_dim(whole, got, owner * rows, 0)
    return whole


def accurate_matmul_result(first_factor, second_factor):
    return jnp.dot(first_factor, second_factor, precision=lax.Precision.HIGHEST)


def greet_partners(index, peers, other, rounds):
    barrier = pltpu.get_barrier_semaphore()
    partners = 0
    for r in range(rounds):
        distance = 1 << r
        for partner, exists in ((index + distance, index + distance < peers),
                                (index - distance, index - distance >= 0)):
            @pl.when(exists)
            def _():
                pl.semaphore_signal(barrier, inc=1, device_id=(partner, other),
                                    device_id_type=pl.DeviceIdType.MESH)

            partners = partners + jnp.where(exists, 1, 0)
    pl.semaphore_wait(barrier, partners)


def exact_dot(first, second):
    return jnp.dot(first, second, precision=lax.Precision.HIGHEST,
                   preferred_element_type=jnp.float32)


def maps_kernel(ahead_ref, behind_ref, ahead_out, behind_out, ahead_in, behind_in, sems, *, axis):
    peers, index = (lax.axis_size(axis), lax.axis_index(axis))
    other = lax.axis_index("col")
    rounds = ahead_out.shape[0]
    greet_partners(index, peers, other, max(1, rounds - 1))
    ahead_out[0] = ahead_ref[...]
    behind_out[0] = behind_ref[...]
    for r in range(rounds - 1):
        distance = 1 << r
        up, has_up = index + distance, index + distance < peers
        down, has_down = index - distance, index - distance >= 0
        own_ahead = ahead_ref if r == 0 else ahead_out.at[r]
        own_behind = behind_ref if r == 0 else behind_out.at[r]
        ahead_copy = pltpu.make_async_remote_copy(
            src_ref=own_ahead, dst_ref=ahead_in.at[r], send_sem=sems.at[0, 0, r],
            recv_sem=sems.at[0, 1, r], device_id=(up, other),
            device_id_type=pl.DeviceIdType.MESH)
        behind_copy = pltpu.make_async_remote_copy(
            src_ref=own_behind, dst_ref=behind_in.at[r], send_sem=sems.at[1, 0, r],
            recv_sem=sems.at[1, 1, r], device_id=(down, other),
            device_id_type=pl.DeviceIdType.MESH)

        @pl.when(has_up)
        def _():
            ahead_copy.start()

        @pl.when(has_down)
        def _():
            behind_copy.start()

        @pl.when(has_down)
        def _():
            ahead_copy.wait_recv()
            ahead_out[r + 1] = exact_dot(ahead_in[r], own_ahead[...])

        @pl.when(jnp.logical_not(has_down))
        def _():
            ahead_out[r + 1] = own_ahead[...]

        @pl.when(has_up)
        def _():
            behind_copy.wait_recv()
            behind_out[r + 1] = exact_dot(behind_in[r], own_behind[...])

        @pl.when(jnp.logical_not(has_up))
        def _():
            behind_out[r + 1] = own_behind[...]

        @pl.when(has_up)
        def _():
            ahead_copy.wait_send()

        @pl.when(has_down)
        def _():
            behind_copy.wait_send()


def doubling_maps(ahead, behind, axis, collective_id):
    peers = lax.axis_size(axis)
    rounds = max(1, (peers - 1).bit_length())
    states = ahead.shape[0]
    vmem = pl.BlockSpec(memory_space=pltpu.VMEM)
    stack = jax.ShapeDtypeStruct((rounds, states, states), jnp.float32)
    return pl.pallas_call(
        functools.partial(maps_kernel, axis=axis),
        out_shape=(stack, stack),
        in_specs=[vmem, vmem],
        out_specs=(vmem, vmem),
        scratch_shapes=[
            pltpu.VMEM((max(1, rounds - 1), states, states), jnp.float32),
            pltpu.VMEM((max(1, rounds - 1), states, states), jnp.float32),
            pltpu.SemaphoreType.DMA((2, 2, max(1, rounds - 1))),
        ],
        compiler_params=pltpu.CompilerParams(collective_id=collective_id, has_side_effects=True),
    )(ahead, behind)


def records_kernel(maps_ref, records_ref, out_ref, sums, sum_in, sems, *, axis, reverse):
    peers, index = (lax.axis_size(axis), lax.axis_index(axis))
    other = lax.axis_index("col")
    rounds = maps_ref.shape[0]
    greet_partners(index, peers, other, rounds)
    for r in range(rounds):
        distance = 1 << r
        if reverse:
            target, sends = index - distance, index - distance >= 0
            receives = index + distance < peers
        else:
            target, sends = index + distance, index + distance < peers
            receives = index - distance >= 0
        own_sum = records_ref if r == 0 else sums.at[r]
        sum_copy = pltpu.make_async_remote_copy(
            src_ref=own_sum, dst_ref=sum_in.at[r], send_sem=sems.at[0, r],
            recv_sem=sems.at[1, r], device_id=(target, other),
            device_id_type=pl.DeviceIdType.MESH)

        @pl.when(sends)
        def _():
            sum_copy.start()

        @pl.when(receives)
        def _():
            sum_copy.wait_recv()
            sums[r + 1] = exact_dot(sum_in[r], maps_ref[r]) + own_sum[...]

        @pl.when(jnp.logical_not(receives))
        def _():
            sums[r + 1] = own_sum[...]

        @pl.when(sends)
        def _():
            sum_copy.wait_send()

    out_ref[...] = sums[rounds]


def doubling_records(maps, records, axis, reverse, collective_id):
    rounds = maps.shape[0]
    vmem = pl.BlockSpec(memory_space=pltpu.VMEM)
    return pl.pallas_call(
        functools.partial(records_kernel, axis=axis, reverse=reverse),
        out_shape=jax.ShapeDtypeStruct(records.shape, jnp.float32),
        in_specs=[vmem, vmem],
        out_specs=vmem,
        scratch_shapes=[
            pltpu.VMEM((rounds + 1,) + records.shape, jnp.float32),
            pltpu.VMEM((rounds,) + records.shape, jnp.float32),
            pltpu.SemaphoreType.DMA((2, rounds)),
        ],
        compiler_params=pltpu.CompilerParams(collective_id=collective_id, has_side_effects=True),
    )(maps, records)


def diffusion_matrices(diffusivity, side_cells):
    cell_count = side_cells * side_cells
    cell_ids = jnp.arange(cell_count)
    cell_row = cell_ids // side_cells
    cell_col = cell_ids % side_cells
    adjacent = (
        jnp.abs(cell_row[:, None] - cell_row[None, :])
        + jnp.abs(cell_col[:, None] - cell_col[None, :])
        == 1
    )
    coupling = (
        0.5 * (diffusivity[:, :, None] + diffusivity[:, None, :]) * adjacent.astype(jnp.float32)
    )
    keeping = 1.0 - jnp.sum(coupling, axis=2)
    return coupling + keeping[:, :, None] * jnp.eye(cell_count, dtype=jnp.float32)


def recurrence_kernel(*refs, steps, reverse, store_all, side):
    if side:
        pick_ref, side_pick_ref, start_ref, table_ref, side_ref, source_ref, out_ref, side_out_ref = refs
    else:
        pick_ref, start_ref, table_ref, source_ref, out_ref = refs
    def advance(i, rows):
        t = steps - 1 - i if reverse else i
        if side:
            side_out_ref[t] = jnp.dot(
                rows,
                side_ref[side_pick_ref[t]],
                precision=lax.Precision.HIGHEST,
                preferred_element_type=jnp.float32,
            )
        rows = (
            jnp.dot(
                rows,
                table_ref[pick_ref[t]],
                precision=lax.Precision.HIGHEST,
                preferred_element_type=jnp.float32,
            )
            + source_ref[t]
        )
        if store_all:
            out_ref[t] = rows
        return rows

    rows = lax.fori_loop(0, steps, advance, start_ref[...], unroll=UNROLL)
    if not store_all:
        out_ref[...] = rows


def recurrence(pick, start, table, source, reverse, store_all, side=None):
    steps = source.shape[0]
    smem = pl.BlockSpec(memory_space=pltpu.SMEM)
    vmem = pl.BlockSpec(memory_space=pltpu.VMEM)
    out_shape = jax.ShapeDtypeStruct(source.shape if store_all else start.shape, jnp.float32)
    if side is None:
        operands = (pick, start, table, source)
        in_specs = [smem, vmem, vmem, vmem]
        out_specs = vmem
    else:
        side_pick, side_table = side
        operands = (pick, side_pick, start, table, side_table, source)
        in_specs = [smem, smem, vmem, vmem, vmem, vmem]
        out_shape = (out_shape, jax.ShapeDtypeStruct(source.shape, jnp.float32))
        out_specs = (vmem, vmem)
    return pl.pallas_call(
        functools.partial(
            recurrence_kernel,
            steps=steps,
            reverse=reverse,
            store_all=store_all,
            side=side is not None,
        ),
        out_shape=out_shape,
        in_specs=in_specs,
        out_specs=out_specs,
    )(*operands)


def per_band_products(lines, factors, weights):
    steps, rows, states = lines.shape
    bands = factors.shape[0]
    every = accurate_matmul_result(
        lines.reshape(steps * rows, states),
        jnp.transpose(factors, (1, 0, 2)).reshape(states, bands * states),
    ).reshape(steps, rows, bands, states)
    return jnp.sum(every * weights[:, None, :, None], axis=2)


def shards(
    observations,
    band_index,
    obs_mask,
    diffusivity,
    mode_correction_factors,
    mode_backward_factors,
    initial_mean,
):
    steps_dev = observations.shape[0]
    record_rows = observations.shape[1]
    states = initial_mean.shape[0]
    bands = diffusivity.shape[0]
    column_share = states // lax.axis_size("col")
    column_index = lax.axis_index("col")
    time_devices = lax.axis_size("tm")
    time_index = lax.axis_index("tm")
    dynamics = diffusion_matrices(diffusivity, GRID)
    gain = jnp.transpose(mode_correction_factors, (0, 2, 1))
    corrected = dynamics - jnp.einsum(
        "bij,bjk->bik", dynamics, gain, precision=lax.Precision.HIGHEST
    )
    forward_table = jnp.stack([dynamics, corrected], axis=1).reshape(2 * bands, states, states)
    forward_pick = 2 * band_index + obs_mask
    identity = jnp.eye(states, dtype=jnp.float32)
    own_identity = lax.dynamic_slice_in_dim(identity, column_index * column_share, column_share, 0)
    blank_columns = jnp.zeros((steps_dev, column_share, states), jnp.float32)
    band_weights = (band_index[:, None] == jnp.arange(bands)[None, :]).astype(jnp.float32)
    observed_weights = band_weights * obs_mask.astype(jnp.float32)[:, None]
    measured = per_band_products(observations, gain, observed_weights)

    blank_records = jnp.zeros((record_rows, states), jnp.float32)
    forward_rows = recurrence(
        forward_pick, own_identity, forward_table, blank_columns, False, False
    )
    whole_matrix = gathered_rows(forward_rows, "col")
    first_block = time_index == 0

    final_here = (time_index == time_devices - 1) & (jnp.arange(steps_dev) == steps_dev - 1)
    backward = jnp.transpose(mode_backward_factors, (0, 2, 1))
    backward_table = jnp.concatenate([backward, jnp.zeros_like(backward[:1])], axis=0)
    backward_pick = jnp.where(final_here, bands, band_index)
    backward_rows = recurrence(
        backward_pick, own_identity, backward_table, blank_columns, True, False
    )
    whole_back = gathered_rows(backward_rows, "col")
    forward_maps, backward_maps = doubling_maps(
        jnp.where(first_block, jnp.zeros_like(whole_matrix), whole_matrix), whole_back, "tm", 0
    )

    block_records = recurrence(
        forward_pick, blank_records, forward_table, measured, False, False
    )
    folded_records = jnp.where(
        first_block,
        accurate_matmul_result(initial_mean[None, :], whole_matrix) + block_records,
        block_records,
    )
    ending_records = doubling_records(forward_maps, folded_records, "tm", False, 1)
    start_rows = jnp.where(
        first_block,
        jnp.broadcast_to(initial_mean[None, :], (record_rows, states)),
        passed_along(ending_records, "tm", 1),
    )

    filtered, predicted = recurrence(
        forward_pick,
        start_rows,
        forward_table,
        measured,
        False,
        True,
        side=(band_index, dynamics),
    )
    following = passed_along(predicted[0], "tm", -1)
    next_predicted = jnp.concatenate([predicted[1:], following[None]], axis=0)

    live_weights = band_weights * (1.0 - final_here.astype(jnp.float32))[:, None]
    shift = filtered - per_band_products(next_predicted, backward, live_weights)

    back_records = recurrence(backward_pick, blank_records, backward_table, shift, True, False)
    opening_records = doubling_records(backward_maps, back_records, "tm", True, 2)
    after_records = passed_along(opening_records, "tm", -1)

    smoothed = recurrence(backward_pick, after_records, backward_table, shift, True, True)
    return (filtered, smoothed)


def solution(mesh):
    return jax.shard_map(
        shards,
        mesh=mesh,
        in_specs=(P("tm", "col", None), P("tm"), P("tm"), P(), P(), P(), P()),
        out_specs=(P("tm", "col", None), P("tm", "col", None)),
        check_vma=False,
    )
```

```python
import functools

import jax
import jax.numpy as jnp
from jax import lax
from jax.experimental import pallas as pl
from jax.experimental.pallas import tpu as pltpu
from jax.sharding import PartitionSpec as P

GRID = 16
UNROLL = 4


def passed_along(block, axis, distance):
    devices = range(lax.axis_size(axis))
    route = [(i - distance, i) for i in devices if i - distance in devices]
    return lax.ppermute(block, axis, route)


def gathered_rows(part, axis):
    peers, index = (lax.axis_size(axis), lax.axis_index(axis))
    rows = part.shape[0]
    whole = jnp.zeros((peers * rows,) + part.shape[1:], part.dtype)
    for shift in range(peers):
        if shift == 0:
            got = part
        else:
            got = lax.ppermute(part, axis, [(i, (i + shift) % peers) for i in range(peers)])
        owner = lax.rem(index - shift + peers, peers)
        whole = lax.dynamic_update_slice_in_dim(whole, got, owner * rows, 0)
    return whole


def accurate_matmul_result(first_factor, second_factor):
    return jnp.dot(first_factor, second_factor, precision=lax.Precision.HIGHEST)


def greet_partners(index, peers, other, rounds):
    barrier = pltpu.get_barrier_semaphore()
    partners = 0
    for r in range(rounds):
        distance = 1 << r
        for partner, exists in ((index + distance, index + distance < peers),
                                (index - distance, index - distance >= 0)):
            @pl.when(exists)
            def _():
                pl.semaphore_signal(barrier, inc=1, device_id=(partner, other),
                                    device_id_type=pl.DeviceIdType.MESH)

            partners = partners + jnp.where(exists, 1, 0)
    pl.semaphore_wait(barrier, partners)


def exact_dot(first, second):
    return jnp.dot(first, second, precision=lax.Precision.HIGHEST,
                   preferred_element_type=jnp.float32)


def maps_kernel(ahead_ref, behind_ref, records_ref, ahead_out, behind_out, records_out,
                ahead_in, behind_in, sums, sum_in, sems, sum_sems, *, axis):
    peers, index = (lax.axis_size(axis), lax.axis_index(axis))
    other = lax.axis_index("col")
    rounds = ahead_out.shape[0]
    greet_partners(index, peers, other, rounds)
    ahead_out[0] = ahead_ref[...]
    behind_out[0] = behind_ref[...]
    for r in range(rounds):
        distance = 1 << r
        up, has_up = index + distance, index + distance < peers
        down, has_down = index - distance, index - distance >= 0
        own_ahead = ahead_ref if r == 0 else ahead_out.at[r]
        own_sum = records_ref if r == 0 else sums.at[r]
        sum_copy = pltpu.make_async_remote_copy(
            src_ref=own_sum, dst_ref=sum_in.at[r], send_sem=sum_sems.at[0, r],
            recv_sem=sum_sems.at[1, r], device_id=(up, other),
            device_id_type=pl.DeviceIdType.MESH)

        @pl.when(has_up)
        def _():
            sum_copy.start()

        if r == rounds - 1:
            @pl.when(has_down)
            def _():
                sum_copy.wait_recv()
                sums[r + 1] = exact_dot(sum_in[r], own_ahead[...]) + own_sum[...]

            @pl.when(jnp.logical_not(has_down))
            def _():
                sums[r + 1] = own_sum[...]

            @pl.when(has_up)
            def _():
                sum_copy.wait_send()

            break
        own_behind = behind_ref if r == 0 else behind_out.at[r]
        ahead_copy = pltpu.make_async_remote_copy(
            src_ref=own_ahead, dst_ref=ahead_in.at[r], send_sem=sems.at[0, 0, r],
            recv_sem=sems.at[0, 1, r], device_id=(up, other),
            device_id_type=pl.DeviceIdType.MESH)
        behind_copy = pltpu.make_async_remote_copy(
            src_ref=own_behind, dst_ref=behind_in.at[r], send_sem=sems.at[1, 0, r],
            recv_sem=sems.at[1, 1, r], device_id=(down, other),
            device_id_type=pl.DeviceIdType.MESH)

        @pl.when(has_up)
        def _():
            ahead_copy.start()

        @pl.when(has_down)
        def _():
            behind_copy.start()

        @pl.when(has_down)
        def _():
            sum_copy.wait_recv()
            sums[r + 1] = exact_dot(sum_in[r], own_ahead[...]) + own_sum[...]

        @pl.when(jnp.logical_not(has_down))
        def _():
            sums[r + 1] = own_sum[...]

        @pl.when(has_down)
        def _():
            ahead_copy.wait_recv()
            ahead_out[r + 1] = exact_dot(ahead_in[r], own_ahead[...])

        @pl.when(jnp.logical_not(has_down))
        def _():
            ahead_out[r + 1] = own_ahead[...]

        @pl.when(has_up)
        def _():
            behind_copy.wait_recv()
            behind_out[r + 1] = exact_dot(behind_in[r], own_behind[...])

        @pl.when(jnp.logical_not(has_up))
        def _():
            behind_out[r + 1] = own_behind[...]

        @pl.when(has_up)
        def _():
            ahead_copy.wait_send()
            sum_copy.wait_send()

        @pl.when(has_down)
        def _():
            behind_copy.wait_send()

    records_out[...] = sums[rounds]


def doubling_maps(ahead, behind, records, axis, collective_id):
    peers = lax.axis_size(axis)
    rounds = max(1, (peers - 1).bit_length())
    states = ahead.shape[0]
    vmem = pl.BlockSpec(memory_space=pltpu.VMEM)
    stack = jax.ShapeDtypeStruct((rounds, states, states), jnp.float32)
    return pl.pallas_call(
        functools.partial(maps_kernel, axis=axis),
        out_shape=(stack, stack, jax.ShapeDtypeStruct(records.shape, jnp.float32)),
        in_specs=[vmem, vmem, vmem],
        out_specs=(vmem, vmem, vmem),
        scratch_shapes=[
            pltpu.VMEM((max(1, rounds - 1), states, states), jnp.float32),
            pltpu.VMEM((max(1, rounds - 1), states, states), jnp.float32),
            pltpu.VMEM((rounds + 1,) + records.shape, jnp.float32),
            pltpu.VMEM((rounds,) + records.shape, jnp.float32),
            pltpu.SemaphoreType.DMA((2, 2, max(1, rounds - 1))),
            pltpu.SemaphoreType.DMA((2, rounds)),
        ],
        compiler_params=pltpu.CompilerParams(collective_id=collective_id, has_side_effects=True),
    )(ahead, behind, records)


def records_kernel(maps_ref, records_ref, out_ref, sums, sum_in, sems, *, axis, reverse):
    peers, index = (lax.axis_size(axis), lax.axis_index(axis))
    other = lax.axis_index("col")
    rounds = maps_ref.shape[0]
    greet_partners(index, peers, other, rounds)
    for r in range(rounds):
        distance = 1 << r
        if reverse:
            target, sends = index - distance, index - distance >= 0
            receives = index + distance < peers
        else:
            target, sends = index + distance, index + distance < peers
            receives = index - distance >= 0
        own_sum = records_ref if r == 0 else sums.at[r]
        sum_copy = pltpu.make_async_remote_copy(
            src_ref=own_sum, dst_ref=sum_in.at[r], send_sem=sems.at[0, r],
            recv_sem=sems.at[1, r], device_id=(target, other),
            device_id_type=pl.DeviceIdType.MESH)

        @pl.when(sends)
        def _():
            sum_copy.start()

        @pl.when(receives)
        def _():
            sum_copy.wait_recv()
            sums[r + 1] = exact_dot(sum_in[r], maps_ref[r]) + own_sum[...]

        @pl.when(jnp.logical_not(receives))
        def _():
            sums[r + 1] = own_sum[...]

        @pl.when(sends)
        def _():
            sum_copy.wait_send()

    out_ref[...] = sums[rounds]


def doubling_records(maps, records, axis, reverse, collective_id):
    rounds = maps.shape[0]
    vmem = pl.BlockSpec(memory_space=pltpu.VMEM)
    return pl.pallas_call(
        functools.partial(records_kernel, axis=axis, reverse=reverse),
        out_shape=jax.ShapeDtypeStruct(records.shape, jnp.float32),
        in_specs=[vmem, vmem],
        out_specs=vmem,
        scratch_shapes=[
            pltpu.VMEM((rounds + 1,) + records.shape, jnp.float32),
            pltpu.VMEM((rounds,) + records.shape, jnp.float32),
            pltpu.SemaphoreType.DMA((2, rounds)),
        ],
        compiler_params=pltpu.CompilerParams(collective_id=collective_id, has_side_effects=True),
    )(maps, records)


def diffusion_matrices(diffusivity, side_cells):
    cell_count = side_cells * side_cells
    cell_ids = jnp.arange(cell_count)
    cell_row = cell_ids // side_cells
    cell_col = cell_ids % side_cells
    adjacent = (
        jnp.abs(cell_row[:, None] - cell_row[None, :])
        + jnp.abs(cell_col[:, None] - cell_col[None, :])
        == 1
    )
    coupling = (
        0.5 * (diffusivity[:, :, None] + diffusivity[:, None, :]) * adjacent.astype(jnp.float32)
    )
    keeping = 1.0 - jnp.sum(coupling, axis=2)
    return coupling + keeping[:, :, None] * jnp.eye(cell_count, dtype=jnp.float32)


def recurrence_kernel(*refs, steps, reverse, store_all, side):
    if side:
        pick_ref, side_pick_ref, start_ref, table_ref, side_ref, source_ref, out_ref, side_out_ref = refs
    else:
        pick_ref, start_ref, table_ref, source_ref, out_ref = refs
    def advance(i, rows):
        t = steps - 1 - i if reverse else i
        if side:
            side_out_ref[t] = jnp.dot(
                rows,
                side_ref[side_pick_ref[t]],
                precision=lax.Precision.HIGHEST,
                preferred_element_type=jnp.float32,
            )
        rows = (
            jnp.dot(
                rows,
                table_ref[pick_ref[t]],
                precision=lax.Precision.HIGHEST,
                preferred_element_type=jnp.float32,
            )
            + source_ref[t]
        )
        if store_all:
            out_ref[t] = rows
        return rows

    rows = lax.fori_loop(0, steps, advance, start_ref[...], unroll=UNROLL)
    if not store_all:
        out_ref[...] = rows


def recurrence(pick, start, table, source, reverse, store_all, side=None):
    steps = source.shape[0]
    smem = pl.BlockSpec(memory_space=pltpu.SMEM)
    vmem = pl.BlockSpec(memory_space=pltpu.VMEM)
    out_shape = jax.ShapeDtypeStruct(source.shape if store_all else start.shape, jnp.float32)
    if side is None:
        operands = (pick, start, table, source)
        in_specs = [smem, vmem, vmem, vmem]
        out_specs = vmem
    else:
        side_pick, side_table = side
        operands = (pick, side_pick, start, table, side_table, source)
        in_specs = [smem, smem, vmem, vmem, vmem, vmem]
        out_shape = (out_shape, jax.ShapeDtypeStruct(source.shape, jnp.float32))
        out_specs = (vmem, vmem)
    return pl.pallas_call(
        functools.partial(
            recurrence_kernel,
            steps=steps,
            reverse=reverse,
            store_all=store_all,
            side=side is not None,
        ),
        out_shape=out_shape,
        in_specs=in_specs,
        out_specs=out_specs,
    )(*operands)


def per_band_products(lines, factors, weights):
    steps, rows, states = lines.shape
    bands = factors.shape[0]
    every = accurate_matmul_result(
        lines.reshape(steps * rows, states),
        jnp.transpose(factors, (1, 0, 2)).reshape(states, bands * states),
    ).reshape(steps, rows, bands, states)
    return jnp.sum(every * weights[:, None, :, None], axis=2)


def shards(
    observations,
    band_index,
    obs_mask,
    diffusivity,
    mode_correction_factors,
    mode_backward_factors,
    initial_mean,
):
    steps_dev = observations.shape[0]
    record_rows = observations.shape[1]
    states = initial_mean.shape[0]
    bands = diffusivity.shape[0]
    column_share = states // lax.axis_size("col")
    column_index = lax.axis_index("col")
    time_devices = lax.axis_size("tm")
    time_index = lax.axis_index("tm")
    dynamics = diffusion_matrices(diffusivity, GRID)
    gain = jnp.transpose(mode_correction_factors, (0, 2, 1))
    corrected = dynamics - jnp.einsum(
        "bij,bjk->bik", dynamics, gain, precision=lax.Precision.HIGHEST
    )
    forward_table = jnp.stack([dynamics, corrected], axis=1).reshape(2 * bands, states, states)
    forward_pick = 2 * band_index + obs_mask
    identity = jnp.eye(states, dtype=jnp.float32)
    own_identity = lax.dynamic_slice_in_dim(identity, column_index * column_share, column_share, 0)
    blank_columns = jnp.zeros((steps_dev, column_share, states), jnp.float32)
    band_weights = (band_index[:, None] == jnp.arange(bands)[None, :]).astype(jnp.float32)
    observed_weights = band_weights * obs_mask.astype(jnp.float32)[:, None]
    measured = per_band_products(observations, gain, observed_weights)

    blank_records = jnp.zeros((record_rows, states), jnp.float32)
    forward_rows = recurrence(
        forward_pick, own_identity, forward_table, blank_columns, False, False
    )
    whole_matrix = gathered_rows(forward_rows, "col")
    first_block = time_index == 0

    final_here = (time_index == time_devices - 1) & (jnp.arange(steps_dev) == steps_dev - 1)
    backward = jnp.transpose(mode_backward_factors, (0, 2, 1))
    backward_table = jnp.concatenate([backward, jnp.zeros_like(backward[:1])], axis=0)
    backward_pick = jnp.where(final_here, bands, band_index)
    backward_rows = recurrence(
        backward_pick, own_identity, backward_table, blank_columns, True, False
    )
    whole_back = gathered_rows(backward_rows, "col")
    block_records = recurrence(
        forward_pick, blank_records, forward_table, measured, False, False
    )
    folded_records = jnp.where(
        first_block,
        accurate_matmul_result(initial_mean[None, :], whole_matrix) + block_records,
        block_records,
    )
    _, backward_maps, ending_records = doubling_maps(
        jnp.where(first_block, jnp.zeros_like(whole_matrix), whole_matrix),
        whole_back,
        folded_records,
        "tm",
        0,
    )
    start_rows = jnp.where(
        first_block,
        jnp.broadcast_to(initial_mean[None, :], (record_rows, states)),
        passed_along(ending_records, "tm", 1),
    )

    filtered, predicted = recurrence(
        forward_pick,
        start_rows,
        forward_table,
        measured,
        False,
        True,
        side=(band_index, dynamics),
    )
    following = passed_along(predicted[0], "tm", -1)
    next_predicted = jnp.concatenate([predicted[1:], following[None]], axis=0)

    live_weights = band_weights * (1.0 - final_here.astype(jnp.float32))[:, None]
    shift = filtered - per_band_products(next_predicted, backward, live_weights)

    back_records = recurrence(backward_pick, blank_records, backward_table, shift, True, False)
    opening_records = doubling_records(backward_maps, back_records, "tm", True, 1)
    after_records = passed_along(opening_records, "tm", -1)

    smoothed = recurrence(backward_pick, after_records, backward_table, shift, True, True)
    return (filtered, smoothed)


def solution(mesh):
    return jax.shard_map(
        shards,
        mesh=mesh,
        in_specs=(P("tm", "col", None), P("tm"), P("tm"), P(), P(), P(), P()),
        out_specs=(P("tm", "col", None), P("tm", "col", None)),
        check_vma=False,
    )
```

```python
import functools

import jax
import jax.numpy as jnp
from jax import lax
from jax.experimental import pallas as pl
from jax.experimental.pallas import tpu as pltpu
from jax.sharding import PartitionSpec as P

GRID = 16
UNROLL = 4


def passed_along(block, axis, distance):
    devices = range(lax.axis_size(axis))
    route = [(i - distance, i) for i in devices if i - distance in devices]
    return lax.ppermute(block, axis, route)


def gathered_rows(part, axis):
    peers, index = (lax.axis_size(axis), lax.axis_index(axis))
    rows = part.shape[0]
    whole = jnp.zeros((peers * rows,) + part.shape[1:], part.dtype)
    for shift in range(peers):
        if shift == 0:
            got = part
        else:
            got = lax.ppermute(part, axis, [(i, (i + shift) % peers) for i in range(peers)])
        owner = lax.rem(index - shift + peers, peers)
        whole = lax.dynamic_update_slice_in_dim(whole, got, owner * rows, 0)
    return whole


def accurate_matmul_result(first_factor, second_factor):
    return jnp.dot(first_factor, second_factor, precision=lax.Precision.HIGHEST)


def greet_partners(index, peers, other, rounds):
    barrier = pltpu.get_barrier_semaphore()
    partners = 0
    for r in range(rounds):
        distance = 1 << r
        for partner, exists in ((index + distance, index + distance < peers),
                                (index - distance, index - distance >= 0)):
            @pl.when(exists)
            def _():
                pl.semaphore_signal(barrier, inc=1, device_id=(partner, other),
                                    device_id_type=pl.DeviceIdType.MESH)

            partners = partners + jnp.where(exists, 1, 0)
    pl.semaphore_wait(barrier, partners)


def exact_dot(first, second):
    return jnp.dot(first, second, precision=lax.Precision.HIGHEST,
                   preferred_element_type=jnp.float32)


def maps_kernel(ahead_ref, behind_ref, records_ref, ahead_out, behind_out, records_out,
                ahead_in, behind_in, sums, sum_in, sems, sum_sems, *, axis):
    peers, index = (lax.axis_size(axis), lax.axis_index(axis))
    other = lax.axis_index("col")
    rounds = ahead_out.shape[0]
    greet_partners(index, peers, other, rounds)
    ahead_out[0] = ahead_ref[...]
    behind_out[0] = behind_ref[...]
    for r in range(rounds):
        distance = 1 << r
        up, has_up = index + distance, index + distance < peers
        down, has_down = index - distance, index - distance >= 0
        own_ahead = ahead_ref if r == 0 else ahead_out.at[r]
        own_sum = records_ref if r == 0 else sums.at[r]
        sum_copy = pltpu.make_async_remote_copy(
            src_ref=own_sum, dst_ref=sum_in.at[r], send_sem=sum_sems.at[0, r],
            recv_sem=sum_sems.at[1, r], device_id=(up, other),
            device_id_type=pl.DeviceIdType.MESH)

        @pl.when(has_up)
        def _():
            sum_copy.start()

        if r == rounds - 1:
            @pl.when(has_down)
            def _():
                sum_copy.wait_recv()
                sums[r + 1] = exact_dot(sum_in[r], own_ahead[...]) + own_sum[...]

            @pl.when(jnp.logical_not(has_down))
            def _():
                sums[r + 1] = own_sum[...]

            @pl.when(has_up)
            def _():
                sum_copy.wait_send()

            break
        own_behind = behind_ref if r == 0 else behind_out.at[r]
        ahead_copy = pltpu.make_async_remote_copy(
            src_ref=own_ahead, dst_ref=ahead_in.at[r], send_sem=sems.at[0, 0, r],
            recv_sem=sems.at[0, 1, r], device_id=(up, other),
            device_id_type=pl.DeviceIdType.MESH)
        behind_copy = pltpu.make_async_remote_copy(
            src_ref=own_behind, dst_ref=behind_in.at[r], send_sem=sems.at[1, 0, r],
            recv_sem=sems.at[1, 1, r], device_id=(down, other),
            device_id_type=pl.DeviceIdType.MESH)

        @pl.when(has_up)
        def _():
            ahead_copy.start()

        @pl.when(has_down)
        def _():
            behind_copy.start()

        @pl.when(has_down)
        def _():
            sum_copy.wait_recv()
            sums[r + 1] = exact_dot(sum_in[r], own_ahead[...]) + own_sum[...]

        @pl.when(jnp.logical_not(has_down))
        def _():
            sums[r + 1] = own_sum[...]

        @pl.when(has_down)
        def _():
            ahead_copy.wait_recv()
            ahead_out[r + 1] = exact_dot(ahead_in[r], own_ahead[...])

        @pl.when(jnp.logical_not(has_down))
        def _():
            ahead_out[r + 1] = own_ahead[...]

        @pl.when(has_up)
        def _():
            behind_copy.wait_recv()
            behind_out[r + 1] = exact_dot(behind_in[r], own_behind[...])

        @pl.when(jnp.logical_not(has_up))
        def _():
            behind_out[r + 1] = own_behind[...]

        @pl.when(has_up)
        def _():
            ahead_copy.wait_send()
            sum_copy.wait_send()

        @pl.when(has_down)
        def _():
            behind_copy.wait_send()

    records_out[...] = sums[rounds]


def doubling_maps(ahead, behind, records, axis, collective_id):
    peers = lax.axis_size(axis)
    rounds = max(1, (peers - 1).bit_length())
    states = ahead.shape[0]
    vmem = pl.BlockSpec(memory_space=pltpu.VMEM)
    stack = jax.ShapeDtypeStruct((rounds, states, states), jnp.float32)
    return pl.pallas_call(
        functools.partial(maps_kernel, axis=axis),
        out_shape=(stack, stack, jax.ShapeDtypeStruct(records.shape, jnp.float32)),
        in_specs=[vmem, vmem, vmem],
        out_specs=(vmem, vmem, vmem),
        scratch_shapes=[
            pltpu.VMEM((max(1, rounds - 1), states, states), jnp.float32),
            pltpu.VMEM((max(1, rounds - 1), states, states), jnp.float32),
            pltpu.VMEM((rounds + 1,) + records.shape, jnp.float32),
            pltpu.VMEM((rounds,) + records.shape, jnp.float32),
            pltpu.SemaphoreType.DMA((2, 2, max(1, rounds - 1))),
            pltpu.SemaphoreType.DMA((2, rounds)),
        ],
        compiler_params=pltpu.CompilerParams(collective_id=collective_id, has_side_effects=True),
    )(ahead, behind, records)


def records_kernel(maps_ref, records_ref, out_ref, sums, sum_in, sems, *, axis, reverse):
    peers, index = (lax.axis_size(axis), lax.axis_index(axis))
    other = lax.axis_index("col")
    rounds = maps_ref.shape[0]
    greet_partners(index, peers, other, rounds)
    for r in range(rounds):
        distance = 1 << r
        if reverse:
            target, sends = index - distance, index - distance >= 0
            receives = index + distance < peers
        else:
            target, sends = index + distance, index + distance < peers
            receives = index - distance >= 0
        own_sum = records_ref if r == 0 else sums.at[r]
        sum_copy = pltpu.make_async_remote_copy(
            src_ref=own_sum, dst_ref=sum_in.at[r], send_sem=sems.at[0, r],
            recv_sem=sems.at[1, r], device_id=(target, other),
            device_id_type=pl.DeviceIdType.MESH)

        @pl.when(sends)
        def _():
            sum_copy.start()

        @pl.when(receives)
        def _():
            sum_copy.wait_recv()
            sums[r + 1] = exact_dot(sum_in[r], maps_ref[r]) + own_sum[...]

        @pl.when(jnp.logical_not(receives))
        def _():
            sums[r + 1] = own_sum[...]

        @pl.when(sends)
        def _():
            sum_copy.wait_send()

    out_ref[...] = sums[rounds]


def doubling_records(maps, records, axis, reverse, collective_id):
    rounds = maps.shape[0]
    vmem = pl.BlockSpec(memory_space=pltpu.VMEM)
    return pl.pallas_call(
        functools.partial(records_kernel, axis=axis, reverse=reverse),
        out_shape=jax.ShapeDtypeStruct(records.shape, jnp.float32),
        in_specs=[vmem, vmem],
        out_specs=vmem,
        scratch_shapes=[
            pltpu.VMEM((rounds + 1,) + records.shape, jnp.float32),
            pltpu.VMEM((rounds,) + records.shape, jnp.float32),
            pltpu.SemaphoreType.DMA((2, rounds)),
        ],
        compiler_params=pltpu.CompilerParams(collective_id=collective_id, has_side_effects=True),
    )(maps, records)


def diffusion_matrices(diffusivity, side_cells):
    cell_count = side_cells * side_cells
    cell_ids = jnp.arange(cell_count)
    cell_row = cell_ids // side_cells
    cell_col = cell_ids % side_cells
    adjacent = (
        jnp.abs(cell_row[:, None] - cell_row[None, :])
        + jnp.abs(cell_col[:, None] - cell_col[None, :])
        == 1
    )
    coupling = (
        0.5 * (diffusivity[:, :, None] + diffusivity[:, None, :]) * adjacent.astype(jnp.float32)
    )
    keeping = 1.0 - jnp.sum(coupling, axis=2)
    return coupling + keeping[:, :, None] * jnp.eye(cell_count, dtype=jnp.float32)


def recurrence_kernel(*refs, steps, reverse, store_all, side):
    if side:
        pick_ref, side_pick_ref, start_ref, table_ref, side_ref, source_ref, out_ref, side_out_ref = refs
    else:
        pick_ref, start_ref, table_ref, source_ref, out_ref = refs
    def advance(i, rows):
        t = steps - 1 - i if reverse else i
        if side:
            side_out_ref[t] = jnp.dot(
                rows,
                side_ref[side_pick_ref[t]],
                precision=lax.Precision.HIGHEST,
                preferred_element_type=jnp.float32,
            )
        rows = (
            jnp.dot(
                rows,
                table_ref[pick_ref[t]],
                precision=lax.Precision.HIGHEST,
                preferred_element_type=jnp.float32,
            )
            + source_ref[t]
        )
        if store_all:
            out_ref[t] = rows
        return rows

    rows = lax.fori_loop(0, steps, advance, start_ref[...], unroll=UNROLL)
    if not store_all:
        out_ref[...] = rows


def recurrence(pick, start, table, source, reverse, store_all, side=None):
    steps = source.shape[0]
    smem = pl.BlockSpec(memory_space=pltpu.SMEM)
    vmem = pl.BlockSpec(memory_space=pltpu.VMEM)
    out_shape = jax.ShapeDtypeStruct(source.shape if store_all else start.shape, jnp.float32)
    if side is None:
        operands = (pick, start, table, source)
        in_specs = [smem, vmem, vmem, vmem]
        out_specs = vmem
    else:
        side_pick, side_table = side
        operands = (pick, side_pick, start, table, side_table, source)
        in_specs = [smem, smem, vmem, vmem, vmem, vmem]
        out_shape = (out_shape, jax.ShapeDtypeStruct(source.shape, jnp.float32))
        out_specs = (vmem, vmem)
    return pl.pallas_call(
        functools.partial(
            recurrence_kernel,
            steps=steps,
            reverse=reverse,
            store_all=store_all,
            side=side is not None,
        ),
        out_shape=out_shape,
        in_specs=in_specs,
        out_specs=out_specs,
    )(*operands)


def paired_kernel(ahead_pick_ref, behind_pick_ref, ahead_start_ref, behind_start_ref,
                  ahead_table_ref, behind_table_ref, ahead_source_ref, ahead_out, behind_out,
                  *, steps):
    def advance(i, carry):
        ahead, behind = carry
        back = steps - 1 - i
        ahead = exact_dot(ahead, ahead_table_ref[ahead_pick_ref[i]]) + ahead_source_ref[i]
        behind = exact_dot(behind, behind_table_ref[behind_pick_ref[back]])
        return ahead, behind

    ahead, behind = lax.fori_loop(
        0, steps, advance, (ahead_start_ref[...], behind_start_ref[...]), unroll=UNROLL
    )
    ahead_out[...] = ahead
    behind_out[...] = behind


def paired_maps(ahead_pick, behind_pick, ahead_start, behind_start, ahead_table, behind_table,
                ahead_source):
    smem = pl.BlockSpec(memory_space=pltpu.SMEM)
    vmem = pl.BlockSpec(memory_space=pltpu.VMEM)
    return pl.pallas_call(
        functools.partial(paired_kernel, steps=ahead_source.shape[0]),
        out_shape=(
            jax.ShapeDtypeStruct(ahead_start.shape, jnp.float32),
            jax.ShapeDtypeStruct(behind_start.shape, jnp.float32),
        ),
        in_specs=[smem, smem, vmem, vmem, vmem, vmem, vmem],
        out_specs=(vmem, vmem),
    )(ahead_pick, behind_pick, ahead_start, behind_start, ahead_table, behind_table, ahead_source)


def per_band_products(lines, factors, weights):
    steps, rows, states = lines.shape
    bands = factors.shape[0]
    every = accurate_matmul_result(
        lines.reshape(steps * rows, states),
        jnp.transpose(factors, (1, 0, 2)).reshape(states, bands * states),
    ).reshape(steps, rows, bands, states)
    return jnp.sum(every * weights[:, None, :, None], axis=2)


def shards(
    observations,
    band_index,
    obs_mask,
    diffusivity,
    mode_correction_factors,
    mode_backward_factors,
    initial_mean,
):
    steps_dev = observations.shape[0]
    record_rows = observations.shape[1]
    states = initial_mean.shape[0]
    bands = diffusivity.shape[0]
    column_share = states // lax.axis_size("col")
    column_index = lax.axis_index("col")
    time_devices = lax.axis_size("tm")
    time_index = lax.axis_index("tm")
    dynamics = diffusion_matrices(diffusivity, GRID)
    gain = jnp.transpose(mode_correction_factors, (0, 2, 1))
    corrected = dynamics - jnp.einsum(
        "bij,bjk->bik", dynamics, gain, precision=lax.Precision.HIGHEST
    )
    forward_table = jnp.stack([dynamics, corrected], axis=1).reshape(2 * bands, states, states)
    forward_pick = 2 * band_index + obs_mask
    identity = jnp.eye(states, dtype=jnp.float32)
    own_identity = lax.dynamic_slice_in_dim(identity, column_index * column_share, column_share, 0)
    blank_columns = jnp.zeros((steps_dev, column_share, states), jnp.float32)
    band_weights = (band_index[:, None] == jnp.arange(bands)[None, :]).astype(jnp.float32)
    observed_weights = band_weights * obs_mask.astype(jnp.float32)[:, None]
    measured = per_band_products(observations, gain, observed_weights)

    blank_records = jnp.zeros((record_rows, states), jnp.float32)
    first_block = time_index == 0
    final_here = (time_index == time_devices - 1) & (jnp.arange(steps_dev) == steps_dev - 1)
    backward = jnp.transpose(mode_backward_factors, (0, 2, 1))
    backward_table = jnp.concatenate([backward, jnp.zeros_like(backward[:1])], axis=0)
    backward_pick = jnp.where(final_here, bands, band_index)
    forward_rows, backward_rows = paired_maps(
        forward_pick,
        backward_pick,
        jnp.concatenate([own_identity, blank_records], axis=0),
        own_identity,
        forward_table,
        backward_table,
        jnp.concatenate([blank_columns, measured], axis=1),
    )
    whole_matrix = gathered_rows(forward_rows[:column_share], "col")
    whole_back = gathered_rows(backward_rows, "col")
    block_records = forward_rows[column_share:]
    folded_records = jnp.where(
        first_block,
        accurate_matmul_result(initial_mean[None, :], whole_matrix) + block_records,
        block_records,
    )
    _, backward_maps, ending_records = doubling_maps(
        jnp.where(first_block, jnp.zeros_like(whole_matrix), whole_matrix),
        whole_back,
        folded_records,
        "tm",
        0,
    )
    start_rows = jnp.where(
        first_block,
        jnp.broadcast_to(initial_mean[None, :], (record_rows, states)),
        passed_along(ending_records, "tm", 1),
    )

    filtered, predicted = recurrence(
        forward_pick,
        start_rows,
        forward_table,
        measured,
        False,
        True,
        side=(band_index, dynamics),
    )
    following = passed_along(predicted[0], "tm", -1)
    next_predicted = jnp.concatenate([predicted[1:], following[None]], axis=0)

    live_weights = band_weights * (1.0 - final_here.astype(jnp.float32))[:, None]
    shift = filtered - per_band_products(next_predicted, backward, live_weights)

    back_records = recurrence(backward_pick, blank_records, backward_table, shift, True, False)
    opening_records = doubling_records(backward_maps, back_records, "tm", True, 1)
    after_records = passed_along(opening_records, "tm", -1)

    smoothed = recurrence(backward_pick, after_records, backward_table, shift, True, True)
    return (filtered, smoothed)


def solution(mesh):
    return jax.shard_map(
        shards,
        mesh=mesh,
        in_specs=(P("tm", "col", None), P("tm"), P("tm"), P(), P(), P(), P()),
        out_specs=(P("tm", "col", None), P("tm", "col", None)),
        check_vma=False,
    )
```

```python
import functools

import jax
import jax.numpy as jnp
from jax import lax
from jax.experimental import pallas as pl
from jax.experimental.pallas import tpu as pltpu
from jax.sharding import PartitionSpec as P

GRID = 16
UNROLL = 4


def passed_along(block, axis, distance):
    devices = range(lax.axis_size(axis))
    route = [(i - distance, i) for i in devices if i - distance in devices]
    return lax.ppermute(block, axis, route)


def gathered_rows(part, axis):
    peers, index = (lax.axis_size(axis), lax.axis_index(axis))
    rows = part.shape[0]
    whole = jnp.zeros((peers * rows,) + part.shape[1:], part.dtype)
    for shift in range(peers):
        if shift == 0:
            got = part
        else:
            got = lax.ppermute(part, axis, [(i, (i + shift) % peers) for i in range(peers)])
        owner = lax.rem(index - shift + peers, peers)
        whole = lax.dynamic_update_slice_in_dim(whole, got, owner * rows, 0)
    return whole


def accurate_matmul_result(first_factor, second_factor):
    return jnp.dot(first_factor, second_factor, precision=lax.Precision.HIGHEST)


def greet_partners(index, peers, other, rounds):
    barrier = pltpu.get_barrier_semaphore()
    partners = 0
    for r in range(rounds):
        distance = 1 << r
        for partner, exists in ((index + distance, index + distance < peers),
                                (index - distance, index - distance >= 0)):
            @pl.when(exists)
            def _():
                pl.semaphore_signal(barrier, inc=1, device_id=(partner, other),
                                    device_id_type=pl.DeviceIdType.MESH)

            partners = partners + jnp.where(exists, 1, 0)
    pl.semaphore_wait(barrier, partners)


def map_dot(first, second):
    return jnp.dot(first, second, precision=lax.Precision.HIGH,
                   preferred_element_type=jnp.float32)


def exact_dot(first, second):
    return jnp.dot(first, second, precision=lax.Precision.HIGHEST,
                   preferred_element_type=jnp.float32)


def maps_kernel(ahead_ref, behind_ref, records_ref, ahead_out, behind_out, records_out,
                ahead_in, behind_in, sums, sum_in, sems, sum_sems, *, axis):
    peers, index = (lax.axis_size(axis), lax.axis_index(axis))
    other = lax.axis_index("col")
    rounds = ahead_out.shape[0]
    greet_partners(index, peers, other, rounds)
    ahead_out[0] = ahead_ref[...]
    behind_out[0] = behind_ref[...]
    for r in range(rounds):
        distance = 1 << r
        up, has_up = index + distance, index + distance < peers
        down, has_down = index - distance, index - distance >= 0
        own_ahead = ahead_ref if r == 0 else ahead_out.at[r]
        own_sum = records_ref if r == 0 else sums.at[r]
        sum_copy = pltpu.make_async_remote_copy(
            src_ref=own_sum, dst_ref=sum_in.at[r], send_sem=sum_sems.at[0, r],
            recv_sem=sum_sems.at[1, r], device_id=(up, other),
            device_id_type=pl.DeviceIdType.MESH)

        @pl.when(has_up)
        def _():
            sum_copy.start()

        if r == rounds - 1:
            @pl.when(has_down)
            def _():
                sum_copy.wait_recv()
                sums[r + 1] = exact_dot(sum_in[r], own_ahead[...]) + own_sum[...]

            @pl.when(jnp.logical_not(has_down))
            def _():
                sums[r + 1] = own_sum[...]

            @pl.when(has_up)
            def _():
                sum_copy.wait_send()

            break
        own_behind = behind_ref if r == 0 else behind_out.at[r]
        ahead_copy = pltpu.make_async_remote_copy(
            src_ref=own_ahead, dst_ref=ahead_in.at[r], send_sem=sems.at[0, 0, r],
            recv_sem=sems.at[0, 1, r], device_id=(up, other),
            device_id_type=pl.DeviceIdType.MESH)
        behind_copy = pltpu.make_async_remote_copy(
            src_ref=own_behind, dst_ref=behind_in.at[r], send_sem=sems.at[1, 0, r],
            recv_sem=sems.at[1, 1, r], device_id=(down, other),
            device_id_type=pl.DeviceIdType.MESH)

        @pl.when(has_up)
        def _():
            ahead_copy.start()

        @pl.when(has_down)
        def _():
            behind_copy.start()

        @pl.when(has_down)
        def _():
            sum_copy.wait_recv()
            sums[r + 1] = exact_dot(sum_in[r], own_ahead[...]) + own_sum[...]

        @pl.when(jnp.logical_not(has_down))
        def _():
            sums[r + 1] = own_sum[...]

        @pl.when(has_down)
        def _():
            ahead_copy.wait_recv()
            ahead_out[r + 1] = map_dot(ahead_in[r], own_ahead[...])

        @pl.when(jnp.logical_not(has_down))
        def _():
            ahead_out[r + 1] = own_ahead[...]

        @pl.when(has_up)
        def _():
            behind_copy.wait_recv()
            behind_out[r + 1] = map_dot(behind_in[r], own_behind[...])

        @pl.when(jnp.logical_not(has_up))
        def _():
            behind_out[r + 1] = own_behind[...]

        @pl.when(has_up)
        def _():
            ahead_copy.wait_send()
            sum_copy.wait_send()

        @pl.when(has_down)
        def _():
            behind_copy.wait_send()

    records_out[...] = sums[rounds]


def doubling_maps(ahead, behind, records, axis, collective_id):
    peers = lax.axis_size(axis)
    rounds = max(1, (peers - 1).bit_length())
    states = ahead.shape[0]
    vmem = pl.BlockSpec(memory_space=pltpu.VMEM)
    stack = jax.ShapeDtypeStruct((rounds, states, states), jnp.float32)
    return pl.pallas_call(
        functools.partial(maps_kernel, axis=axis),
        out_shape=(stack, stack, jax.ShapeDtypeStruct(records.shape, jnp.float32)),
        in_specs=[vmem, vmem, vmem],
        out_specs=(vmem, vmem, vmem),
        scratch_shapes=[
            pltpu.VMEM((max(1, rounds - 1), states, states), jnp.float32),
            pltpu.VMEM((max(1, rounds - 1), states, states), jnp.float32),
            pltpu.VMEM((rounds + 1,) + records.shape, jnp.float32),
            pltpu.VMEM((rounds,) + records.shape, jnp.float32),
            pltpu.SemaphoreType.DMA((2, 2, max(1, rounds - 1))),
            pltpu.SemaphoreType.DMA((2, rounds)),
        ],
        compiler_params=pltpu.CompilerParams(collective_id=collective_id, has_side_effects=True),
    )(ahead, behind, records)


def records_kernel(maps_ref, records_ref, out_ref, sums, sum_in, sems, *, axis, reverse):
    peers, index = (lax.axis_size(axis), lax.axis_index(axis))
    other = lax.axis_index("col")
    rounds = maps_ref.shape[0]
    greet_partners(index, peers, other, rounds)
    for r in range(rounds):
        distance = 1 << r
        if reverse:
            target, sends = index - distance, index - distance >= 0
            receives = index + distance < peers
        else:
            target, sends = index + distance, index + distance < peers
            receives = index - distance >= 0
        own_sum = records_ref if r == 0 else sums.at[r]
        sum_copy = pltpu.make_async_remote_copy(
            src_ref=own_sum, dst_ref=sum_in.at[r], send_sem=sems.at[0, r],
            recv_sem=sems.at[1, r], device_id=(target, other),
            device_id_type=pl.DeviceIdType.MESH)

        @pl.when(sends)
        def _():
            sum_copy.start()

        @pl.when(receives)
        def _():
            sum_copy.wait_recv()
            sums[r + 1] = exact_dot(sum_in[r], maps_ref[r]) + own_sum[...]

        @pl.when(jnp.logical_not(receives))
        def _():
            sums[r + 1] = own_sum[...]

        @pl.when(sends)
        def _():
            sum_copy.wait_send()

    out_ref[...] = sums[rounds]


def doubling_records(maps, records, axis, reverse, collective_id):
    rounds = maps.shape[0]
    vmem = pl.BlockSpec(memory_space=pltpu.VMEM)
    return pl.pallas_call(
        functools.partial(records_kernel, axis=axis, reverse=reverse),
        out_shape=jax.ShapeDtypeStruct(records.shape, jnp.float32),
        in_specs=[vmem, vmem],
        out_specs=vmem,
        scratch_shapes=[
            pltpu.VMEM((rounds + 1,) + records.shape, jnp.float32),
            pltpu.VMEM((rounds,) + records.shape, jnp.float32),
            pltpu.SemaphoreType.DMA((2, rounds)),
        ],
        compiler_params=pltpu.CompilerParams(collective_id=collective_id, has_side_effects=True),
    )(maps, records)


def diffusion_matrices(diffusivity, side_cells):
    cell_count = side_cells * side_cells
    cell_ids = jnp.arange(cell_count)
    cell_row = cell_ids // side_cells
    cell_col = cell_ids % side_cells
    adjacent = (
        jnp.abs(cell_row[:, None] - cell_row[None, :])
        + jnp.abs(cell_col[:, None] - cell_col[None, :])
        == 1
    )
    coupling = (
        0.5 * (diffusivity[:, :, None] + diffusivity[:, None, :]) * adjacent.astype(jnp.float32)
    )
    keeping = 1.0 - jnp.sum(coupling, axis=2)
    return coupling + keeping[:, :, None] * jnp.eye(cell_count, dtype=jnp.float32)


def recurrence_kernel(*refs, steps, reverse, store_all, side):
    if side:
        pick_ref, side_pick_ref, start_ref, table_ref, side_ref, source_ref, out_ref, side_out_ref = refs
    else:
        pick_ref, start_ref, table_ref, source_ref, out_ref = refs
    def advance(i, rows):
        t = steps - 1 - i if reverse else i
        if side:
            side_out_ref[t] = jnp.dot(
                rows,
                side_ref[side_pick_ref[t]],
                precision=lax.Precision.HIGHEST,
                preferred_element_type=jnp.float32,
            )
        rows = (
            jnp.dot(
                rows,
                table_ref[pick_ref[t]],
                precision=lax.Precision.HIGHEST,
                preferred_element_type=jnp.float32,
            )
            + source_ref[t]
        )
        if store_all:
            out_ref[t] = rows
        return rows

    rows = lax.fori_loop(0, steps, advance, start_ref[...], unroll=UNROLL)
    if not store_all:
        out_ref[...] = rows


def recurrence(pick, start, table, source, reverse, store_all, side=None):
    steps = source.shape[0]
    smem = pl.BlockSpec(memory_space=pltpu.SMEM)
    vmem = pl.BlockSpec(memory_space=pltpu.VMEM)
    out_shape = jax.ShapeDtypeStruct(source.shape if store_all else start.shape, jnp.float32)
    if side is None:
        operands = (pick, start, table, source)
        in_specs = [smem, vmem, vmem, vmem]
        out_specs = vmem
    else:
        side_pick, side_table = side
        operands = (pick, side_pick, start, table, side_table, source)
        in_specs = [smem, smem, vmem, vmem, vmem, vmem]
        out_shape = (out_shape, jax.ShapeDtypeStruct(source.shape, jnp.float32))
        out_specs = (vmem, vmem)
    return pl.pallas_call(
        functools.partial(
            recurrence_kernel,
            steps=steps,
            reverse=reverse,
            store_all=store_all,
            side=side is not None,
        ),
        out_shape=out_shape,
        in_specs=in_specs,
        out_specs=out_specs,
    )(*operands)


def paired_kernel(ahead_pick_ref, behind_pick_ref, ahead_start_ref, behind_start_ref,
                  ahead_table_ref, behind_table_ref, ahead_source_ref, ahead_out, behind_out,
                  *, steps):
    def advance(i, carry):
        ahead, behind = carry
        back = steps - 1 - i
        ahead = exact_dot(ahead, ahead_table_ref[ahead_pick_ref[i]]) + ahead_source_ref[i]
        behind = exact_dot(behind, behind_table_ref[behind_pick_ref[back]])
        return ahead, behind

    ahead, behind = lax.fori_loop(
        0, steps, advance, (ahead_start_ref[...], behind_start_ref[...]), unroll=UNROLL
    )
    ahead_out[...] = ahead
    behind_out[...] = behind


def paired_maps(ahead_pick, behind_pick, ahead_start, behind_start, ahead_table, behind_table,
                ahead_source):
    smem = pl.BlockSpec(memory_space=pltpu.SMEM)
    vmem = pl.BlockSpec(memory_space=pltpu.VMEM)
    return pl.pallas_call(
        functools.partial(paired_kernel, steps=ahead_source.shape[0]),
        out_shape=(
            jax.ShapeDtypeStruct(ahead_start.shape, jnp.float32),
            jax.ShapeDtypeStruct(behind_start.shape, jnp.float32),
        ),
        in_specs=[smem, smem, vmem, vmem, vmem, vmem, vmem],
        out_specs=(vmem, vmem),
    )(ahead_pick, behind_pick, ahead_start, behind_start, ahead_table, behind_table, ahead_source)


def per_band_products(lines, factors, weights):
    steps, rows, states = lines.shape
    bands = factors.shape[0]
    every = accurate_matmul_result(
        lines.reshape(steps * rows, states),
        jnp.transpose(factors, (1, 0, 2)).reshape(states, bands * states),
    ).reshape(steps, rows, bands, states)
    return jnp.sum(every * weights[:, None, :, None], axis=2)


def shards(
    observations,
    band_index,
    obs_mask,
    diffusivity,
    mode_correction_factors,
    mode_backward_factors,
    initial_mean,
):
    steps_dev = observations.shape[0]
    record_rows = observations.shape[1]
    states = initial_mean.shape[0]
    bands = diffusivity.shape[0]
    column_share = states // lax.axis_size("col")
    column_index = lax.axis_index("col")
    time_devices = lax.axis_size("tm")
    time_index = lax.axis_index("tm")
    dynamics = diffusion_matrices(diffusivity, GRID)
    gain = jnp.transpose(mode_correction_factors, (0, 2, 1))
    corrected = dynamics - jnp.einsum(
        "bij,bjk->bik", dynamics, gain, precision=lax.Precision.HIGHEST
    )
    forward_table = jnp.stack([dynamics, corrected], axis=1).reshape(2 * bands, states, states)
    forward_pick = 2 * band_index + obs_mask
    identity = jnp.eye(states, dtype=jnp.float32)
    own_identity = lax.dynamic_slice_in_dim(identity, column_index * column_share, column_share, 0)
    blank_columns = jnp.zeros((steps_dev, column_share, states), jnp.float32)
    band_weights = (band_index[:, None] == jnp.arange(bands)[None, :]).astype(jnp.float32)
    observed_weights = band_weights * obs_mask.astype(jnp.float32)[:, None]
    measured = per_band_products(observations, gain, observed_weights)

    blank_records = jnp.zeros((record_rows, states), jnp.float32)
    first_block = time_index == 0
    final_here = (time_index == time_devices - 1) & (jnp.arange(steps_dev) == steps_dev - 1)
    backward = jnp.transpose(mode_backward_factors, (0, 2, 1))
    backward_table = jnp.concatenate([backward, jnp.zeros_like(backward[:1])], axis=0)
    backward_pick = jnp.where(final_here, bands, band_index)
    forward_rows, backward_rows = paired_maps(
        forward_pick,
        backward_pick,
        jnp.concatenate([own_identity, blank_records], axis=0),
        own_identity,
        forward_table,
        backward_table,
        jnp.concatenate([blank_columns, measured], axis=1),
    )
    whole_matrix = gathered_rows(forward_rows[:column_share], "col")
    whole_back = gathered_rows(backward_rows, "col")
    block_records = forward_rows[column_share:]
    folded_records = jnp.where(
        first_block,
        accurate_matmul_result(initial_mean[None, :], whole_matrix) + block_records,
        block_records,
    )
    _, backward_maps, ending_records = doubling_maps(
        jnp.where(first_block, jnp.zeros_like(whole_matrix), whole_matrix),
        whole_back,
        folded_records,
        "tm",
        0,
    )
    start_rows = jnp.where(
        first_block,
        jnp.broadcast_to(initial_mean[None, :], (record_rows, states)),
        passed_along(ending_records, "tm", 1),
    )

    filtered, predicted = recurrence(
        forward_pick,
        start_rows,
        forward_table,
        measured,
        False,
        True,
        side=(band_index, dynamics),
    )
    following = passed_along(predicted[0], "tm", -1)
    next_predicted = jnp.concatenate([predicted[1:], following[None]], axis=0)

    live_weights = band_weights * (1.0 - final_here.astype(jnp.float32))[:, None]
    shift = filtered - per_band_products(next_predicted, backward, live_weights)

    back_records = recurrence(backward_pick, blank_records, backward_table, shift, True, False)
    opening_records = doubling_records(backward_maps, back_records, "tm", True, 1)
    after_records = passed_along(opening_records, "tm", -1)

    smoothed = recurrence(backward_pick, after_records, backward_table, shift, True, True)
    return (filtered, smoothed)


def solution(mesh):
    return jax.shard_map(
        shards,
        mesh=mesh,
        in_specs=(P("tm", "col", None), P("tm"), P("tm"), P(), P(), P(), P()),
        out_specs=(P("tm", "col", None), P("tm", "col", None)),
        check_vma=False,
    )
```

```python
import functools

import jax
import jax.numpy as jnp
from jax import lax
from jax.experimental import pallas as pl
from jax.experimental.pallas import tpu as pltpu
from jax.sharding import PartitionSpec as P

GRID = 16
UNROLL = 4


def passed_along(block, axis, distance):
    devices = range(lax.axis_size(axis))
    route = [(i - distance, i) for i in devices if i - distance in devices]
    return lax.ppermute(block, axis, route)


def gathered_rows(part, axis):
    peers, index = (lax.axis_size(axis), lax.axis_index(axis))
    rows = part.shape[0]
    whole = jnp.zeros((peers * rows,) + part.shape[1:], part.dtype)
    for shift in range(peers):
        if shift == 0:
            got = part
        else:
            got = lax.ppermute(part, axis, [(i, (i + shift) % peers) for i in range(peers)])
        owner = lax.rem(index - shift + peers, peers)
        whole = lax.dynamic_update_slice_in_dim(whole, got, owner * rows, 0)
    return whole


def accurate_matmul_result(first_factor, second_factor):
    return jnp.dot(first_factor, second_factor, precision=lax.Precision.HIGHEST)


def greet_partners(index, peers, other, rounds, columns=1):
    barrier = pltpu.get_barrier_semaphore()
    partners = 0
    for r in range(rounds):
        distance = 1 << r
        for partner, exists in ((index + distance, index + distance < peers),
                                (index - distance, index - distance >= 0)):
            @pl.when(exists)
            def _():
                pl.semaphore_signal(barrier, inc=1, device_id=(partner, other),
                                    device_id_type=pl.DeviceIdType.MESH)

            partners = partners + jnp.where(exists, 1, 0)
    for shift in range(1, columns):
        pl.semaphore_signal(barrier, inc=1, device_id=(index, lax.rem(other + shift, columns)),
                            device_id_type=pl.DeviceIdType.MESH)
        partners = partners + 1
    pl.semaphore_wait(barrier, partners)


def exact_dot(first, second):
    return jnp.dot(first, second, precision=lax.Precision.HIGHEST,
                   preferred_element_type=jnp.float32)


def share_rows(full, slot, mine, index, other, columns, sems):
    copies = []
    for shift in range(1, columns):
        copy = pltpu.make_async_remote_copy(
            src_ref=full.at[slot, mine], dst_ref=full.at[slot, mine],
            send_sem=sems.at[0, shift - 1], recv_sem=sems.at[1, shift - 1],
            device_id=(index, lax.rem(other + shift, columns)),
            device_id_type=pl.DeviceIdType.MESH)
        copy.start()
        copies.append(copy)
    for copy in copies:
        copy.wait_recv()
    for copy in copies:
        copy.wait_send()


def maps_kernel(ahead_ref, behind_ref, records_ref, behind_out, records_out, fulls,
                ahead_in, behind_in, sums, sum_in, sems, sum_sems, col_sems, *, axis):
    peers, index = (lax.axis_size(axis), lax.axis_index(axis))
    other = lax.axis_index("col")
    columns = lax.axis_size("col")
    rounds = behind_out.shape[0]
    share = ahead_ref.shape[0] // columns
    mine = pl.ds(pl.multiple_of(other * share, share), share)
    greet_partners(index, peers, other, rounds, columns)
    fulls[0, 0] = ahead_ref[...]
    fulls[1, 0] = behind_ref[...]
    ahead_full = fulls.at[0]
    behind_full = fulls.at[1]
    for r in range(rounds):
        distance = 1 << r
        up, has_up = index + distance, index + distance < peers
        down, has_down = index - distance, index - distance >= 0
        own_ahead = ahead_full.at[r]
        own_sum = records_ref if r == 0 else sums.at[r]
        sum_copy = pltpu.make_async_remote_copy(
            src_ref=own_sum, dst_ref=sum_in.at[r], send_sem=sum_sems.at[0, r],
            recv_sem=sum_sems.at[1, r], device_id=(up, other),
            device_id_type=pl.DeviceIdType.MESH)

        @pl.when(has_up)
        def _():
            sum_copy.start()

        if r == rounds - 1:
            @pl.when(has_down)
            def _():
                sum_copy.wait_recv()
                sums[r + 1] = exact_dot(sum_in[r], own_ahead[...]) + own_sum[...]

            @pl.when(jnp.logical_not(has_down))
            def _():
                sums[r + 1] = own_sum[...]

            @pl.when(has_up)
            def _():
                sum_copy.wait_send()

            break
        own_behind = behind_full.at[r]
        ahead_copy = pltpu.make_async_remote_copy(
            src_ref=own_ahead.at[mine], dst_ref=ahead_in.at[r], send_sem=sems.at[0, 0, r],
            recv_sem=sems.at[0, 1, r], device_id=(up, other),
            device_id_type=pl.DeviceIdType.MESH)
        behind_copy = pltpu.make_async_remote_copy(
            src_ref=own_behind.at[mine], dst_ref=behind_in.at[r], send_sem=sems.at[1, 0, r],
            recv_sem=sems.at[1, 1, r], device_id=(down, other),
            device_id_type=pl.DeviceIdType.MESH)

        @pl.when(has_up)
        def _():
            ahead_copy.start()

        @pl.when(has_down)
        def _():
            behind_copy.start()

        @pl.when(has_down)
        def _():
            sum_copy.wait_recv()
            sums[r + 1] = exact_dot(sum_in[r], own_ahead[...]) + own_sum[...]

        @pl.when(jnp.logical_not(has_down))
        def _():
            sums[r + 1] = own_sum[...]

        @pl.when(has_down)
        def _():
            ahead_copy.wait_recv()
            ahead_full[r + 1, mine] = exact_dot(ahead_in[r], own_ahead[...])
            share_rows(ahead_full, r + 1, mine, index, other, columns, col_sems.at[0, r])

        @pl.when(jnp.logical_not(has_down))
        def _():
            ahead_full[r + 1] = own_ahead[...]

        @pl.when(has_up)
        def _():
            behind_copy.wait_recv()
            behind_full[r + 1, mine] = exact_dot(behind_in[r], own_behind[...])
            share_rows(behind_full, r + 1, mine, index, other, columns, col_sems.at[1, r])

        @pl.when(jnp.logical_not(has_up))
        def _():
            behind_full[r + 1] = own_behind[...]

        @pl.when(has_up)
        def _():
            ahead_copy.wait_send()
            sum_copy.wait_send()

        @pl.when(has_down)
        def _():
            behind_copy.wait_send()

    behind_out[...] = behind_full[...]
    records_out[...] = sums[rounds]


def doubling_maps(ahead, behind, records, axis, collective_id):
    peers = lax.axis_size(axis)
    columns = lax.axis_size("col")
    rounds = max(1, (peers - 1).bit_length())
    states = ahead.shape[0]
    vmem = pl.BlockSpec(memory_space=pltpu.VMEM)
    stack = jax.ShapeDtypeStruct((rounds, states, states), jnp.float32)
    return pl.pallas_call(
        functools.partial(maps_kernel, axis=axis),
        out_shape=(stack, jax.ShapeDtypeStruct(records.shape, jnp.float32)),
        in_specs=[vmem, vmem, vmem],
        out_specs=(vmem, vmem),
        scratch_shapes=[
            pltpu.VMEM((2, rounds, states, states), jnp.float32),
            pltpu.VMEM((max(1, rounds - 1), states // columns, states), jnp.float32),
            pltpu.VMEM((max(1, rounds - 1), states // columns, states), jnp.float32),
            pltpu.VMEM((rounds + 1,) + records.shape, jnp.float32),
            pltpu.VMEM((rounds,) + records.shape, jnp.float32),
            pltpu.SemaphoreType.DMA((2, 2, max(1, rounds - 1))),
            pltpu.SemaphoreType.DMA((2, rounds)),
            pltpu.SemaphoreType.DMA((2, max(1, rounds - 1), 2, max(1, columns - 1))),
        ],
        compiler_params=pltpu.CompilerParams(collective_id=collective_id, has_side_effects=True),
    )(ahead, behind, records)


def records_kernel(maps_ref, records_ref, out_ref, sums, sum_in, sems, *, axis, reverse):
    peers, index = (lax.axis_size(axis), lax.axis_index(axis))
    other = lax.axis_index("col")
    rounds = maps_ref.shape[0]
    greet_partners(index, peers, other, rounds)
    for r in range(rounds):
        distance = 1 << r
        if reverse:
            target, sends = index - distance, index - distance >= 0
            receives = index + distance < peers
        else:
            target, sends = index + distance, index + distance < peers
            receives = index - distance >= 0
        own_sum = records_ref if r == 0 else sums.at[r]
        sum_copy = pltpu.make_async_remote_copy(
            src_ref=own_sum, dst_ref=sum_in.at[r], send_sem=sems.at[0, r],
            recv_sem=sems.at[1, r], device_id=(target, other),
            device_id_type=pl.DeviceIdType.MESH)

        @pl.when(sends)
        def _():
            sum_copy.start()

        @pl.when(receives)
        def _():
            sum_copy.wait_recv()
            sums[r + 1] = exact_dot(sum_in[r], maps_ref[r]) + own_sum[...]

        @pl.when(jnp.logical_not(receives))
        def _():
            sums[r + 1] = own_sum[...]

        @pl.when(sends)
        def _():
            sum_copy.wait_send()

    out_ref[...] = sums[rounds]


def doubling_records(maps, records, axis, reverse, collective_id):
    rounds = maps.shape[0]
    vmem = pl.BlockSpec(memory_space=pltpu.VMEM)
    return pl.pallas_call(
        functools.partial(records_kernel, axis=axis, reverse=reverse),
        out_shape=jax.ShapeDtypeStruct(records.shape, jnp.float32),
        in_specs=[vmem, vmem],
        out_specs=vmem,
        scratch_shapes=[
            pltpu.VMEM((rounds + 1,) + records.shape, jnp.float32),
            pltpu.VMEM((rounds,) + records.shape, jnp.float32),
            pltpu.SemaphoreType.DMA((2, rounds)),
        ],
        compiler_params=pltpu.CompilerParams(collective_id=collective_id, has_side_effects=True),
    )(maps, records)


def diffusion_matrices(diffusivity, side_cells):
    cell_count = side_cells * side_cells
    cell_ids = jnp.arange(cell_count)
    cell_row = cell_ids // side_cells
    cell_col = cell_ids % side_cells
    adjacent = (
        jnp.abs(cell_row[:, None] - cell_row[None, :])
        + jnp.abs(cell_col[:, None] - cell_col[None, :])
        == 1
    )
    coupling = (
        0.5 * (diffusivity[:, :, None] + diffusivity[:, None, :]) * adjacent.astype(jnp.float32)
    )
    keeping = 1.0 - jnp.sum(coupling, axis=2)
    return coupling + keeping[:, :, None] * jnp.eye(cell_count, dtype=jnp.float32)


def recurrence_kernel(*refs, steps, reverse, store_all, side):
    if side:
        pick_ref, side_pick_ref, start_ref, table_ref, side_ref, source_ref, out_ref, side_out_ref = refs
    else:
        pick_ref, start_ref, table_ref, source_ref, out_ref = refs
    def advance(i, rows):
        t = steps - 1 - i if reverse else i
        if side:
            side_out_ref[t] = jnp.dot(
                rows,
                side_ref[side_pick_ref[t]],
                precision=lax.Precision.HIGHEST,
                preferred_element_type=jnp.float32,
            )
        rows = (
            jnp.dot(
                rows,
                table_ref[pick_ref[t]],
                precision=lax.Precision.HIGHEST,
                preferred_element_type=jnp.float32,
            )
            + source_ref[t]
        )
        if store_all:
            out_ref[t] = rows
        return rows

    rows = lax.fori_loop(0, steps, advance, start_ref[...], unroll=UNROLL)
    if not store_all:
        out_ref[...] = rows


def recurrence(pick, start, table, source, reverse, store_all, side=None):
    steps = source.shape[0]
    smem = pl.BlockSpec(memory_space=pltpu.SMEM)
    vmem = pl.BlockSpec(memory_space=pltpu.VMEM)
    out_shape = jax.ShapeDtypeStruct(source.shape if store_all else start.shape, jnp.float32)
    if side is None:
        operands = (pick, start, table, source)
        in_specs = [smem, vmem, vmem, vmem]
        out_specs = vmem
    else:
        side_pick, side_table = side
        operands = (pick, side_pick, start, table, side_table, source)
        in_specs = [smem, smem, vmem, vmem, vmem, vmem]
        out_shape = (out_shape, jax.ShapeDtypeStruct(source.shape, jnp.float32))
        out_specs = (vmem, vmem)
    return pl.pallas_call(
        functools.partial(
            recurrence_kernel,
            steps=steps,
            reverse=reverse,
            store_all=store_all,
            side=side is not None,
        ),
        out_shape=out_shape,
        in_specs=in_specs,
        out_specs=out_specs,
    )(*operands)


def paired_kernel(ahead_pick_ref, behind_pick_ref, ahead_start_ref, behind_start_ref,
                  ahead_table_ref, behind_table_ref, ahead_source_ref, ahead_out, behind_out,
                  *, steps):
    def advance(i, carry):
        ahead, behind = carry
        back = steps - 1 - i
        ahead = exact_dot(ahead, ahead_table_ref[ahead_pick_ref[i]]) + ahead_source_ref[i]
        behind = exact_dot(behind, behind_table_ref[behind_pick_ref[back]])
        return ahead, behind

    ahead, behind = lax.fori_loop(
        0, steps, advance, (ahead_start_ref[...], behind_start_ref[...]), unroll=UNROLL
    )
    ahead_out[...] = ahead
    behind_out[...] = behind


def paired_maps(ahead_pick, behind_pick, ahead_start, behind_start, ahead_table, behind_table,
                ahead_source):
    smem = pl.BlockSpec(memory_space=pltpu.SMEM)
    vmem = pl.BlockSpec(memory_space=pltpu.VMEM)
    return pl.pallas_call(
        functools.partial(paired_kernel, steps=ahead_source.shape[0]),
        out_shape=(
            jax.ShapeDtypeStruct(ahead_start.shape, jnp.float32),
            jax.ShapeDtypeStruct(behind_start.shape, jnp.float32),
        ),
        in_specs=[smem, smem, vmem, vmem, vmem, vmem, vmem],
        out_specs=(vmem, vmem),
    )(ahead_pick, behind_pick, ahead_start, behind_start, ahead_table, behind_table, ahead_source)


def per_band_products(lines, factors, weights):
    steps, rows, states = lines.shape
    bands = factors.shape[0]
    every = accurate_matmul_result(
        lines.reshape(steps * rows, states),
        jnp.transpose(factors, (1, 0, 2)).reshape(states, bands * states),
    ).reshape(steps, rows, bands, states)
    return jnp.sum(every * weights[:, None, :, None], axis=2)


def shards(
    observations,
    band_index,
    obs_mask,
    diffusivity,
    mode_correction_factors,
    mode_backward_factors,
    initial_mean,
):
    steps_dev = observations.shape[0]
    record_rows = observations.shape[1]
    states = initial_mean.shape[0]
    bands = diffusivity.shape[0]
    column_share = states // lax.axis_size("col")
    column_index = lax.axis_index("col")
    time_devices = lax.axis_size("tm")
    time_index = lax.axis_index("tm")
    dynamics = diffusion_matrices(diffusivity, GRID)
    gain = jnp.transpose(mode_correction_factors, (0, 2, 1))
    corrected = dynamics - jnp.einsum(
        "bij,bjk->bik", dynamics, gain, precision=lax.Precision.HIGHEST
    )
    forward_table = jnp.stack([dynamics, corrected], axis=1).reshape(2 * bands, states, states)
    forward_pick = 2 * band_index + obs_mask
    identity = jnp.eye(states, dtype=jnp.float32)
    own_identity = lax.dynamic_slice_in_dim(identity, column_index * column_share, column_share, 0)
    blank_columns = jnp.zeros((steps_dev, column_share, states), jnp.float32)
    band_weights = (band_index[:, None] == jnp.arange(bands)[None, :]).astype(jnp.float32)
    observed_weights = band_weights * obs_mask.astype(jnp.float32)[:, None]
    measured = per_band_products(observations, gain, observed_weights)

    blank_records = jnp.zeros((record_rows, states), jnp.float32)
    first_block = time_index == 0
    final_here = (time_index == time_devices - 1) & (jnp.arange(steps_dev) == steps_dev - 1)
    backward = jnp.transpose(mode_backward_factors, (0, 2, 1))
    backward_table = jnp.concatenate([backward, jnp.zeros_like(backward[:1])], axis=0)
    backward_pick = jnp.where(final_here, bands, band_index)
    forward_rows, backward_rows = paired_maps(
        forward_pick,
        backward_pick,
        jnp.concatenate([own_identity, blank_records], axis=0),
        own_identity,
        forward_table,
        backward_table,
        jnp.concatenate([blank_columns, measured], axis=1),
    )
    whole_matrix = gathered_rows(forward_rows[:column_share], "col")
    whole_back = gathered_rows(backward_rows, "col")
    block_records = forward_rows[column_share:]
    folded_records = jnp.where(
        first_block,
        accurate_matmul_result(initial_mean[None, :], whole_matrix) + block_records,
        block_records,
    )
    backward_maps, ending_records = doubling_maps(
        jnp.where(first_block, jnp.zeros_like(whole_matrix), whole_matrix),
        whole_back,
        folded_records,
        "tm",
        0,
    )
    start_rows = jnp.where(
        first_block,
        jnp.broadcast_to(initial_mean[None, :], (record_rows, states)),
        passed_along(ending_records, "tm", 1),
    )

    filtered, predicted = recurrence(
        forward_pick,
        start_rows,
        forward_table,
        measured,
        False,
        True,
        side=(band_index, dynamics),
    )
    following = passed_along(predicted[0], "tm", -1)
    next_predicted = jnp.concatenate([predicted[1:], following[None]], axis=0)

    live_weights = band_weights * (1.0 - final_here.astype(jnp.float32))[:, None]
    shift = filtered - per_band_products(next_predicted, backward, live_weights)

    back_records = recurrence(backward_pick, blank_records, backward_table, shift, True, False)
    opening_records = doubling_records(backward_maps, back_records, "tm", True, 1)
    after_records = passed_along(opening_records, "tm", -1)

    smoothed = recurrence(backward_pick, after_records, backward_table, shift, True, True)
    return (filtered, smoothed)


def solution(mesh):
    return jax.shard_map(
        shards,
        mesh=mesh,
        in_specs=(P("tm", "col", None), P("tm"), P("tm"), P(), P(), P(), P()),
        out_specs=(P("tm", "col", None), P("tm", "col", None)),
        check_vma=False,
    )
```

```python
import functools

import jax
import jax.numpy as jnp
from jax import lax
from jax.experimental import pallas as pl
from jax.experimental.pallas import tpu as pltpu
from jax.sharding import PartitionSpec as P

GRID = 16
UNROLL = 4


def passed_along(block, axis, distance):
    devices = range(lax.axis_size(axis))
    route = [(i - distance, i) for i in devices if i - distance in devices]
    return lax.ppermute(block, axis, route)


def gathered_rows(part, axis):
    peers, index = (lax.axis_size(axis), lax.axis_index(axis))
    rows = part.shape[0]
    whole = jnp.zeros((peers * rows,) + part.shape[1:], part.dtype)
    for shift in range(peers):
        if shift == 0:
            got = part
        else:
            got = lax.ppermute(part, axis, [(i, (i + shift) % peers) for i in range(peers)])
        owner = lax.rem(index - shift + peers, peers)
        whole = lax.dynamic_update_slice_in_dim(whole, got, owner * rows, 0)
    return whole


def accurate_matmul_result(first_factor, second_factor):
    return jnp.dot(first_factor, second_factor, precision=lax.Precision.HIGHEST)


def greet_partners(index, peers, other, rounds):
    barrier = pltpu.get_barrier_semaphore()
    partners = 0
    for r in range(rounds):
        distance = 1 << r
        for partner, exists in ((index + distance, index + distance < peers),
                                (index - distance, index - distance >= 0)):
            @pl.when(exists)
            def _():
                pl.semaphore_signal(barrier, inc=1, device_id=(partner, other),
                                    device_id_type=pl.DeviceIdType.MESH)

            partners = partners + jnp.where(exists, 1, 0)
    pl.semaphore_wait(barrier, partners)


def exact_dot(first, second):
    return jnp.dot(first, second, precision=lax.Precision.HIGHEST,
                   preferred_element_type=jnp.float32)


def maps_kernel(ahead_ref, behind_ref, records_ref, ahead_out, behind_out, records_out,
                ahead_in, behind_in, sums, sum_in, sems, sum_sems, *, axis):
    peers, index = (lax.axis_size(axis), lax.axis_index(axis))
    other = lax.axis_index("col")
    rounds = ahead_out.shape[0]
    greet_partners(index, peers, other, rounds)
    ahead_out[0] = ahead_ref[...]
    behind_out[0] = behind_ref[...]
    pending = []
    for r in range(rounds):
        distance = 1 << r
        up, has_up = index + distance, index + distance < peers
        down, has_down = index - distance, index - distance >= 0
        own_ahead = ahead_ref if r == 0 else ahead_out.at[r]
        own_sum = records_ref if r == 0 else sums.at[r]
        sum_copy = pltpu.make_async_remote_copy(
            src_ref=own_sum, dst_ref=sum_in.at[r], send_sem=sum_sems.at[0, r],
            recv_sem=sum_sems.at[1, r], device_id=(up, other),
            device_id_type=pl.DeviceIdType.MESH)

        @pl.when(has_up)
        def _():
            sum_copy.start()

        if r == rounds - 1:
            @pl.when(has_down)
            def _():
                sum_copy.wait_recv()
                sums[r + 1] = exact_dot(sum_in[r], own_ahead[...]) + own_sum[...]

            @pl.when(jnp.logical_not(has_down))
            def _():
                sums[r + 1] = own_sum[...]

            pending.append((has_up, sum_copy))
            break
        own_behind = behind_ref if r == 0 else behind_out.at[r]
        ahead_copy = pltpu.make_async_remote_copy(
            src_ref=own_ahead, dst_ref=ahead_in.at[r], send_sem=sems.at[0, 0, r],
            recv_sem=sems.at[0, 1, r], device_id=(up, other),
            device_id_type=pl.DeviceIdType.MESH)
        behind_copy = pltpu.make_async_remote_copy(
            src_ref=own_behind, dst_ref=behind_in.at[r], send_sem=sems.at[1, 0, r],
            recv_sem=sems.at[1, 1, r], device_id=(down, other),
            device_id_type=pl.DeviceIdType.MESH)

        @pl.when(has_up)
        def _():
            ahead_copy.start()

        @pl.when(has_down)
        def _():
            behind_copy.start()

        @pl.when(has_down)
        def _():
            sum_copy.wait_recv()
            sums[r + 1] = exact_dot(sum_in[r], own_ahead[...]) + own_sum[...]

        @pl.when(jnp.logical_not(has_down))
        def _():
            sums[r + 1] = own_sum[...]

        @pl.when(has_down)
        def _():
            ahead_copy.wait_recv()
            ahead_out[r + 1] = exact_dot(ahead_in[r], own_ahead[...])

        @pl.when(jnp.logical_not(has_down))
        def _():
            ahead_out[r + 1] = own_ahead[...]

        @pl.when(has_up)
        def _():
            behind_copy.wait_recv()
            behind_out[r + 1] = exact_dot(behind_in[r], own_behind[...])

        @pl.when(jnp.logical_not(has_up))
        def _():
            behind_out[r + 1] = own_behind[...]

        pending += [(has_up, ahead_copy), (has_up, sum_copy), (has_down, behind_copy)]

    for sent, copy in pending:
        @pl.when(sent)
        def _():
            copy.wait_send()

    records_out[...] = sums[rounds]


def doubling_maps(ahead, behind, records, axis, collective_id):
    peers = lax.axis_size(axis)
    rounds = max(1, (peers - 1).bit_length())
    states = ahead.shape[0]
    vmem = pl.BlockSpec(memory_space=pltpu.VMEM)
    stack = jax.ShapeDtypeStruct((rounds, states, states), jnp.float32)
    return pl.pallas_call(
        functools.partial(maps_kernel, axis=axis),
        out_shape=(stack, stack, jax.ShapeDtypeStruct(records.shape, jnp.float32)),
        in_specs=[vmem, vmem, vmem],
        out_specs=(vmem, vmem, vmem),
        scratch_shapes=[
            pltpu.VMEM((max(1, rounds - 1), states, states), jnp.float32),
            pltpu.VMEM((max(1, rounds - 1), states, states), jnp.float32),
            pltpu.VMEM((rounds + 1,) + records.shape, jnp.float32),
            pltpu.VMEM((rounds,) + records.shape, jnp.float32),
            pltpu.SemaphoreType.DMA((2, 2, max(1, rounds - 1))),
            pltpu.SemaphoreType.DMA((2, rounds)),
        ],
        compiler_params=pltpu.CompilerParams(collective_id=collective_id, has_side_effects=True),
    )(ahead, behind, records)


def records_kernel(maps_ref, records_ref, out_ref, sums, sum_in, sems, *, axis, reverse):
    peers, index = (lax.axis_size(axis), lax.axis_index(axis))
    other = lax.axis_index("col")
    rounds = maps_ref.shape[0]
    greet_partners(index, peers, other, rounds)
    pending = []
    for r in range(rounds):
        distance = 1 << r
        if reverse:
            target, sends = index - distance, index - distance >= 0
            receives = index + distance < peers
        else:
            target, sends = index + distance, index + distance < peers
            receives = index - distance >= 0
        own_sum = records_ref if r == 0 else sums.at[r]
        sum_copy = pltpu.make_async_remote_copy(
            src_ref=own_sum, dst_ref=sum_in.at[r], send_sem=sems.at[0, r],
            recv_sem=sems.at[1, r], device_id=(target, other),
            device_id_type=pl.DeviceIdType.MESH)

        @pl.when(sends)
        def _():
            sum_copy.start()

        @pl.when(receives)
        def _():
            sum_copy.wait_recv()
            sums[r + 1] = exact_dot(sum_in[r], maps_ref[r]) + own_sum[...]

        @pl.when(jnp.logical_not(receives))
        def _():
            sums[r + 1] = own_sum[...]

        pending.append((sends, sum_copy))

    for sent, copy in pending:
        @pl.when(sent)
        def _():
            copy.wait_send()

    out_ref[...] = sums[rounds]


def doubling_records(maps, records, axis, reverse, collective_id):
    rounds = maps.shape[0]
    vmem = pl.BlockSpec(memory_space=pltpu.VMEM)
    return pl.pallas_call(
        functools.partial(records_kernel, axis=axis, reverse=reverse),
        out_shape=jax.ShapeDtypeStruct(records.shape, jnp.float32),
        in_specs=[vmem, vmem],
        out_specs=vmem,
        scratch_shapes=[
            pltpu.VMEM((rounds + 1,) + records.shape, jnp.float32),
            pltpu.VMEM((rounds,) + records.shape, jnp.float32),
            pltpu.SemaphoreType.DMA((2, rounds)),
        ],
        compiler_params=pltpu.CompilerParams(collective_id=collective_id, has_side_effects=True),
    )(maps, records)


def diffusion_matrices(diffusivity, side_cells):
    cell_count = side_cells * side_cells
    cell_ids = jnp.arange(cell_count)
    cell_row = cell_ids // side_cells
    cell_col = cell_ids % side_cells
    adjacent = (
        jnp.abs(cell_row[:, None] - cell_row[None, :])
        + jnp.abs(cell_col[:, None] - cell_col[None, :])
        == 1
    )
    coupling = (
        0.5 * (diffusivity[:, :, None] + diffusivity[:, None, :]) * adjacent.astype(jnp.float32)
    )
    keeping = 1.0 - jnp.sum(coupling, axis=2)
    return coupling + keeping[:, :, None] * jnp.eye(cell_count, dtype=jnp.float32)


def recurrence_kernel(*refs, steps, reverse, store_all, side):
    if side:
        pick_ref, side_pick_ref, start_ref, table_ref, side_ref, source_ref, out_ref, side_out_ref = refs
    else:
        pick_ref, start_ref, table_ref, source_ref, out_ref = refs
    def advance(i, rows):
        t = steps - 1 - i if reverse else i
        if side:
            side_out_ref[t] = jnp.dot(
                rows,
                side_ref[side_pick_ref[t]],
                precision=lax.Precision.HIGHEST,
                preferred_element_type=jnp.float32,
            )
        rows = (
            jnp.dot(
                rows,
                table_ref[pick_ref[t]],
                precision=lax.Precision.HIGHEST,
                preferred_element_type=jnp.float32,
            )
            + source_ref[t]
        )
        if store_all:
            out_ref[t] = rows
        return rows

    rows = lax.fori_loop(0, steps, advance, start_ref[...], unroll=UNROLL)
    if not store_all:
        out_ref[...] = rows


def recurrence(pick, start, table, source, reverse, store_all, side=None):
    steps = source.shape[0]
    smem = pl.BlockSpec(memory_space=pltpu.SMEM)
    vmem = pl.BlockSpec(memory_space=pltpu.VMEM)
    out_shape = jax.ShapeDtypeStruct(source.shape if store_all else start.shape, jnp.float32)
    if side is None:
        operands = (pick, start, table, source)
        in_specs = [smem, vmem, vmem, vmem]
        out_specs = vmem
    else:
        side_pick, side_table = side
        operands = (pick, side_pick, start, table, side_table, source)
        in_specs = [smem, smem, vmem, vmem, vmem, vmem]
        out_shape = (out_shape, jax.ShapeDtypeStruct(source.shape, jnp.float32))
        out_specs = (vmem, vmem)
    return pl.pallas_call(
        functools.partial(
            recurrence_kernel,
            steps=steps,
            reverse=reverse,
            store_all=store_all,
            side=side is not None,
        ),
        out_shape=out_shape,
        in_specs=in_specs,
        out_specs=out_specs,
    )(*operands)


def paired_kernel(ahead_pick_ref, behind_pick_ref, ahead_start_ref, behind_start_ref,
                  ahead_table_ref, behind_table_ref, ahead_source_ref, ahead_out, behind_out,
                  *, steps):
    def advance(i, carry):
        ahead, behind = carry
        back = steps - 1 - i
        ahead = exact_dot(ahead, ahead_table_ref[ahead_pick_ref[i]]) + ahead_source_ref[i]
        behind = exact_dot(behind, behind_table_ref[behind_pick_ref[back]])
        return ahead, behind

    ahead, behind = lax.fori_loop(
        0, steps, advance, (ahead_start_ref[...], behind_start_ref[...]), unroll=UNROLL
    )
    ahead_out[...] = ahead
    behind_out[...] = behind


def paired_maps(ahead_pick, behind_pick, ahead_start, behind_start, ahead_table, behind_table,
                ahead_source):
    smem = pl.BlockSpec(memory_space=pltpu.SMEM)
    vmem = pl.BlockSpec(memory_space=pltpu.VMEM)
    return pl.pallas_call(
        functools.partial(paired_kernel, steps=ahead_source.shape[0]),
        out_shape=(
            jax.ShapeDtypeStruct(ahead_start.shape, jnp.float32),
            jax.ShapeDtypeStruct(behind_start.shape, jnp.float32),
        ),
        in_specs=[smem, smem, vmem, vmem, vmem, vmem, vmem],
        out_specs=(vmem, vmem),
    )(ahead_pick, behind_pick, ahead_start, behind_start, ahead_table, behind_table, ahead_source)


def per_band_products(lines, factors, weights):
    steps, rows, states = lines.shape
    bands = factors.shape[0]
    every = accurate_matmul_result(
        lines.reshape(steps * rows, states),
        jnp.transpose(factors, (1, 0, 2)).reshape(states, bands * states),
    ).reshape(steps, rows, bands, states)
    return jnp.sum(every * weights[:, None, :, None], axis=2)


def shards(
    observations,
    band_index,
    obs_mask,
    diffusivity,
    mode_correction_factors,
    mode_backward_factors,
    initial_mean,
):
    steps_dev = observations.shape[0]
    record_rows = observations.shape[1]
    states = initial_mean.shape[0]
    bands = diffusivity.shape[0]
    column_share = states // lax.axis_size("col")
    column_index = lax.axis_index("col")
    time_devices = lax.axis_size("tm")
    time_index = lax.axis_index("tm")
    dynamics = diffusion_matrices(diffusivity, GRID)
    gain = jnp.transpose(mode_correction_factors, (0, 2, 1))
    corrected = dynamics - jnp.einsum(
        "bij,bjk->bik", dynamics, gain, precision=lax.Precision.HIGHEST
    )
    forward_table = jnp.stack([dynamics, corrected], axis=1).reshape(2 * bands, states, states)
    forward_pick = 2 * band_index + obs_mask
    identity = jnp.eye(states, dtype=jnp.float32)
    own_identity = lax.dynamic_slice_in_dim(identity, column_index * column_share, column_share, 0)
    blank_columns = jnp.zeros((steps_dev, column_share, states), jnp.float32)
    band_weights = (band_index[:, None] == jnp.arange(bands)[None, :]).astype(jnp.float32)
    observed_weights = band_weights * obs_mask.astype(jnp.float32)[:, None]
    measured = per_band_products(observations, gain, observed_weights)

    blank_records = jnp.zeros((record_rows, states), jnp.float32)
    first_block = time_index == 0
    final_here = (time_index == time_devices - 1) & (jnp.arange(steps_dev) == steps_dev - 1)
    backward = jnp.transpose(mode_backward_factors, (0, 2, 1))
    backward_table = jnp.concatenate([backward, jnp.zeros_like(backward[:1])], axis=0)
    backward_pick = jnp.where(final_here, bands, band_index)
    forward_rows, backward_rows = paired_maps(
        forward_pick,
        backward_pick,
        jnp.concatenate([own_identity, blank_records], axis=0),
        own_identity,
        forward_table,
        backward_table,
        jnp.concatenate([blank_columns, measured], axis=1),
    )
    whole_matrix = gathered_rows(forward_rows[:column_share], "col")
    whole_back = gathered_rows(backward_rows, "col")
    block_records = forward_rows[column_share:]
    folded_records = jnp.where(
        first_block,
        accurate_matmul_result(initial_mean[None, :], whole_matrix) + block_records,
        block_records,
    )
    _, backward_maps, ending_records = doubling_maps(
        jnp.where(first_block, jnp.zeros_like(whole_matrix), whole_matrix),
        whole_back,
        folded_records,
        "tm",
        0,
    )
    start_rows = jnp.where(
        first_block,
        jnp.broadcast_to(initial_mean[None, :], (record_rows, states)),
        passed_along(ending_records, "tm", 1),
    )

    filtered, predicted = recurrence(
        forward_pick,
        start_rows,
        forward_table,
        measured,
        False,
        True,
        side=(band_index, dynamics),
    )
    following = passed_along(predicted[0], "tm", -1)
    next_predicted = jnp.concatenate([predicted[1:], following[None]], axis=0)

    live_weights = band_weights * (1.0 - final_here.astype(jnp.float32))[:, None]
    shift = filtered - per_band_products(next_predicted, backward, live_weights)

    back_records = recurrence(backward_pick, blank_records, backward_table, shift, True, False)
    opening_records = doubling_records(backward_maps, back_records, "tm", True, 1)
    after_records = passed_along(opening_records, "tm", -1)

    smoothed = recurrence(backward_pick, after_records, backward_table, shift, True, True)
    return (filtered, smoothed)


def solution(mesh):
    return jax.shard_map(
        shards,
        mesh=mesh,
        in_specs=(P("tm", "col", None), P("tm"), P("tm"), P(), P(), P(), P()),
        out_specs=(P("tm", "col", None), P("tm", "col", None)),
        check_vma=False,
    )
```

```python
import functools

import jax
import jax.numpy as jnp
from jax import lax
from jax.experimental import pallas as pl
from jax.experimental.pallas import tpu as pltpu
from jax.sharding import PartitionSpec as P

GRID = 16
UNROLL = 4


def passed_along(block, axis, distance):
    devices = range(lax.axis_size(axis))
    route = [(i - distance, i) for i in devices if i - distance in devices]
    return lax.ppermute(block, axis, route)


def gathered_rows(part, axis):
    peers, index = (lax.axis_size(axis), lax.axis_index(axis))
    rows = part.shape[0]
    whole = jnp.zeros((peers * rows,) + part.shape[1:], part.dtype)
    for shift in range(peers):
        if shift == 0:
            got = part
        else:
            got = lax.ppermute(part, axis, [(i, (i + shift) % peers) for i in range(peers)])
        owner = lax.rem(index - shift + peers, peers)
        whole = lax.dynamic_update_slice_in_dim(whole, got, owner * rows, 0)
    return whole


def accurate_matmul_result(first_factor, second_factor):
    return jnp.dot(first_factor, second_factor, precision=lax.Precision.HIGHEST)


def greet_partners(index, peers, other, rounds):
    barrier = pltpu.get_barrier_semaphore()
    partners = 0
    for r in range(rounds):
        distance = 1 << r
        for partner, exists in ((index + distance, index + distance < peers),
                                (index - distance, index - distance >= 0)):
            @pl.when(exists)
            def _():
                pl.semaphore_signal(barrier, inc=1, device_id=(partner, other),
                                    device_id_type=pl.DeviceIdType.MESH)

            partners = partners + jnp.where(exists, 1, 0)
    pl.semaphore_wait(barrier, partners)


def exact_dot(first, second):
    return jnp.dot(first, second, precision=lax.Precision.HIGHEST,
                   preferred_element_type=jnp.float32)


def maps_kernel(ahead_ref, behind_ref, records_ref, ahead_out, behind_out, records_out,
                ahead_in, behind_in, sums, sum_in, sems, sum_sems, *, axis):
    peers, index = (lax.axis_size(axis), lax.axis_index(axis))
    other = lax.axis_index("col")
    rounds = ahead_out.shape[0]
    greet_partners(index, peers, other, rounds)
    ahead_out[0] = ahead_ref[...]
    behind_out[0] = behind_ref[...]
    pending = []
    for r in range(rounds):
        distance = 1 << r
        up, has_up = index + distance, index + distance < peers
        down, has_down = index - distance, index - distance >= 0
        own_ahead = ahead_ref if r == 0 else ahead_out.at[r]
        own_sum = records_ref if r == 0 else sums.at[r]
        sum_copy = pltpu.make_async_remote_copy(
            src_ref=own_sum, dst_ref=sum_in.at[r], send_sem=sum_sems.at[0, r],
            recv_sem=sum_sems.at[1, r], device_id=(up, other),
            device_id_type=pl.DeviceIdType.MESH)

        @pl.when(has_up)
        def _():
            sum_copy.start()

        if r == rounds - 1:
            @pl.when(has_down)
            def _():
                sum_copy.wait_recv()
                sums[r + 1] = exact_dot(sum_in[r], own_ahead[...]) + own_sum[...]

            @pl.when(jnp.logical_not(has_down))
            def _():
                sums[r + 1] = own_sum[...]

            pending.append((has_up, sum_copy))
            break
        own_behind = behind_ref if r == 0 else behind_out.at[r]
        ahead_copy = pltpu.make_async_remote_copy(
            src_ref=own_ahead, dst_ref=ahead_in.at[r], send_sem=sems.at[0, 0, r],
            recv_sem=sems.at[0, 1, r], device_id=(up, other),
            device_id_type=pl.DeviceIdType.MESH)
        behind_copy = pltpu.make_async_remote_copy(
            src_ref=own_behind, dst_ref=behind_in.at[r], send_sem=sems.at[1, 0, r],
            recv_sem=sems.at[1, 1, r], device_id=(down, other),
            device_id_type=pl.DeviceIdType.MESH)

        @pl.when(has_up)
        def _():
            ahead_copy.start()

        @pl.when(has_down)
        def _():
            behind_copy.start()

        @pl.when(has_down)
        def _():
            sum_copy.wait_recv()
            sums[r + 1] = exact_dot(sum_in[r], own_ahead[...]) + own_sum[...]

        @pl.when(jnp.logical_not(has_down))
        def _():
            sums[r + 1] = own_sum[...]

        @pl.when(has_down)
        def _():
            ahead_copy.wait_recv()
            ahead_out[r + 1] = exact_dot(ahead_in[r], own_ahead[...])

        @pl.when(jnp.logical_not(has_down))
        def _():
            ahead_out[r + 1] = own_ahead[...]

        @pl.when(has_up)
        def _():
            behind_copy.wait_recv()
            behind_out[r + 1] = exact_dot(behind_in[r], own_behind[...])

        @pl.when(jnp.logical_not(has_up))
        def _():
            behind_out[r + 1] = own_behind[...]

        pending += [(has_up, ahead_copy), (has_up, sum_copy), (has_down, behind_copy)]

    for sent, copy in pending:
        @pl.when(sent)
        def _():
            copy.wait_send()

    records_out[...] = sums[rounds]


def doubling_maps(ahead, behind, records, axis, collective_id):
    peers = lax.axis_size(axis)
    rounds = max(1, (peers - 1).bit_length())
    states = ahead.shape[0]
    vmem = pl.BlockSpec(memory_space=pltpu.VMEM)
    stack = jax.ShapeDtypeStruct((rounds, states, states), jnp.float32)
    return pl.pallas_call(
        functools.partial(maps_kernel, axis=axis),
        out_shape=(stack, stack, jax.ShapeDtypeStruct(records.shape, jnp.float32)),
        in_specs=[vmem, vmem, vmem],
        out_specs=(vmem, vmem, vmem),
        scratch_shapes=[
            pltpu.VMEM((max(1, rounds - 1), states, states), jnp.float32),
            pltpu.VMEM((max(1, rounds - 1), states, states), jnp.float32),
            pltpu.VMEM((rounds + 1,) + records.shape, jnp.float32),
            pltpu.VMEM((rounds,) + records.shape, jnp.float32),
            pltpu.SemaphoreType.DMA((2, 2, max(1, rounds - 1))),
            pltpu.SemaphoreType.DMA((2, rounds)),
        ],
        compiler_params=pltpu.CompilerParams(collective_id=collective_id, has_side_effects=True),
    )(ahead, behind, records)


def records_kernel(maps_ref, records_ref, out_ref, sums, sum_in, sems, *, axis, reverse):
    peers, index = (lax.axis_size(axis), lax.axis_index(axis))
    other = lax.axis_index("col")
    rounds = maps_ref.shape[0]
    greet_partners(index, peers, other, rounds)
    pending = []
    for r in range(rounds):
        distance = 1 << r
        if reverse:
            target, sends = index - distance, index - distance >= 0
            receives = index + distance < peers
        else:
            target, sends = index + distance, index + distance < peers
            receives = index - distance >= 0
        own_sum = records_ref if r == 0 else sums.at[r]
        sum_copy = pltpu.make_async_remote_copy(
            src_ref=own_sum, dst_ref=sum_in.at[r], send_sem=sems.at[0, r],
            recv_sem=sems.at[1, r], device_id=(target, other),
            device_id_type=pl.DeviceIdType.MESH)

        @pl.when(sends)
        def _():
            sum_copy.start()

        @pl.when(receives)
        def _():
            sum_copy.wait_recv()
            sums[r + 1] = exact_dot(sum_in[r], maps_ref[r]) + own_sum[...]

        @pl.when(jnp.logical_not(receives))
        def _():
            sums[r + 1] = own_sum[...]

        pending.append((sends, sum_copy))

    for sent, copy in pending:
        @pl.when(sent)
        def _():
            copy.wait_send()

    out_ref[...] = sums[rounds]


def doubling_records(maps, records, axis, reverse, collective_id):
    rounds = maps.shape[0]
    vmem = pl.BlockSpec(memory_space=pltpu.VMEM)
    return pl.pallas_call(
        functools.partial(records_kernel, axis=axis, reverse=reverse),
        out_shape=jax.ShapeDtypeStruct(records.shape, jnp.float32),
        in_specs=[vmem, vmem],
        out_specs=vmem,
        scratch_shapes=[
            pltpu.VMEM((rounds + 1,) + records.shape, jnp.float32),
            pltpu.VMEM((rounds,) + records.shape, jnp.float32),
            pltpu.SemaphoreType.DMA((2, rounds)),
        ],
        compiler_params=pltpu.CompilerParams(collective_id=collective_id, has_side_effects=True),
    )(maps, records)


def diffusion_matrices(diffusivity, side_cells):
    cell_count = side_cells * side_cells
    cell_ids = jnp.arange(cell_count)
    cell_row = cell_ids // side_cells
    cell_col = cell_ids % side_cells
    adjacent = (
        jnp.abs(cell_row[:, None] - cell_row[None, :])
        + jnp.abs(cell_col[:, None] - cell_col[None, :])
        == 1
    )
    coupling = (
        0.5 * (diffusivity[:, :, None] + diffusivity[:, None, :]) * adjacent.astype(jnp.float32)
    )
    keeping = 1.0 - jnp.sum(coupling, axis=2)
    return coupling + keeping[:, :, None] * jnp.eye(cell_count, dtype=jnp.float32)


def recurrence_kernel(*refs, steps, reverse, store_all, side):
    if side:
        pick_ref, side_pick_ref, start_ref, table_ref, side_ref, source_ref, out_ref, side_out_ref = refs
    else:
        pick_ref, start_ref, table_ref, source_ref, out_ref = refs
    def advance(i, rows):
        t = steps - 1 - i if reverse else i
        if side:
            side_out_ref[t] = jnp.dot(
                rows,
                side_ref[side_pick_ref[t]],
                precision=lax.Precision.HIGHEST,
                preferred_element_type=jnp.float32,
            )
        rows = (
            jnp.dot(
                rows,
                table_ref[pick_ref[t]],
                precision=lax.Precision.HIGHEST,
                preferred_element_type=jnp.float32,
            )
            + source_ref[t]
        )
        if store_all:
            out_ref[t] = rows
        return rows

    rows = lax.fori_loop(0, steps, advance, start_ref[...], unroll=UNROLL)
    if not store_all:
        out_ref[...] = rows


def recurrence(pick, start, table, source, reverse, store_all, side=None):
    steps = source.shape[0]
    smem = pl.BlockSpec(memory_space=pltpu.SMEM)
    vmem = pl.BlockSpec(memory_space=pltpu.VMEM)
    out_shape = jax.ShapeDtypeStruct(source.shape if store_all else start.shape, jnp.float32)
    if side is None:
        operands = (pick, start, table, source)
        in_specs = [smem, vmem, vmem, vmem]
        out_specs = vmem
    else:
        side_pick, side_table = side
        operands = (pick, side_pick, start, table, side_table, source)
        in_specs = [smem, smem, vmem, vmem, vmem, vmem]
        out_shape = (out_shape, jax.ShapeDtypeStruct(source.shape, jnp.float32))
        out_specs = (vmem, vmem)
    return pl.pallas_call(
        functools.partial(
            recurrence_kernel,
            steps=steps,
            reverse=reverse,
            store_all=store_all,
            side=side is not None,
        ),
        out_shape=out_shape,
        in_specs=in_specs,
        out_specs=out_specs,
        cost_estimate=pl.CostEstimate(
            flops=2 * steps * start.shape[0] * table.shape[1] * table.shape[2] * (2 if side else 1),
            bytes_accessed=4 * (table.size + 3 * source.size),
            transcendentals=0,
        ),
    )(*operands)


def paired_kernel(ahead_pick_ref, behind_pick_ref, ahead_start_ref, behind_start_ref,
                  ahead_table_ref, behind_table_ref, ahead_source_ref, ahead_out, behind_out,
                  *, steps):
    def advance(i, carry):
        ahead, behind = carry
        back = steps - 1 - i
        ahead = exact_dot(ahead, ahead_table_ref[ahead_pick_ref[i]]) + ahead_source_ref[i]
        behind = exact_dot(behind, behind_table_ref[behind_pick_ref[back]])
        return ahead, behind

    ahead, behind = lax.fori_loop(
        0, steps, advance, (ahead_start_ref[...], behind_start_ref[...]), unroll=UNROLL
    )
    ahead_out[...] = ahead
    behind_out[...] = behind


def paired_maps(ahead_pick, behind_pick, ahead_start, behind_start, ahead_table, behind_table,
                ahead_source):
    smem = pl.BlockSpec(memory_space=pltpu.SMEM)
    vmem = pl.BlockSpec(memory_space=pltpu.VMEM)
    return pl.pallas_call(
        functools.partial(paired_kernel, steps=ahead_source.shape[0]),
        out_shape=(
            jax.ShapeDtypeStruct(ahead_start.shape, jnp.float32),
            jax.ShapeDtypeStruct(behind_start.shape, jnp.float32),
        ),
        in_specs=[smem, smem, vmem, vmem, vmem, vmem, vmem],
        out_specs=(vmem, vmem),
    )(ahead_pick, behind_pick, ahead_start, behind_start, ahead_table, behind_table, ahead_source)


def per_band_products(lines, factors, weights):
    steps, rows, states = lines.shape
    bands = factors.shape[0]
    every = accurate_matmul_result(
        lines.reshape(steps * rows, states),
        jnp.transpose(factors, (1, 0, 2)).reshape(states, bands * states),
    ).reshape(steps, rows, bands, states)
    return jnp.sum(every * weights[:, None, :, None], axis=2)


def shards(
    observations,
    band_index,
    obs_mask,
    diffusivity,
    mode_correction_factors,
    mode_backward_factors,
    initial_mean,
):
    steps_dev = observations.shape[0]
    record_rows = observations.shape[1]
    states = initial_mean.shape[0]
    bands = diffusivity.shape[0]
    column_share = states // lax.axis_size("col")
    column_index = lax.axis_index("col")
    time_devices = lax.axis_size("tm")
    time_index = lax.axis_index("tm")
    dynamics = diffusion_matrices(diffusivity, GRID)
    gain = jnp.transpose(mode_correction_factors, (0, 2, 1))
    corrected = dynamics - jnp.einsum(
        "bij,bjk->bik", dynamics, gain, precision=lax.Precision.HIGHEST
    )
    forward_table = jnp.stack([dynamics, corrected], axis=1).reshape(2 * bands, states, states)
    forward_pick = 2 * band_index + obs_mask
    identity = jnp.eye(states, dtype=jnp.float32)
    own_identity = lax.dynamic_slice_in_dim(identity, column_index * column_share, column_share, 0)
    blank_columns = jnp.zeros((steps_dev, column_share, states), jnp.float32)
    band_weights = (band_index[:, None] == jnp.arange(bands)[None, :]).astype(jnp.float32)
    observed_weights = band_weights * obs_mask.astype(jnp.float32)[:, None]
    measured = per_band_products(observations, gain, observed_weights)

    blank_records = jnp.zeros((record_rows, states), jnp.float32)
    first_block = time_index == 0
    final_here = (time_index == time_devices - 1) & (jnp.arange(steps_dev) == steps_dev - 1)
    backward = jnp.transpose(mode_backward_factors, (0, 2, 1))
    backward_table = jnp.concatenate([backward, jnp.zeros_like(backward[:1])], axis=0)
    backward_pick = jnp.where(final_here, bands, band_index)
    forward_rows, backward_rows = paired_maps(
        forward_pick,
        backward_pick,
        jnp.concatenate([own_identity, blank_records], axis=0),
        own_identity,
        forward_table,
        backward_table,
        jnp.concatenate([blank_columns, measured], axis=1),
    )
    whole_matrix = gathered_rows(forward_rows[:column_share], "col")
    whole_back = gathered_rows(backward_rows, "col")
    block_records = forward_rows[column_share:]
    folded_records = jnp.where(
        first_block,
        accurate_matmul_result(initial_mean[None, :], whole_matrix) + block_records,
        block_records,
    )
    _, backward_maps, ending_records = doubling_maps(
        jnp.where(first_block, jnp.zeros_like(whole_matrix), whole_matrix),
        whole_back,
        folded_records,
        "tm",
        0,
    )
    start_rows = jnp.where(
        first_block,
        jnp.broadcast_to(initial_mean[None, :], (record_rows, states)),
        passed_along(ending_records, "tm", 1),
    )

    first_prediction = accurate_matmul_result(start_rows, dynamics[band_index[0]])
    filtered, predicted = recurrence(
        forward_pick,
        start_rows,
        forward_table,
        measured,
        False,
        True,
        side=(band_index, dynamics),
    )
    following = passed_along(first_prediction, "tm", -1)
    next_predicted = jnp.concatenate([predicted[1:], following[None]], axis=0)

    live_weights = band_weights * (1.0 - final_here.astype(jnp.float32))[:, None]
    shift = filtered - per_band_products(next_predicted, backward, live_weights)

    back_records = recurrence(backward_pick, blank_records, backward_table, shift, True, False)
    opening_records = doubling_records(backward_maps, back_records, "tm", True, 1)
    after_records = passed_along(opening_records, "tm", -1)

    smoothed = recurrence(backward_pick, after_records, backward_table, shift, True, True)
    return (filtered, smoothed)


def solution(mesh):
    return jax.shard_map(
        shards,
        mesh=mesh,
        in_specs=(P("tm", "col", None), P("tm"), P("tm"), P(), P(), P(), P()),
        out_specs=(P("tm", "col", None), P("tm", "col", None)),
        check_vma=False,
    )
```

```python
import functools

import jax
import jax.numpy as jnp
from jax import lax
from jax.experimental import pallas as pl
from jax.experimental.pallas import tpu as pltpu
from jax.sharding import PartitionSpec as P

GRID = 16
UNROLL = 4


def passed_along(block, axis, distance):
    devices = range(lax.axis_size(axis))
    route = [(i - distance, i) for i in devices if i - distance in devices]
    return lax.ppermute(block, axis, route)


def gathered_rows(part, axis):
    peers, index = (lax.axis_size(axis), lax.axis_index(axis))
    rows = part.shape[0]
    whole = jnp.zeros((peers * rows,) + part.shape[1:], part.dtype)
    for shift in range(peers):
        if shift == 0:
            got = part
        else:
            got = lax.ppermute(part, axis, [(i, (i + shift) % peers) for i in range(peers)])
        owner = lax.rem(index - shift + peers, peers)
        whole = lax.dynamic_update_slice_in_dim(whole, got, owner * rows, 0)
    return whole


def accurate_matmul_result(first_factor, second_factor):
    return jnp.dot(first_factor, second_factor, precision=lax.Precision.HIGHEST)


def greet_partners(index, peers, other, rounds):
    barrier = pltpu.get_barrier_semaphore()
    partners = 0
    for r in range(rounds):
        distance = 1 << r
        for partner, exists in ((index + distance, index + distance < peers),
                                (index - distance, index - distance >= 0)):
            @pl.when(exists)
            def _():
                pl.semaphore_signal(barrier, inc=1, device_id=(partner, other),
                                    device_id_type=pl.DeviceIdType.MESH)

            partners = partners + jnp.where(exists, 1, 0)
    pl.semaphore_wait(barrier, partners)


def exact_dot(first, second):
    return jnp.dot(first, second, precision=lax.Precision.HIGHEST,
                   preferred_element_type=jnp.float32)


def maps_kernel(ahead_ref, behind_ref, records_ref, ahead_out, behind_out, records_out,
                ahead_in, behind_in, sums, sum_in, sems, sum_sems, *, axis):
    peers, index = (lax.axis_size(axis), lax.axis_index(axis))
    other = lax.axis_index("col")
    rounds = ahead_out.shape[0]
    greet_partners(index, peers, other, rounds)
    ahead_out[0] = ahead_ref[...]
    behind_out[0] = behind_ref[...]
    pending = []
    for r in range(rounds):
        distance = 1 << r
        up, has_up = index + distance, index + distance < peers
        down, has_down = index - distance, index - distance >= 0
        own_ahead = ahead_ref if r == 0 else ahead_out.at[r]
        own_sum = records_ref if r == 0 else sums.at[r]
        sum_copy = pltpu.make_async_remote_copy(
            src_ref=own_sum, dst_ref=sum_in.at[r], send_sem=sum_sems.at[0, r],
            recv_sem=sum_sems.at[1, r], device_id=(up, other),
            device_id_type=pl.DeviceIdType.MESH)

        @pl.when(has_up)
        def _():
            sum_copy.start()

        if r == rounds - 1:
            @pl.when(has_down)
            def _():
                sum_copy.wait_recv()
                sums[r + 1] = exact_dot(sum_in[r], own_ahead[...]) + own_sum[...]

            @pl.when(jnp.logical_not(has_down))
            def _():
                sums[r + 1] = own_sum[...]

            pending.append((has_up, sum_copy))
            break
        own_behind = behind_ref if r == 0 else behind_out.at[r]
        ahead_copy = pltpu.make_async_remote_copy(
            src_ref=own_ahead, dst_ref=ahead_in.at[r], send_sem=sems.at[0, 0, r],
            recv_sem=sems.at[0, 1, r], device_id=(up, other),
            device_id_type=pl.DeviceIdType.MESH)
        behind_copy = pltpu.make_async_remote_copy(
            src_ref=own_behind, dst_ref=behind_in.at[r], send_sem=sems.at[1, 0, r],
            recv_sem=sems.at[1, 1, r], device_id=(down, other),
            device_id_type=pl.DeviceIdType.MESH)

        @pl.when(has_up)
        def _():
            ahead_copy.start()

        @pl.when(has_down)
        def _():
            behind_copy.start()

        @pl.when(has_down)
        def _():
            sum_copy.wait_recv()
            sums[r + 1] = exact_dot(sum_in[r], own_ahead[...]) + own_sum[...]

        @pl.when(jnp.logical_not(has_down))
        def _():
            sums[r + 1] = own_sum[...]

        @pl.when(has_down)
        def _():
            ahead_copy.wait_recv()
            ahead_out[r + 1] = exact_dot(ahead_in[r], own_ahead[...])

        @pl.when(jnp.logical_not(has_down))
        def _():
            ahead_out[r + 1] = own_ahead[...]

        @pl.when(has_up)
        def _():
            behind_copy.wait_recv()
            behind_out[r + 1] = exact_dot(behind_in[r], own_behind[...])

        @pl.when(jnp.logical_not(has_up))
        def _():
            behind_out[r + 1] = own_behind[...]

        pending += [(has_up, ahead_copy), (has_up, sum_copy), (has_down, behind_copy)]

    for sent, copy in pending:
        @pl.when(sent)
        def _():
            copy.wait_send()

    records_out[...] = sums[rounds]


def doubling_maps(ahead, behind, records, axis, collective_id):
    peers = lax.axis_size(axis)
    rounds = max(1, (peers - 1).bit_length())
    states = ahead.shape[0]
    vmem = pl.BlockSpec(memory_space=pltpu.VMEM)
    stack = jax.ShapeDtypeStruct((rounds, states, states), jnp.float32)
    return pl.pallas_call(
        functools.partial(maps_kernel, axis=axis),
        out_shape=(stack, stack, jax.ShapeDtypeStruct(records.shape, jnp.float32)),
        in_specs=[vmem, vmem, vmem],
        out_specs=(vmem, vmem, vmem),
        scratch_shapes=[
            pltpu.VMEM((max(1, rounds - 1), states, states), jnp.float32),
            pltpu.VMEM((max(1, rounds - 1), states, states), jnp.float32),
            pltpu.VMEM((rounds + 1,) + records.shape, jnp.float32),
            pltpu.VMEM((rounds,) + records.shape, jnp.float32),
            pltpu.SemaphoreType.DMA((2, 2, max(1, rounds - 1))),
            pltpu.SemaphoreType.DMA((2, rounds)),
        ],
        compiler_params=pltpu.CompilerParams(collective_id=collective_id, has_side_effects=True),
    )(ahead, behind, records)


def records_kernel(maps_ref, records_ref, out_ref, sums, sum_in, handed, hand_sems, sems, *,
                   axis, reverse):
    peers, index = (lax.axis_size(axis), lax.axis_index(axis))
    other = lax.axis_index("col")
    rounds = maps_ref.shape[0]
    greet_partners(index, peers, other, rounds)
    pending = []
    for r in range(rounds):
        distance = 1 << r
        if reverse:
            target, sends = index - distance, index - distance >= 0
            receives = index + distance < peers
        else:
            target, sends = index + distance, index + distance < peers
            receives = index - distance >= 0
        own_sum = records_ref if r == 0 else sums.at[r]
        sum_copy = pltpu.make_async_remote_copy(
            src_ref=own_sum, dst_ref=sum_in.at[r], send_sem=sems.at[0, r],
            recv_sem=sems.at[1, r], device_id=(target, other),
            device_id_type=pl.DeviceIdType.MESH)

        @pl.when(sends)
        def _():
            sum_copy.start()

        @pl.when(receives)
        def _():
            sum_copy.wait_recv()
            sums[r + 1] = exact_dot(sum_in[r], maps_ref[r]) + own_sum[...]

        @pl.when(jnp.logical_not(receives))
        def _():
            sums[r + 1] = own_sum[...]

        pending.append((sends, sum_copy))

    if reverse:
        target, sends, receives = index - 1, index - 1 >= 0, index + 1 < peers
    else:
        target, sends, receives = index + 1, index + 1 < peers, index - 1 >= 0
    hand_copy = pltpu.make_async_remote_copy(
        src_ref=sums.at[rounds], dst_ref=handed, send_sem=hand_sems.at[0],
        recv_sem=hand_sems.at[1], device_id=(target, other),
        device_id_type=pl.DeviceIdType.MESH)

    @pl.when(sends)
    def _():
        hand_copy.start()

    @pl.when(receives)
    def _():
        hand_copy.wait_recv()
        out_ref[...] = handed[...]

    @pl.when(jnp.logical_not(receives))
    def _():
        out_ref[...] = jnp.zeros_like(handed)

    pending.append((sends, hand_copy))
    for sent, copy in pending:
        @pl.when(sent)
        def _():
            copy.wait_send()


def doubling_records(maps, records, axis, reverse, collective_id):
    rounds = maps.shape[0]
    vmem = pl.BlockSpec(memory_space=pltpu.VMEM)
    return pl.pallas_call(
        functools.partial(records_kernel, axis=axis, reverse=reverse),
        out_shape=jax.ShapeDtypeStruct(records.shape, jnp.float32),
        in_specs=[vmem, vmem],
        out_specs=vmem,
        scratch_shapes=[
            pltpu.VMEM((rounds + 1,) + records.shape, jnp.float32),
            pltpu.VMEM((rounds,) + records.shape, jnp.float32),
            pltpu.VMEM(records.shape, jnp.float32),
            pltpu.SemaphoreType.DMA((2,)),
            pltpu.SemaphoreType.DMA((2, rounds)),
        ],
        compiler_params=pltpu.CompilerParams(collective_id=collective_id, has_side_effects=True),
    )(maps, records)


def diffusion_matrices(diffusivity, side_cells):
    cell_count = side_cells * side_cells
    cell_ids = jnp.arange(cell_count)
    cell_row = cell_ids // side_cells
    cell_col = cell_ids % side_cells
    adjacent = (
        jnp.abs(cell_row[:, None] - cell_row[None, :])
        + jnp.abs(cell_col[:, None] - cell_col[None, :])
        == 1
    )
    coupling = (
        0.5 * (diffusivity[:, :, None] + diffusivity[:, None, :]) * adjacent.astype(jnp.float32)
    )
    keeping = 1.0 - jnp.sum(coupling, axis=2)
    return coupling + keeping[:, :, None] * jnp.eye(cell_count, dtype=jnp.float32)


def recurrence_kernel(*refs, steps, reverse, store_all, side):
    if side:
        pick_ref, side_pick_ref, start_ref, table_ref, side_ref, source_ref, out_ref, side_out_ref = refs
    else:
        pick_ref, start_ref, table_ref, source_ref, out_ref = refs
    def advance(i, rows):
        t = steps - 1 - i if reverse else i
        if side:
            side_out_ref[t] = jnp.dot(
                rows,
                side_ref[side_pick_ref[t]],
                precision=lax.Precision.HIGHEST,
                preferred_element_type=jnp.float32,
            )
        rows = (
            jnp.dot(
                rows,
                table_ref[pick_ref[t]],
                precision=lax.Precision.HIGHEST,
                preferred_element_type=jnp.float32,
            )
            + source_ref[t]
        )
        if store_all:
            out_ref[t] = rows
        return rows

    rows = lax.fori_loop(0, steps, advance, start_ref[...], unroll=UNROLL)
    if not store_all:
        out_ref[...] = rows


def recurrence(pick, start, table, source, reverse, store_all, side=None):
    steps = source.shape[0]
    smem = pl.BlockSpec(memory_space=pltpu.SMEM)
    vmem = pl.BlockSpec(memory_space=pltpu.VMEM)
    out_shape = jax.ShapeDtypeStruct(source.shape if store_all else start.shape, jnp.float32)
    if side is None:
        operands = (pick, start, table, source)
        in_specs = [smem, vmem, vmem, vmem]
        out_specs = vmem
    else:
        side_pick, side_table = side
        operands = (pick, side_pick, start, table, side_table, source)
        in_specs = [smem, smem, vmem, vmem, vmem, vmem]
        out_shape = (out_shape, jax.ShapeDtypeStruct(source.shape, jnp.float32))
        out_specs = (vmem, vmem)
    return pl.pallas_call(
        functools.partial(
            recurrence_kernel,
            steps=steps,
            reverse=reverse,
            store_all=store_all,
            side=side is not None,
        ),
        out_shape=out_shape,
        in_specs=in_specs,
        out_specs=out_specs,
        cost_estimate=pl.CostEstimate(
            flops=2 * steps * start.shape[0] * table.shape[1] * table.shape[2] * (2 if side else 1),
            bytes_accessed=4 * (table.size + 3 * source.size),
            transcendentals=0,
        ),
    )(*operands)


def paired_kernel(ahead_pick_ref, behind_pick_ref, ahead_start_ref, behind_start_ref,
                  ahead_table_ref, behind_table_ref, ahead_source_ref, ahead_out, behind_out,
                  *, steps):
    def advance(i, carry):
        ahead, behind = carry
        back = steps - 1 - i
        ahead = exact_dot(ahead, ahead_table_ref[ahead_pick_ref[i]]) + ahead_source_ref[i]
        behind = exact_dot(behind, behind_table_ref[behind_pick_ref[back]])
        return ahead, behind

    ahead, behind = lax.fori_loop(
        0, steps, advance, (ahead_start_ref[...], behind_start_ref[...]), unroll=UNROLL
    )
    ahead_out[...] = ahead
    behind_out[...] = behind


def paired_maps(ahead_pick, behind_pick, ahead_start, behind_start, ahead_table, behind_table,
                ahead_source):
    smem = pl.BlockSpec(memory_space=pltpu.SMEM)
    vmem = pl.BlockSpec(memory_space=pltpu.VMEM)
    return pl.pallas_call(
        functools.partial(paired_kernel, steps=ahead_source.shape[0]),
        out_shape=(
            jax.ShapeDtypeStruct(ahead_start.shape, jnp.float32),
            jax.ShapeDtypeStruct(behind_start.shape, jnp.float32),
        ),
        in_specs=[smem, smem, vmem, vmem, vmem, vmem, vmem],
        out_specs=(vmem, vmem),
    )(ahead_pick, behind_pick, ahead_start, behind_start, ahead_table, behind_table, ahead_source)


def per_band_products(lines, factors, weights):
    steps, rows, states = lines.shape
    bands = factors.shape[0]
    every = accurate_matmul_result(
        lines.reshape(steps * rows, states),
        jnp.transpose(factors, (1, 0, 2)).reshape(states, bands * states),
    ).reshape(steps, rows, bands, states)
    return jnp.sum(every * weights[:, None, :, None], axis=2)


def shards(
    observations,
    band_index,
    obs_mask,
    diffusivity,
    mode_correction_factors,
    mode_backward_factors,
    initial_mean,
):
    steps_dev = observations.shape[0]
    record_rows = observations.shape[1]
    states = initial_mean.shape[0]
    bands = diffusivity.shape[0]
    column_share = states // lax.axis_size("col")
    column_index = lax.axis_index("col")
    time_devices = lax.axis_size("tm")
    time_index = lax.axis_index("tm")
    dynamics = diffusion_matrices(diffusivity, GRID)
    gain = jnp.transpose(mode_correction_factors, (0, 2, 1))
    corrected = dynamics - jnp.einsum(
        "bij,bjk->bik", dynamics, gain, precision=lax.Precision.HIGHEST
    )
    forward_table = jnp.stack([dynamics, corrected], axis=1).reshape(2 * bands, states, states)
    forward_pick = 2 * band_index + obs_mask
    identity = jnp.eye(states, dtype=jnp.float32)
    own_identity = lax.dynamic_slice_in_dim(identity, column_index * column_share, column_share, 0)
    blank_columns = jnp.zeros((steps_dev, column_share, states), jnp.float32)
    band_weights = (band_index[:, None] == jnp.arange(bands)[None, :]).astype(jnp.float32)
    observed_weights = band_weights * obs_mask.astype(jnp.float32)[:, None]
    measured = per_band_products(observations, gain, observed_weights)

    blank_records = jnp.zeros((record_rows, states), jnp.float32)
    first_block = time_index == 0
    final_here = (time_index == time_devices - 1) & (jnp.arange(steps_dev) == steps_dev - 1)
    backward = jnp.transpose(mode_backward_factors, (0, 2, 1))
    backward_table = jnp.concatenate([backward, jnp.zeros_like(backward[:1])], axis=0)
    backward_pick = jnp.where(final_here, bands, band_index)
    forward_rows, backward_rows = paired_maps(
        forward_pick,
        backward_pick,
        jnp.concatenate([own_identity, blank_records], axis=0),
        own_identity,
        forward_table,
        backward_table,
        jnp.concatenate([blank_columns, measured], axis=1),
    )
    whole_matrix = gathered_rows(forward_rows[:column_share], "col")
    whole_back = gathered_rows(backward_rows, "col")
    block_records = forward_rows[column_share:]
    folded_records = jnp.where(
        first_block,
        accurate_matmul_result(initial_mean[None, :], whole_matrix) + block_records,
        block_records,
    )
    _, backward_maps, ending_records = doubling_maps(
        jnp.where(first_block, jnp.zeros_like(whole_matrix), whole_matrix),
        whole_back,
        folded_records,
        "tm",
        0,
    )
    start_rows = jnp.where(
        first_block,
        jnp.broadcast_to(initial_mean[None, :], (record_rows, states)),
        passed_along(ending_records, "tm", 1),
    )

    first_prediction = accurate_matmul_result(start_rows, dynamics[band_index[0]])
    filtered, predicted = recurrence(
        forward_pick,
        start_rows,
        forward_table,
        measured,
        False,
        True,
        side=(band_index, dynamics),
    )
    following = passed_along(first_prediction, "tm", -1)
    next_predicted = jnp.concatenate([predicted[1:], following[None]], axis=0)

    live_weights = band_weights * (1.0 - final_here.astype(jnp.float32))[:, None]
    shift = filtered - per_band_products(next_predicted, backward, live_weights)

    back_records = recurrence(backward_pick, blank_records, backward_table, shift, True, False)
    after_records = doubling_records(backward_maps, back_records, "tm", True, 1)

    smoothed = recurrence(backward_pick, after_records, backward_table, shift, True, True)
    return (filtered, smoothed)


def solution(mesh):
    return jax.shard_map(
        shards,
        mesh=mesh,
        in_specs=(P("tm", "col", None), P("tm"), P("tm"), P(), P(), P(), P()),
        out_specs=(P("tm", "col", None), P("tm", "col", None)),
        check_vma=False,
    )
```

```python
import functools

import jax
import jax.numpy as jnp
from jax import lax
from jax.experimental import pallas as pl
from jax.experimental.pallas import tpu as pltpu
from jax.sharding import PartitionSpec as P

GRID = 16
UNROLL = 4


def passed_along(block, axis, distance):
    devices = range(lax.axis_size(axis))
    route = [(i - distance, i) for i in devices if i - distance in devices]
    return lax.ppermute(block, axis, route)


def gathered_rows(part, axis):
    peers, index = (lax.axis_size(axis), lax.axis_index(axis))
    rows = part.shape[0]
    whole = jnp.zeros((peers * rows,) + part.shape[1:], part.dtype)
    for shift in range(peers):
        if shift == 0:
            got = part
        else:
            got = lax.ppermute(part, axis, [(i, (i + shift) % peers) for i in range(peers)])
        owner = lax.rem(index - shift + peers, peers)
        whole = lax.dynamic_update_slice_in_dim(whole, got, owner * rows, 0)
    return whole


def accurate_matmul_result(first_factor, second_factor):
    return jnp.dot(first_factor, second_factor, precision=lax.Precision.HIGHEST)


def greet_partners(index, peers, other, rounds):
    barrier = pltpu.get_barrier_semaphore()
    partners = 0
    for r in range(rounds):
        distance = 1 << r
        for partner, exists in ((index + distance, index + distance < peers),
                                (index - distance, index - distance >= 0)):
            @pl.when(exists)
            def _():
                pl.semaphore_signal(barrier, inc=1, device_id=(partner, other),
                                    device_id_type=pl.DeviceIdType.MESH)

            partners = partners + jnp.where(exists, 1, 0)
    pl.semaphore_wait(barrier, partners)


def exact_dot(first, second):
    return jnp.dot(first, second, precision=lax.Precision.HIGHEST,
                   preferred_element_type=jnp.float32)


def maps_kernel(ahead_ref, behind_ref, records_ref, ahead_out, behind_out, records_out,
                ahead_in, behind_in, sums, sum_in, handed, hand_sems, sems, sum_sems, *, axis):
    peers, index = (lax.axis_size(axis), lax.axis_index(axis))
    other = lax.axis_index("col")
    rounds = ahead_out.shape[0]
    greet_partners(index, peers, other, rounds)
    ahead_out[0] = ahead_ref[...]
    behind_out[0] = behind_ref[...]
    pending = []
    for r in range(rounds):
        distance = 1 << r
        up, has_up = index + distance, index + distance < peers
        down, has_down = index - distance, index - distance >= 0
        own_ahead = ahead_ref if r == 0 else ahead_out.at[r]
        own_sum = records_ref if r == 0 else sums.at[r]
        sum_copy = pltpu.make_async_remote_copy(
            src_ref=own_sum, dst_ref=sum_in.at[r], send_sem=sum_sems.at[0, r],
            recv_sem=sum_sems.at[1, r], device_id=(up, other),
            device_id_type=pl.DeviceIdType.MESH)

        @pl.when(has_up)
        def _():
            sum_copy.start()

        if r == rounds - 1:
            @pl.when(has_down)
            def _():
                sum_copy.wait_recv()
                sums[r + 1] = exact_dot(sum_in[r], own_ahead[...]) + own_sum[...]

            @pl.when(jnp.logical_not(has_down))
            def _():
                sums[r + 1] = own_sum[...]

            pending.append((has_up, sum_copy))
            break
        own_behind = behind_ref if r == 0 else behind_out.at[r]
        ahead_copy = pltpu.make_async_remote_copy(
            src_ref=own_ahead, dst_ref=ahead_in.at[r], send_sem=sems.at[0, 0, r],
            recv_sem=sems.at[0, 1, r], device_id=(up, other),
            device_id_type=pl.DeviceIdType.MESH)
        behind_copy = pltpu.make_async_remote_copy(
            src_ref=own_behind, dst_ref=behind_in.at[r], send_sem=sems.at[1, 0, r],
            recv_sem=sems.at[1, 1, r], device_id=(down, other),
            device_id_type=pl.DeviceIdType.MESH)

        @pl.when(has_up)
        def _():
            ahead_copy.start()

        @pl.when(has_down)
        def _():
            behind_copy.start()

        @pl.when(has_down)
        def _():
            sum_copy.wait_recv()
            sums[r + 1] = exact_dot(sum_in[r], own_ahead[...]) + own_sum[...]

        @pl.when(jnp.logical_not(has_down))
        def _():
            sums[r + 1] = own_sum[...]

        @pl.when(has_down)
        def _():
            ahead_copy.wait_recv()
            ahead_out[r + 1] = exact_dot(ahead_in[r], own_ahead[...])

        @pl.when(jnp.logical_not(has_down))
        def _():
            ahead_out[r + 1] = own_ahead[...]

        @pl.when(has_up)
        def _():
            behind_copy.wait_recv()
            behind_out[r + 1] = exact_dot(behind_in[r], own_behind[...])

        @pl.when(jnp.logical_not(has_up))
        def _():
            behind_out[r + 1] = own_behind[...]

        pending += [(has_up, ahead_copy), (has_up, sum_copy), (has_down, behind_copy)]

    sends, receives = index + 1 < peers, index - 1 >= 0
    hand_copy = pltpu.make_async_remote_copy(
        src_ref=sums.at[rounds], dst_ref=handed, send_sem=hand_sems.at[0],
        recv_sem=hand_sems.at[1], device_id=(index + 1, other),
        device_id_type=pl.DeviceIdType.MESH)

    @pl.when(sends)
    def _():
        hand_copy.start()

    @pl.when(receives)
    def _():
        hand_copy.wait_recv()
        records_out[...] = handed[...]

    @pl.when(jnp.logical_not(receives))
    def _():
        records_out[...] = jnp.zeros_like(handed)

    pending.append((sends, hand_copy))
    for sent, copy in pending:
        @pl.when(sent)
        def _():
            copy.wait_send()


def doubling_maps(ahead, behind, records, axis, collective_id):
    peers = lax.axis_size(axis)
    rounds = max(1, (peers - 1).bit_length())
    states = ahead.shape[0]
    vmem = pl.BlockSpec(memory_space=pltpu.VMEM)
    stack = jax.ShapeDtypeStruct((rounds, states, states), jnp.float32)
    return pl.pallas_call(
        functools.partial(maps_kernel, axis=axis),
        out_shape=(stack, stack, jax.ShapeDtypeStruct(records.shape, jnp.float32)),
        in_specs=[vmem, vmem, vmem],
        out_specs=(vmem, vmem, vmem),
        scratch_shapes=[
            pltpu.VMEM((max(1, rounds - 1), states, states), jnp.float32),
            pltpu.VMEM((max(1, rounds - 1), states, states), jnp.float32),
            pltpu.VMEM((rounds + 1,) + records.shape, jnp.float32),
            pltpu.VMEM((rounds,) + records.shape, jnp.float32),
            pltpu.VMEM(records.shape, jnp.float32),
            pltpu.SemaphoreType.DMA((2,)),
            pltpu.SemaphoreType.DMA((2, 2, max(1, rounds - 1))),
            pltpu.SemaphoreType.DMA((2, rounds)),
        ],
        compiler_params=pltpu.CompilerParams(collective_id=collective_id, has_side_effects=True),
    )(ahead, behind, records)


def records_kernel(maps_ref, records_ref, out_ref, sums, sum_in, handed, hand_sems, sems, *,
                   axis, reverse):
    peers, index = (lax.axis_size(axis), lax.axis_index(axis))
    other = lax.axis_index("col")
    rounds = maps_ref.shape[0]
    greet_partners(index, peers, other, rounds)
    pending = []
    for r in range(rounds):
        distance = 1 << r
        if reverse:
            target, sends = index - distance, index - distance >= 0
            receives = index + distance < peers
        else:
            target, sends = index + distance, index + distance < peers
            receives = index - distance >= 0
        own_sum = records_ref if r == 0 else sums.at[r]
        sum_copy = pltpu.make_async_remote_copy(
            src_ref=own_sum, dst_ref=sum_in.at[r], send_sem=sems.at[0, r],
            recv_sem=sems.at[1, r], device_id=(target, other),
            device_id_type=pl.DeviceIdType.MESH)

        @pl.when(sends)
        def _():
            sum_copy.start()

        @pl.when(receives)
        def _():
            sum_copy.wait_recv()
            sums[r + 1] = exact_dot(sum_in[r], maps_ref[r]) + own_sum[...]

        @pl.when(jnp.logical_not(receives))
        def _():
            sums[r + 1] = own_sum[...]

        pending.append((sends, sum_copy))

    if reverse:
        target, sends, receives = index - 1, index - 1 >= 0, index + 1 < peers
    else:
        target, sends, receives = index + 1, index + 1 < peers, index - 1 >= 0
    hand_copy = pltpu.make_async_remote_copy(
        src_ref=sums.at[rounds], dst_ref=handed, send_sem=hand_sems.at[0],
        recv_sem=hand_sems.at[1], device_id=(target, other),
        device_id_type=pl.DeviceIdType.MESH)

    @pl.when(sends)
    def _():
        hand_copy.start()

    @pl.when(receives)
    def _():
        hand_copy.wait_recv()
        out_ref[...] = handed[...]

    @pl.when(jnp.logical_not(receives))
    def _():
        out_ref[...] = jnp.zeros_like(handed)

    pending.append((sends, hand_copy))
    for sent, copy in pending:
        @pl.when(sent)
        def _():
            copy.wait_send()


def doubling_records(maps, records, axis, reverse, collective_id):
    rounds = maps.shape[0]
    vmem = pl.BlockSpec(memory_space=pltpu.VMEM)
    return pl.pallas_call(
        functools.partial(records_kernel, axis=axis, reverse=reverse),
        out_shape=jax.ShapeDtypeStruct(records.shape, jnp.float32),
        in_specs=[vmem, vmem],
        out_specs=vmem,
        scratch_shapes=[
            pltpu.VMEM((rounds + 1,) + records.shape, jnp.float32),
            pltpu.VMEM((rounds,) + records.shape, jnp.float32),
            pltpu.VMEM(records.shape, jnp.float32),
            pltpu.SemaphoreType.DMA((2,)),
            pltpu.SemaphoreType.DMA((2, rounds)),
        ],
        compiler_params=pltpu.CompilerParams(collective_id=collective_id, has_side_effects=True),
    )(maps, records)


def diffusion_matrices(diffusivity, side_cells):
    cell_count = side_cells * side_cells
    cell_ids = jnp.arange(cell_count)
    cell_row = cell_ids // side_cells
    cell_col = cell_ids % side_cells
    adjacent = (
        jnp.abs(cell_row[:, None] - cell_row[None, :])
        + jnp.abs(cell_col[:, None] - cell_col[None, :])
        == 1
    )
    coupling = (
        0.5 * (diffusivity[:, :, None] + diffusivity[:, None, :]) * adjacent.astype(jnp.float32)
    )
    keeping = 1.0 - jnp.sum(coupling, axis=2)
    return coupling + keeping[:, :, None] * jnp.eye(cell_count, dtype=jnp.float32)


def recurrence_kernel(*refs, steps, reverse, store_all, side):
    if side:
        pick_ref, side_pick_ref, start_ref, table_ref, side_ref, source_ref, out_ref, side_out_ref = refs
    else:
        pick_ref, start_ref, table_ref, source_ref, out_ref = refs
    def advance(i, rows):
        t = steps - 1 - i if reverse else i
        if side:
            side_out_ref[t] = jnp.dot(
                rows,
                side_ref[side_pick_ref[t]],
                precision=lax.Precision.HIGHEST,
                preferred_element_type=jnp.float32,
            )
        rows = (
            jnp.dot(
                rows,
                table_ref[pick_ref[t]],
                precision=lax.Precision.HIGHEST,
                preferred_element_type=jnp.float32,
            )
            + source_ref[t]
        )
        if store_all:
            out_ref[t] = rows
        return rows

    rows = lax.fori_loop(0, steps, advance, start_ref[...], unroll=UNROLL)
    if not store_all:
        out_ref[...] = rows


def recurrence(pick, start, table, source, reverse, store_all, side=None):
    steps = source.shape[0]
    smem = pl.BlockSpec(memory_space=pltpu.SMEM)
    vmem = pl.BlockSpec(memory_space=pltpu.VMEM)
    out_shape = jax.ShapeDtypeStruct(source.shape if store_all else start.shape, jnp.float32)
    if side is None:
        operands = (pick, start, table, source)
        in_specs = [smem, vmem, vmem, vmem]
        out_specs = vmem
    else:
        side_pick, side_table = side
        operands = (pick, side_pick, start, table, side_table, source)
        in_specs = [smem, smem, vmem, vmem, vmem, vmem]
        out_shape = (out_shape, jax.ShapeDtypeStruct(source.shape, jnp.float32))
        out_specs = (vmem, vmem)
    return pl.pallas_call(
        functools.partial(
            recurrence_kernel,
            steps=steps,
            reverse=reverse,
            store_all=store_all,
            side=side is not None,
        ),
        out_shape=out_shape,
        in_specs=in_specs,
        out_specs=out_specs,
        cost_estimate=pl.CostEstimate(
            flops=2 * steps * start.shape[0] * table.shape[1] * table.shape[2] * (2 if side else 1),
            bytes_accessed=4 * (table.size + 3 * source.size),
            transcendentals=0,
        ),
    )(*operands)


def paired_kernel(ahead_pick_ref, behind_pick_ref, ahead_start_ref, behind_start_ref,
                  ahead_table_ref, behind_table_ref, ahead_source_ref, ahead_out, behind_out,
                  *, steps):
    def advance(i, carry):
        ahead, behind = carry
        back = steps - 1 - i
        ahead = exact_dot(ahead, ahead_table_ref[ahead_pick_ref[i]]) + ahead_source_ref[i]
        behind = exact_dot(behind, behind_table_ref[behind_pick_ref[back]])
        return ahead, behind

    ahead, behind = lax.fori_loop(
        0, steps, advance, (ahead_start_ref[...], behind_start_ref[...]), unroll=UNROLL
    )
    ahead_out[...] = ahead
    behind_out[...] = behind


def paired_maps(ahead_pick, behind_pick, ahead_start, behind_start, ahead_table, behind_table,
                ahead_source):
    smem = pl.BlockSpec(memory_space=pltpu.SMEM)
    vmem = pl.BlockSpec(memory_space=pltpu.VMEM)
    return pl.pallas_call(
        functools.partial(paired_kernel, steps=ahead_source.shape[0]),
        out_shape=(
            jax.ShapeDtypeStruct(ahead_start.shape, jnp.float32),
            jax.ShapeDtypeStruct(behind_start.shape, jnp.float32),
        ),
        in_specs=[smem, smem, vmem, vmem, vmem, vmem, vmem],
        out_specs=(vmem, vmem),
    )(ahead_pick, behind_pick, ahead_start, behind_start, ahead_table, behind_table, ahead_source)


def per_band_products(lines, factors, weights):
    steps, rows, states = lines.shape
    bands = factors.shape[0]
    every = accurate_matmul_result(
        lines.reshape(steps * rows, states),
        jnp.transpose(factors, (1, 0, 2)).reshape(states, bands * states),
    ).reshape(steps, rows, bands, states)
    return jnp.sum(every * weights[:, None, :, None], axis=2)


def shards(
    observations,
    band_index,
    obs_mask,
    diffusivity,
    mode_correction_factors,
    mode_backward_factors,
    initial_mean,
):
    steps_dev = observations.shape[0]
    record_rows = observations.shape[1]
    states = initial_mean.shape[0]
    bands = diffusivity.shape[0]
    column_share = states // lax.axis_size("col")
    column_index = lax.axis_index("col")
    time_devices = lax.axis_size("tm")
    time_index = lax.axis_index("tm")
    dynamics = diffusion_matrices(diffusivity, GRID)
    gain = jnp.transpose(mode_correction_factors, (0, 2, 1))
    corrected = dynamics - jnp.einsum(
        "bij,bjk->bik", dynamics, gain, precision=lax.Precision.HIGHEST
    )
    forward_table = jnp.stack([dynamics, corrected], axis=1).reshape(2 * bands, states, states)
    forward_pick = 2 * band_index + obs_mask
    identity = jnp.eye(states, dtype=jnp.float32)
    own_identity = lax.dynamic_slice_in_dim(identity, column_index * column_share, column_share, 0)
    blank_columns = jnp.zeros((steps_dev, column_share, states), jnp.float32)
    band_weights = (band_index[:, None] == jnp.arange(bands)[None, :]).astype(jnp.float32)
    observed_weights = band_weights * obs_mask.astype(jnp.float32)[:, None]
    measured = per_band_products(observations, gain, observed_weights)

    blank_records = jnp.zeros((record_rows, states), jnp.float32)
    first_block = time_index == 0
    final_here = (time_index == time_devices - 1) & (jnp.arange(steps_dev) == steps_dev - 1)
    backward = jnp.transpose(mode_backward_factors, (0, 2, 1))
    backward_table = jnp.concatenate([backward, jnp.zeros_like(backward[:1])], axis=0)
    backward_pick = jnp.where(final_here, bands, band_index)
    forward_rows, backward_rows = paired_maps(
        forward_pick,
        backward_pick,
        jnp.concatenate([own_identity, blank_records], axis=0),
        own_identity,
        forward_table,
        backward_table,
        jnp.concatenate([blank_columns, measured], axis=1),
    )
    whole_matrix = gathered_rows(forward_rows[:column_share], "col")
    whole_back = gathered_rows(backward_rows, "col")
    block_records = forward_rows[column_share:]
    folded_records = jnp.where(
        first_block,
        accurate_matmul_result(initial_mean[None, :], whole_matrix) + block_records,
        block_records,
    )
    _, backward_maps, ending_records = doubling_maps(
        jnp.where(first_block, jnp.zeros_like(whole_matrix), whole_matrix),
        whole_back,
        folded_records,
        "tm",
        0,
    )
    start_rows = jnp.where(
        first_block,
        jnp.broadcast_to(initial_mean[None, :], (record_rows, states)),
        ending_records,
    )

    first_prediction = accurate_matmul_result(start_rows, dynamics[band_index[0]])
    filtered, predicted = recurrence(
        forward_pick,
        start_rows,
        forward_table,
        measured,
        False,
        True,
        side=(band_index, dynamics),
    )
    following = passed_along(first_prediction, "tm", -1)
    next_predicted = jnp.concatenate([predicted[1:], following[None]], axis=0)

    live_weights = band_weights * (1.0 - final_here.astype(jnp.float32))[:, None]
    shift = filtered - per_band_products(next_predicted, backward, live_weights)

    back_records = recurrence(backward_pick, blank_records, backward_table, shift, True, False)
    after_records = doubling_records(backward_maps, back_records, "tm", True, 1)

    smoothed = recurrence(backward_pick, after_records, backward_table, shift, True, True)
    return (filtered, smoothed)


def solution(mesh):
    return jax.shard_map(
        shards,
        mesh=mesh,
        in_specs=(P("tm", "col", None), P("tm"), P("tm"), P(), P(), P(), P()),
        out_specs=(P("tm", "col", None), P("tm", "col", None)),
        check_vma=False,
    )
```
